256 devices in a mesh: shard: 32 (over z, y), dp: 8 (over x, core).
Axes of the slice: x: 4, y: 4, z: 8, core: 2. Of those that a mesh axis runs over, the one named last changes fastest.
Arguments:
- cold_table: bfloat16 [65536, 256], P('shard'), may hold values from -6 to 6
- cold_accum: float32 [65536], P('shard'), may hold values from 0.005 to 0.5
- dither_bits: int32 [65536, 256], P('shard'), may hold values from 0 to 65280
- hot_table: float32 [1024, 256], replicated, may hold values from -6 to 6
- hot_accum: float32 [1024], replicated, may hold values from 1 to 100
- w_flat: bfloat16 [4096, 512], replicated, may hold values from -0.09375 to 0.09375
- w_inter: bfloat16 [256, 512], replicated, may hold values from -0.09375 to 0.09375
- hidden_bias: float32 [512], replicated, may hold values from -1 to 1
- w_out: float32 [512], replicated, may hold values from -0.25 to 0.25
- targets: float32 [131072], P(('shard', 'dp')), may hold values from 0 to 1
- hot_ids: int32 [131072, 8], P(('shard', 'dp')), may hold values from 0 to 1023
- cold_slots: int32 [131072, 8], P(('shard', 'dp')), may hold values from 0 to 2047, as said below
- requests: int32 [16384, 64], P(('shard', 'dp')), may hold values from 0 to 2047, as said below
- counts: int32 [512, 32], P(('shard', 'dp')), may hold values from 1 to 64, as said below
Outputs:
- cold_out: bfloat16 [65536, 256], P('shard')
- cold_accum_out: float32 [65536], P('shard')
- hot_out: float32 [1024, 256], replicated
- hot_accum_out: float32 [1024], replicated
The draws below stay inside these ranges and needn't reach their ends.
Inputs may be any that keep to these rules, and one draw needn't show every extreme that they name: `requests`: in each row of 64 entries (one device, micro-batch and shard) the entries name distinct rows of that shard's 2048; only the first counts-many are live, the rest name arbitrary rows. `counts`: in every draw, each device has in each micro-batch a shard with exactly 64 live slots. `cold_slots`: index into its device's request rows of that micro-batch, shard * 64 + slot; always a live slot, and every live slot is named by some lookup.
All inputs are finite; a program needn't handle non-finite values.
Results may differ from the reference program's by a relative error of at most 0.001.
The reference program's roundings to bfloat16 on the way (of `stacked`, `pair_dots`, `slopes` and `mirror`) count: a program that leaves them out, or rounds other values in their place, can miss the bound.
Values may be sent and summed in bfloat16 or wider, within the bound.
No kernel may reach another device: no remote copies, remote signals or barrier semaphores. Data moves between devices by JAX's collectives and lax.ppermute only.
A program may use at most 128 MiB of HBM per device.

```python
import math
import jax
import jax.numpy as jnp
import numpy as np
from jax import lax

E = 256
HID = 512
F_COLD = 8
F_HOT = 8
MB = 2
HOT = 1024
BATCH = 256
ROWS_DEV = 2048
FEATS = 16
COLD_ROWS = 65536
SAMPLES = 131072
N_SHARD = 32
N_DP = 8


def request_plan(key):
    base = jax.random.fold_in(key, 4242)
    keys = jax.random.split(base, 6)
    capacity = BATCH * F_COLD // N_SHARD
    device_count = N_SHARD * N_DP
    lookups = BATCH * F_COLD
    levels = jax.random.randint(keys[0], (N_SHARD,), 1, 5)
    low_counts = jnp.maximum(levels * capacity // 8, 1)
    high_counts = jnp.maximum(levels * capacity // 4, low_counts) + 1
    counts = jax.random.randint(keys[1], (device_count, MB, N_SHARD), low_counts, high_counts)
    requester = jnp.arange(device_count)[:, None, None]
    micro_index = jnp.arange(MB)[None, :, None]
    owners = jnp.arange(N_SHARD)[None, None, :]
    counts = jnp.where(owners == (requester + micro_index) % N_SHARD, capacity, counts)
    row_orders = jax.vmap(lambda part_key: jax.random.permutation(part_key, ROWS_DEV))(jax.random.split(keys[2], N_SHARD))
    starts = jax.random.randint(keys[3], (device_count, MB, N_SHARD, 1), 0, ROWS_DEV)
    positions = (starts + jnp.arange(capacity)[None, None, None, :]) % ROWS_DEV
    requests = row_orders[jnp.arange(N_SHARD)[None, None, :, None], positions]
    live_total = jnp.sum(counts, axis=-1, keepdims=True)
    ends = jnp.cumsum(counts, axis=-1)
    order = jnp.arange(lookups)[None, None, :]
    random_pick = jax.random.randint(keys[4], (device_count, MB, lookups), 0, live_total)
    flat_index = jnp.where(order < live_total, order, random_pick)
    owner_of = jax.vmap(jax.vmap(lambda boundaries, chosen: jnp.searchsorted(boundaries, chosen, side='right')))(ends, flat_index)
    owner_of = owner_of.astype(jnp.int32)
    begins = ends - counts
    within = flat_index - jnp.take_along_axis(begins, owner_of, axis=-1)
    slot_index = owner_of * capacity + within
    shuffles = jax.vmap(lambda part_key: jax.random.permutation(part_key, lookups))(jax.random.split(keys[5], device_count * MB))
    slot_index = jnp.take_along_axis(slot_index, shuffles.reshape(device_count, MB, lookups), axis=-1)
    return (requests.reshape(device_count * MB * N_SHARD, capacity).astype(jnp.int32), counts.reshape(device_count * MB, N_SHARD).astype(jnp.int32), slot_index.reshape(device_count * MB * BATCH, F_COLD).astype(jnp.int32))


def draw_requests(key, part):
    return request_plan(key)[0]


def draw_counts(key, part):
    return request_plan(key)[1]


def draw_cold_slots(key, part):
    return request_plan(key)[2]


def with_ends(entries, stream_key, low, largest):
    shape = entries.shape
    index_at = [jax.random.randint(jax.random.fold_in(stream_key, axis), (), 0, shape[axis]) for axis in range(len(shape))]
    entries = entries.at[tuple(index_at)].set(low)
    longest = shape.index(max(shape))
    index_at[longest] = (index_at[longest] + 1) % shape[longest]
    return entries.at[tuple(index_at)].set(largest)


def steps_of(rng, shape, shards, smallest, largest):
    def one(dim, parts):
        draws = jax.random.uniform(jax.random.fold_in(jax.random.fold_in(rng, 6), dim), (parts,), jnp.float32, smallest / len(shards), largest / len(shards))
        return jnp.repeat(jnp.exp(draws), shape[dim] // parts).reshape((-1,) + (1,) * (len(shape) - dim - 1))

    factor_of = one(*shards[0])
    for cut in shards[1:]:
        factor_of = factor_of * one(*cut)
    return factor_of


def cumulative_ranks(count, slope):
    weights = [(1 << 20) // math.isqrt(grade ** slope) + 1 for grade in range(1, count + 1)]
    spread = 1 + sum(weights) // (1 << 30)
    return np.cumsum(np.array([max(1, weight // spread) for weight in weights]))


def skewed_ids(key, extent, number_of, lean):
    listing = cumulative_ranks(number_of, lean)
    pick = jax.random.randint(jax.random.fold_in(key, 1), extent, 0, int(listing[number_of - 1]))
    rank = jnp.searchsorted(jnp.asarray(listing, jnp.int32), pick, side="right")
    return jax.random.permutation(jax.random.fold_in(key, 2), number_of)[rank].astype(jnp.int32)


def gaussian(key, shape, deviation, most, cuts=(), kind=jnp.bfloat16):
    factor_of = steps_of(key, shape, cuts, -0.22, 0.18) if cuts else 1.0
    entries = jax.random.normal(key, shape, jnp.float32) * deviation * factor_of
    return jnp.minimum(jnp.maximum(entries, -most), most).astype(kind)


def setup_inputs(seed: int = 0) -> dict:
    key_list = jax.random.split(jax.random.key(seed), 15)
    return {
        "cold_table": gaussian(key_list[0], (COLD_ROWS, E), 1.0, 6.0, ((0, 32),)),
        "cold_accum": jnp.clip(jnp.exp(math.log(0.5) - 4.6051702 * jax.random.uniform(key_list[1], (COLD_ROWS,), jnp.float32) ** steps_of(key_list[1], (COLD_ROWS,), ((0, 32),), -0.2, 0.2)), 0.005, 0.5),
        "dither_bits": with_ends(jax.random.randint(key_list[2], (COLD_ROWS, E), 0, 65281), jax.random.fold_in(key_list[2], 1), 0, 65280).astype(jnp.int32),
        "hot_table": gaussian(key_list[3], (HOT, E), 1.0, 6.0, (), jnp.float32),
        "hot_accum": jnp.clip(jnp.exp(jax.random.uniform(key_list[4], (HOT,), jnp.float32, math.log(1.0), math.log(100.0))), 1.0, 100.0),
        "w_flat": gaussian(key_list[5], (FEATS * E, HID), (FEATS * E) ** -0.5, 0.09375),
        "w_inter": gaussian(key_list[6], (FEATS * FEATS, HID), (FEATS * E) ** -0.5, 0.09375),
        "hidden_bias": jnp.clip(jax.random.uniform(key_list[7], (HID,), jnp.float32, -1.0, 1.0), -1.0, 1.0),
        "w_out": gaussian(key_list[8], (HID,), HID ** -0.5, 0.25, (), jnp.float32),
        "targets": jnp.clip(1.0 * jax.random.uniform(key_list[9], (SAMPLES,), jnp.float32) ** steps_of(key_list[9], (SAMPLES,), ((0, 256),), -0.2, 0.2), 0.0, 1.0),
        "hot_ids": with_ends(skewed_ids(key_list[10], (SAMPLES, F_HOT), HOT, 2), jax.random.fold_in(key_list[10], 3), 0, HOT - 1).astype(jnp.int32),
        "cold_slots": draw_cold_slots(jax.random.fold_in(key_list[14], 71), 0),
        "requests": draw_requests(jax.random.fold_in(key_list[14], 71), 0),
        "counts": draw_counts(jax.random.fold_in(key_list[14], 71), 0),
    }


learn_rate = 0.3

def backprop(stacked, targets, w_flat, w_inter, hidden_bias, w_out):
    row_count, feature_count, row_width = stacked.shape
    flattened = stacked.reshape(row_count, feature_count * row_width)
    widened = stacked.astype(jnp.float32)
    pair_dots = (jnp.einsum('sfe,sge->sfg', widened, widened) * row_width ** (-0.5)).astype(jnp.bfloat16)
    pre_act = jnp.dot(flattened, w_flat, preferred_element_type=jnp.float32)
    pre_act = pre_act + jnp.dot(pair_dots.reshape(row_count, feature_count * feature_count), w_inter, preferred_element_type=jnp.float32)
    pre_act = pre_act + hidden_bias
    gated = jax.nn.sigmoid(pre_act)
    logits = lax.optimization_barrier(jnp.sum(pre_act * gated * w_out, axis=-1))
    residual = jax.nn.sigmoid(logits) - targets
    slopes = (residual[:, None] * w_out * gated * (1.0 + pre_act * (1.0 - gated))).astype(jnp.bfloat16)
    back_flat = jnp.dot(slopes, w_flat.T, preferred_element_type=jnp.float32)
    back_pairs = jnp.dot(slopes, w_inter.T, preferred_element_type=jnp.float32).reshape(row_count, feature_count, feature_count)
    mirror = ((back_pairs + jnp.swapaxes(back_pairs, 1, 2)) * row_width ** (-0.5)).astype(jnp.bfloat16)
    return back_flat.reshape(row_count, feature_count, row_width) + jnp.einsum('sfg,sge->sfe', mirror.astype(jnp.float32), widened)

def adagrad_rows(table_rows, accum, gradient):
    accum_new = accum + lax.optimization_barrier(jnp.mean(gradient * gradient, axis=-1))
    updated = table_rows - learn_rate * gradient / jnp.sqrt(accum_new)[:, None]
    return (updated, accum_new)

def requantize(updated, bits, touched):
    grid_step = lax.optimization_barrier(jnp.max(jnp.abs(updated), axis=-1, keepdims=True)) / 8.0
    dither = bits.astype(jnp.float32) * (1.0 / 65280.0) - 0.5
    return jnp.where(touched[:, None], updated + grid_step * dither, updated).astype(jnp.bfloat16)

def reference(cold_table, cold_accum, dither_bits, hot_table, hot_accum, w_flat, w_inter, hidden_bias, w_out, targets, hot_ids, cold_slots, requests, counts):
    device_count = N_SHARD * N_DP
    capacity = requests.shape[1]
    per_device = MB * BATCH
    request_rows = requests.reshape(device_count, MB, N_SHARD, capacity)
    slot_rows = cold_slots.reshape(device_count, per_device, F_COLD)
    hot_rows = hot_ids.reshape(device_count, per_device, F_HOT)
    target_rows = targets.reshape(device_count, per_device)
    micro_index = (jnp.arange(per_device, dtype=jnp.int32) // BATCH)[:, None]

    def visit(totals, per_dev):
        hot_grad, cold_grad = totals
        dev_requests, dev_slots, dev_hot, dev_targets = per_dev
        owners = dev_slots // capacity
        slot_index = dev_slots % capacity
        local_rows = dev_requests[micro_index, owners, slot_index]
        row_id = owners * ROWS_DEV + local_rows
        stacked = jnp.concatenate([cold_table[row_id], hot_table[dev_hot].astype(jnp.bfloat16)], axis=1)
        gradients = backprop(stacked, dev_targets, w_flat, w_inter, hidden_bias, w_out)
        hot_grad = hot_grad + jax.ops.segment_sum(gradients[:, F_COLD:].reshape(-1, E), dev_hot.reshape(-1), num_segments=HOT)
        cold_grad = cold_grad.at[row_id.reshape(-1)].add(gradients[:, :F_COLD].reshape(-1, E))
        return ((hot_grad, cold_grad), None)
    start = (jnp.zeros((HOT, E), jnp.float32), jnp.zeros((COLD_ROWS, E), jnp.float32))
    (hot_grad, cold_grad), _ = lax.scan(visit, start, (request_rows, slot_rows, hot_rows, target_rows))
    live_mask = (jnp.arange(capacity, dtype=jnp.int32)[None, None, None, :] < counts.reshape(device_count, MB, N_SHARD)[..., None]).astype(jnp.float32)
    owner_grid = jnp.arange(N_SHARD, dtype=jnp.int32)[None, None, :, None]
    global_rows = owner_grid * ROWS_DEV + request_rows
    touched = jnp.zeros((COLD_ROWS,), jnp.float32).at[global_rows.reshape(-1)].add(live_mask.reshape(-1))
    averaged = cold_grad / jnp.maximum(touched, 1.0)[:, None]
    updated, cold_accum_out = adagrad_rows(cold_table.astype(jnp.float32), cold_accum, averaged)
    cold_out = requantize(updated, dither_bits, touched > 0.5)
    hot_out, hot_accum_out = adagrad_rows(hot_table, hot_accum, hot_grad)
    return (cold_out, cold_accum_out, hot_out, hot_accum_out)
```

```python
import jax
import jax.numpy as jnp
from jax import lax
from jax.experimental import pallas as pl
from jax.experimental.pallas import tpu as pltpu
from jax.sharding import PartitionSpec as P

MB = 2
BATCH = 256
GROUP = 16
FEATS = 16
F_COLD = 8

learn_rate = 0.3

BF = jnp.bfloat16
F32 = jnp.float32

NT = (((1,), (1,)), ((), ()))


def iota(shape, axis):
    return lax.broadcasted_iota(jnp.int32, shape, axis)


def params(limit_mib):
    return pltpu.CompilerParams(vmem_limit_bytes=limit_mib << 20)


def one_hot(ids, shape, axis, base):
    return jnp.where(iota(shape, axis) + base == ids, 1.0, 0.0)


def fetch_kernel(ids_col, table, rows, hits, hot):
    slots = rows.shape[0]
    count = table.shape[0]
    block = 512
    hits[...] = jnp.zeros_like(hits)

    def step(i, carry):
        at = pl.multiple_of(i * block, block)
        ids = ids_col[pl.ds(at, block), :]
        for k in range(count // 256):
            match = one_hot(ids, (block, 256), 1, k * 256)
            hot[:, k * 256 : (k + 1) * 256] = match.astype(BF)
            hits[:, k * 256 : (k + 1) * 256] += jnp.sum(match, axis=0, keepdims=True)
        rows[pl.ds(at, block), :] = jnp.dot(
            hot[...], table[...], preferred_element_type=F32
        ).astype(BF)
        return carry

    lax.fori_loop(0, slots // block, step, 0)


def fetch_rows(ids_col, table):
    slots, width = ids_col.shape[0], table.shape[1]
    return pl.pallas_call(
        fetch_kernel,
        out_shape=(
            jax.ShapeDtypeStruct((slots, width), BF),
            jax.ShapeDtypeStruct((1, table.shape[0]), F32),
        ),
        scratch_shapes=[pltpu.VMEM((512, table.shape[0]), BF)],
        compiler_params=params(32),
        name="fetch_rows",
    )(ids_col, table)


def step_kernel(
    fetched,
    hotb,
    cold_col,
    hot_col,
    cold_row,
    hot_row,
    targets,
    w_flat,
    w_inter,
    w_inter_t,
    bias,
    w_out,
    hot_prev,
    slot_grad,
    hot_grad,
    x,
    a,
    pairs,
    back,
    mirror,
    g_hi,
    g_lo,
    h_hi,
    h_lo,
    match,
    slopes,
):
    width = fetched.shape[1]
    samples = targets.shape[0]
    groups = samples // GROUP
    lane_group = FEATS * GROUP
    half = F_COLD * GROUP
    scale = width ** (-0.5)
    block = 512
    per_block = block // half

    sq = (lane_group, lane_group)
    i_hi = iota(sq, 0) >> 4
    i_lo = iota(sq, 0) & 15
    j_hi = iota(sq, 1) >> 4
    j_lo = iota(sq, 1) & 15

    def gather(source, col, offset):
        count = source.shape[0]

        def body(b, carry):
            at = pl.multiple_of(b * block, block)
            ids = col[pl.ds(at, block), :]
            for k in range(count // 256):
                match[:, k * 256 : (k + 1) * 256] = one_hot(
                    ids, (block, 256), 1, k * 256
                ).astype(BF)
            picked = jnp.dot(
                match[:, :count], source[...], preferred_element_type=F32
            ).astype(BF)
            for q in range(per_block):
                dst = pl.multiple_of((b * per_block + q) * lane_group + offset, half)
                x[pl.ds(dst, half), :] = picked[q * half : (q + 1) * half]
            return carry

        lax.fori_loop(0, col.shape[0] // block, body, 0)

    gather(fetched, cold_col, 0)
    gather(hotb, hot_col, half)

    spread = jnp.where(i_hi == j_lo, 1.0, 0.0).astype(BF)
    spread_t = jnp.where(i_lo == j_hi, 1.0, 0.0).astype(BF)

    def dots(g, carry):
        rows = pl.ds(pl.multiple_of(g * lane_group, lane_group), lane_group)
        part = pl.ds(pl.multiple_of(g * GROUP, GROUP), GROUP)
        xg = x[rows, :]
        for f in range(FEATS):
            a[part, f * width : (f + 1) * width] = xg[f * GROUP : (f + 1) * GROUP]
        gram = lax.dot_general(xg, xg, NT, preferred_element_type=F32) * scale
        own = jnp.where(i_lo == j_lo, gram, 0.0).astype(BF)
        wide = jnp.dot(own, spread, preferred_element_type=F32)
        wide = jnp.where(i_hi == j_hi, wide, 0.0)
        pairs[part, :] = jnp.sum(
            wide.reshape(FEATS, GROUP, lane_group), axis=0
        ).astype(BF)
        return carry

    lax.fori_loop(0, groups, dots, 0)

    pre = jnp.dot(a[...], w_flat[...], preferred_element_type=F32)
    pre = pre + jnp.dot(pairs[...], w_inter[...], preferred_element_type=F32)
    pre = pre + bias[...]
    gated = jax.nn.sigmoid(pre)
    logits = jnp.sum(pre * gated * w_out[...], axis=-1, keepdims=True)
    residual = jax.nn.sigmoid(logits) - targets[...]
    slopes[...] = (residual * w_out[...] * gated * (1.0 + pre * (1.0 - gated))).astype(BF)

    def flat_back(f, carry):
        rows = pl.ds(pl.multiple_of(f * width, width), width)
        back[f] = lax.dot_general(
            slopes[...], w_flat[rows, :], NT, preferred_element_type=F32
        )
        return carry

    lax.fori_loop(0, FEATS, flat_back, 0)
    both = lax.dot_general(slopes[...], w_inter[...], NT, preferred_element_type=F32)
    both = both + lax.dot_general(slopes[...], w_inter_t[...], NT, preferred_element_type=F32)
    mirror[...] = (both * scale).astype(BF)

    def grads(g, carry):
        rows = pl.ds(pl.multiple_of(g * lane_group, lane_group), lane_group)
        part = pl.ds(pl.multiple_of(g * GROUP, GROUP), GROUP)
        mine = mirror[part, :].astype(F32)
        tall = jnp.broadcast_to(mine[None], (FEATS, GROUP, lane_group)).reshape(sq)
        tall = jnp.where(i_hi == j_hi, tall, 0.0).astype(BF)
        wide = jnp.dot(tall, spread_t, preferred_element_type=F32)
        wide = jnp.where(i_lo == j_lo, wide, 0.0).astype(BF)
        total = jnp.dot(wide, x[rows, :], preferred_element_type=F32)
        flat = back[:, part, :].reshape(lane_group, width)
        total = total + flat
        hi = total.astype(BF)
        lo = (total - hi.astype(F32)).astype(BF)
        dst = pl.ds(pl.multiple_of(g * half, half), half)
        g_hi[dst, :] = hi[:half]
        g_lo[dst, :] = lo[:half]
        h_hi[dst, :] = hi[half:]
        h_lo[dst, :] = lo[half:]
        return carry

    lax.fori_loop(0, groups, grads, 0)

    lookups = cold_row.shape[1]

    def scatter(ids_row, hi, lo, write, count):
        def body(b, carry):
            at = pl.multiple_of(b * block, block)
            for k in range(lookups // 256):
                ids = ids_row[:, k * 256 : (k + 1) * 256]
                match[:, k * 256 : (k + 1) * 256] = one_hot(
                    ids - at, (block, 256), 0, 0
                ).astype(BF)
            total = jnp.dot(match[...], hi[...], preferred_element_type=F32)
            total = total + jnp.dot(match[...], lo[...], preferred_element_type=F32)
            write(pl.ds(at, block), total)
            return carry

        lax.fori_loop(0, count // block, body, 0)

    def write_hot(rows, total):
        if hot_prev is None:
            hot_grad[rows, :] = total
        else:
            hot_grad[rows, :] = total + hot_prev[rows, :]

    def write_slot(rows, total):
        slot_grad[rows, :] = total.astype(BF)

    scatter(cold_row, g_hi, g_lo, write_slot, slot_grad.shape[0])
    scatter(hot_row, h_hi, h_lo, write_hot, hot_grad.shape[0])


def first_step_kernel(*refs):
    step_kernel(*refs[:12], None, *refs[12:])


def backprop(args, hot_prev, slots, hot_count):
    width = args[0].shape[1]
    samples = args[6].shape[0]
    hidden = args[7].shape[1]
    lookups = samples * F_COLD
    wide = FEATS * width
    kernel = step_kernel if hot_prev is not None else first_step_kernel
    extra = () if hot_prev is None else (hot_prev,)
    return pl.pallas_call(
        kernel,
        out_shape=(
            jax.ShapeDtypeStruct((slots, width), BF),
            jax.ShapeDtypeStruct((hot_count, width), F32),
        ),
        scratch_shapes=[
            pltpu.VMEM((samples * FEATS, width), BF),
            pltpu.VMEM((samples, wide), BF),
            pltpu.VMEM((samples, FEATS * FEATS), BF),
            pltpu.VMEM((FEATS, samples, width), F32),
            pltpu.VMEM((samples, FEATS * FEATS), BF),
            pltpu.VMEM((lookups, width), BF),
            pltpu.VMEM((lookups, width), BF),
            pltpu.VMEM((lookups, width), BF),
            pltpu.VMEM((lookups, width), BF),
            pltpu.VMEM((512, 2048), BF),
            pltpu.VMEM((samples, hidden), BF),
        ],
        compiler_params=params(48),
        name="train_step",
    )(*args, *extra)


def owner_body(ids_row, grads, match, write):
    block = 512
    slots = grads.shape[0]
    rows = 2048

    def body(b, carry):
        at = pl.multiple_of(b * block, block)
        for k in range(slots // 256):
            ids = ids_row[:, k * 256 : (k + 1) * 256]
            match[:, k * 256 : (k + 1) * 256] = one_hot(
                ids - at, (block, 256), 0, 0
            ).astype(BF)
        write(b, at, jnp.dot(match[...], grads[...], preferred_element_type=F32))
        return carry

    lax.fori_loop(0, rows // block, body, 0)


def owner_first_kernel(ids_row, grads, out, match):
    def write(b, at, total):
        out[pl.ds(at, 512), :] = total

    owner_body(ids_row, grads, match, write)


def owner_second_kernel(ids_row, grads, prev, hits0, hits1, out, match):
    def write(b, at, total):
        total = (total + prev[pl.ds(at, 512), :]).astype(BF)
        out[b * 2, :256, :] = total[:256]
        out[b * 2 + 1, :256, :] = total[256:]

    owner_body(ids_row, grads, match, write)
    hits = hits0[...] + hits1[...]
    for p in range(out.shape[0]):
        mine = hits[:, p * 256 : (p + 1) * 256]
        out[p, 256:, :] = jnp.broadcast_to(mine, (16, 256)).astype(BF)


def owner_first(ids_row, grads):
    return pl.pallas_call(
        owner_first_kernel,
        out_shape=jax.ShapeDtypeStruct((2048, grads.shape[1]), F32),
        scratch_shapes=[pltpu.VMEM((512, 2048), BF)],
        compiler_params=params(32),
        name="owner_first",
    )(ids_row, grads)


def owner_second(ids_row, grads, prev, hits0, hits1):
    return pl.pallas_call(
        owner_second_kernel,
        out_shape=jax.ShapeDtypeStruct((8, 272, 256), BF),
        scratch_shapes=[pltpu.VMEM((512, 2048), BF)],
        compiler_params=params(32),
        name="owner_second",
    )(ids_row, grads, prev, hits0, hits1)


def to_col(row, eye):
    return jnp.sum(jnp.where(eye, row, 0.0), axis=1, keepdims=True)


def to_row(col, eye):
    return jnp.sum(jnp.where(eye, col, 0.0), axis=0, keepdims=True)


def cold_update_kernel(parts, table, accum, bits, out):
    eye = iota((256, 256), 0) == iota((256, 256), 1)
    total = parts[0].astype(F32)
    for p in range(1, parts.shape[0]):
        total = total + parts[p].astype(F32)
    grad = total[:256]
    touched = to_col(total[256:257], eye)
    averaged = grad / jnp.maximum(touched, 1.0)
    mean = jnp.mean(averaged * averaged, axis=-1, keepdims=True)
    accum_new = to_col(accum[...], eye) + mean
    updated = table[...].astype(F32) - learn_rate * averaged / jnp.sqrt(accum_new)
    grid_step = jnp.max(jnp.abs(updated), axis=-1, keepdims=True) / 8.0
    dither = bits[...].astype(F32) * (1.0 / 65280.0) - 0.5
    out[:256, :] = jnp.where(touched > 0.5, updated + grid_step * dither, updated).astype(BF)
    row = to_row(accum_new, eye)
    high = row.astype(BF)
    rest = row - high.astype(F32)
    middle = rest.astype(BF)
    low = rest - middle.astype(F32)
    at = iota((16, 256), 0)
    packed = jnp.where(
        at == 0, high.astype(F32), jnp.where(at == 1, middle.astype(F32), low)
    )
    out[256:, :] = packed.astype(BF)


def cold_update(parts, table, accum, bits):
    return pl.pallas_call(
        cold_update_kernel,
        out_shape=jax.ShapeDtypeStruct((272, 256), BF),
        compiler_params=params(32),
        name="cold_update",
    )(parts, table, accum, bits)


def adagrad_rows(table_rows, accum, gradient):
    accum_new = accum + jnp.mean(gradient * gradient, axis=-1)
    updated = table_rows - learn_rate * gradient / jnp.sqrt(accum_new)[:, None]
    return (updated, accum_new)


def exchange(value, axis):
    return lax.all_to_all(value, axis, split_axis=0, concat_axis=0, tiled=True)


def on_device(
    cold_table,
    cold_accum,
    dither_bits,
    hot_table,
    hot_accum,
    w_flat,
    w_inter,
    hidden_bias,
    w_out,
    targets,
    hot_ids,
    cold_slots,
    requests,
    counts,
):
    shards = lax.axis_size("shard")
    dps = lax.axis_size("dp")
    capacity = requests.shape[1]
    row_count, row_width = cold_table.shape
    hot_count = hot_table.shape[0]
    slots = shards * capacity

    live = jnp.arange(capacity, dtype=jnp.int32) < counts[:, :, None]
    asked = jnp.where(live, requests.reshape(MB, shards, capacity), -1)
    asked = asked.transpose(1, 0, 2).reshape(shards, MB * capacity)
    wanted = exchange(asked, "shard")
    wanted = [wanted[:, m * capacity : (m + 1) * capacity].reshape(slots) for m in range(MB)]

    def arrange(ids, m):
        part = ids[m * BATCH : (m + 1) * BATCH].reshape(BATCH // GROUP, GROUP, F_COLD)
        return part.transpose(0, 2, 1).reshape(-1)

    hot_bf = hot_table.astype(BF)
    inter_t = w_inter.reshape(FEATS, FEATS, -1).transpose(1, 0, 2).reshape(w_inter.shape)

    served = [fetch_rows(wanted[m].reshape(slots, 1), cold_table) for m in range(MB)]
    fetched = [
        exchange(served[m][0].reshape(shards, capacity, row_width), "shard").reshape(
            slots, row_width
        )
        for m in range(MB)
    ]
    hot_grad = None
    owned = []
    for m in range(MB):
        cold_at = arrange(cold_slots, m)
        hot_at = arrange(hot_ids, m)
        args = (
            fetched[m],
            hot_bf,
            cold_at.reshape(-1, 1),
            hot_at.reshape(-1, 1),
            cold_at.reshape(1, -1),
            hot_at.reshape(1, -1),
            targets[m * BATCH : (m + 1) * BATCH].reshape(-1, 1),
            w_flat,
            w_inter,
            inter_t,
            hidden_bias.reshape(1, -1),
            w_out.reshape(1, -1),
        )
        slot_grad, hot_grad = backprop(args, hot_grad, slots, hot_count)
        owned.append(
            exchange(slot_grad.reshape(shards, capacity, row_width), "shard").reshape(
                slots, row_width
            )
        )

    shard_at = lax.axis_index("shard")
    dp_at = lax.axis_index("dp")
    hot_part = hot_count // dps
    hot_own = hot_part // shards
    hot_sum = jnp.sum(exchange(hot_grad.reshape(dps, hot_part, row_width), "dp"), axis=0)
    hot_sum = jnp.sum(
        exchange(hot_sum.reshape(shards, hot_own, row_width), "shard"), axis=0
    )
    first_hot = dp_at * hot_part + shard_at * hot_own
    hot_new, hot_accum_new = adagrad_rows(
        lax.dynamic_slice(hot_table, (first_hot, 0), (hot_own, row_width)),
        lax.dynamic_slice(hot_accum, (first_hot,), (hot_own,)),
        hot_sum,
    )
    hot_pack = jnp.concatenate(
        [hot_new, jnp.broadcast_to(hot_accum_new[:, None], (hot_own, 128))], axis=1
    )
    hot_all = exchange(jnp.broadcast_to(hot_pack[None], (shards,) + hot_pack.shape), "shard")
    hot_all = hot_all.reshape(hot_part, row_width + 128)
    accum_rows = jnp.broadcast_to(
        jnp.pad(hot_all[:, row_width], (0, row_width - hot_part))[None], (8, row_width)
    )
    hot_all = jnp.concatenate([hot_all[:, :row_width], accum_rows], axis=0)
    hot_all = lax.all_gather(hot_all, "dp", axis=0, tiled=False)
    hot_out = hot_all[:, :hot_part].reshape(hot_count, row_width)
    hot_accum_out = hot_all[:, hot_part, :hot_part].reshape(hot_count)

    cold_part = row_count // dps
    first = owner_first(wanted[0].reshape(1, slots), owned[0])
    parts = owner_second(
        wanted[1].reshape(1, slots), owned[1], first, served[0][1], served[1][1]
    )
    parts = exchange(parts, "dp")
    first_cold = dp_at * cold_part
    packed = cold_update(
        parts,
        lax.dynamic_slice(cold_table, (first_cold, 0), (cold_part, row_width)),
        lax.dynamic_slice(cold_accum, (first_cold,), (cold_part,)).reshape(1, -1),
        lax.dynamic_slice(dither_bits, (first_cold, 0), (cold_part, row_width)),
    )
    cold_all = lax.all_gather(packed, "dp", axis=0, tiled=False)
    cold_out = cold_all[:, :cold_part].reshape(row_count, row_width)
    pieces = cold_all[:, cold_part : cold_part + 3].astype(F32)
    cold_accum_out = ((pieces[:, 2] + pieces[:, 1]) + pieces[:, 0]).reshape(row_count)
    return (cold_out, cold_accum_out, hot_out, hot_accum_out)


def solution(mesh):
    return jax.shard_map(
        on_device,
        mesh=mesh,
        in_specs=(
            P("shard", None),
            P("shard"),
            P("shard", None),
            P(),
            P(),
            P(),
            P(),
            P(),
            P(),
            P(("shard", "dp")),
            P(("shard", "dp"), None),
            P(("shard", "dp"), None),
            P(("shard", "dp"), None),
            P(("shard", "dp"), None),
        ),
        out_specs=(P("shard", None), P("shard"), P(), P()),
        check_vma=False,
    )
```

```python
import jax
import jax.numpy as jnp
from jax import lax
from jax.experimental import pallas as pl
from jax.experimental.pallas import tpu as pltpu
from jax.sharding import PartitionSpec as P


MB = 2
GROUP = 16
FEATS = 16
F_COLD = 8
BF = jnp.bfloat16
F32 = jnp.float32
NT = (((1,), (1,)), ((), ()))
HBM = pl.BlockSpec(memory_space=pltpu.HBM)
VMEM = pl.BlockSpec(memory_space=pltpu.VMEM)
SMEM = pl.BlockSpec(memory_space=pltpu.SMEM)
N_DP = 8
learn_rate = 0.3
UNROLL = 4


def iota(shape, axis):
    return lax.broadcasted_iota(jnp.int32, shape, axis)


def as_one(same):
    return jnp.where(same, jnp.ones(same.shape, BF), jnp.zeros(same.shape, BF))


def params(limit_mib):
    return pltpu.CompilerParams(vmem_limit_bytes=limit_mib << 20)


def load_all(pairs, sems):
    copies = [pltpu.make_async_copy(s, d, sems.at[i]) for i, (s, d) in enumerate(pairs)]
    for c in copies:
        c.start()
    return copies


def match_rows(ids, match, at, count):
    lanes = iota((GROUP, count), 1).astype(jnp.int16)
    for f in range(F_COLD):
        mine = jnp.broadcast_to(ids[:, f : f + 1], (GROUP, 128)).astype(jnp.int16)
        same = lanes == jnp.concatenate([mine] * (count // 128), axis=1)
        match[pl.ds(at + f * GROUP, GROUP), :count] = as_one(same)


def hot_rows_kernel(hot_ids, table, out, ids, src, match, res, sems):
    copies = load_all([(hot_ids, ids), (table, src)], sems)
    for c in copies:
        c.wait()
    source = src[...].astype(BF)
    half = F_COLD * GROUP
    block = 4
    steps = ids.shape[0] // GROUP // block

    def body(b, carry):
        for q in range(block):
            part = pl.ds(pl.multiple_of((b * block + q) * GROUP, GROUP), GROUP)
            match_rows(ids[part, :], match, q * half, source.shape[0])
        rows = pl.ds(pl.multiple_of(b * block * half, block * half), block * half)
        res[rows, :] = jnp.dot(match[...], source, preferred_element_type=F32).astype(BF)
        return carry

    lax.fori_loop(0, steps, body, 0)
    done = pltpu.make_async_copy(res, out, sems.at[2])
    done.start()
    done.wait()


def hot_rows(hot_ids, table):
    count, width = table.shape
    rows = hot_ids.shape[0] * F_COLD
    return pl.pallas_call(
        hot_rows_kernel,
        in_specs=[HBM, HBM],
        out_specs=HBM,
        out_shape=jax.ShapeDtypeStruct((rows, width), BF),
        scratch_shapes=[
            pltpu.VMEM(hot_ids.shape, jnp.int32),
            pltpu.VMEM(table.shape, F32),
            pltpu.VMEM((512, count), BF),
            pltpu.VMEM((rows, width), BF),
            pltpu.SemaphoreType.DMA((3,)),
        ],
        compiler_params=params(32),
        name="hot_rows",
    )(hot_ids, table)


def step_kernel(m, *refs):
    (
        fetched_h, xh_h, slots_h, slots_t_h, targets_h, flat_h, inter_h, bias_h, w_out_h,
        slot_grad, hot_hi, hot_lo,
        fetched, x, slots, slots_t, targets, w_flat, w_inter, bias, w_out,
        a, pairs, back, mirror, g_hi, g_lo, h_hi, h_lo, match, slopes, sems,
    ) = refs
    width = fetched.shape[1]
    samples = targets.shape[1]
    groups = samples // GROUP
    lane_group = FEATS * GROUP
    half = F_COLD * GROUP
    scale = width ** (-0.5)
    block = 4
    first = m * samples

    head = load_all(
        [
            (slots_h.at[pl.ds(first, samples), :], slots),
            (fetched_h, fetched),
        ],
        sems,
    )
    hot_copies = [
        pltpu.make_async_copy(
            xh_h.at[pl.ds((m * groups + g) * half, half), :],
            x.at[pl.ds(g * lane_group + half, half), :],
            sems.at[2],
        )
        for g in range(groups)
    ]
    for c in hot_copies:
        c.start()
    tail = load_all(
        [
            (flat_h, w_flat),
            (inter_h, w_inter),
            (bias_h, bias),
            (w_out_h, w_out),
            (targets_h.at[:, pl.ds(first, samples)], targets),
            (slots_t_h.at[:, pl.ds(first, samples)], slots_t),
        ],
        sems.at[pl.ds(3, 6)],
    )

    sq = (lane_group, lane_group)
    i_hi = iota(sq, 0) >> 4
    i_lo = iota(sq, 0) & 15
    j_hi = iota(sq, 1) >> 4
    j_lo = iota(sq, 1) & 15
    spread = jnp.where(i_hi == j_lo, 1.0, 0.0).astype(BF)
    spread_t = jnp.where(i_lo == j_hi, 1.0, 0.0).astype(BF)
    swap = jnp.where((i_hi == j_lo) & (i_lo == j_hi), 1.0, 0.0).astype(BF)

    for c in head:
        c.wait()

    def gather(b, carry):
        for q in range(block):
            part = pl.ds(pl.multiple_of((b * block + q) * GROUP, GROUP), GROUP)
            match_rows(slots[part, :], match, q * half, fetched.shape[0])
        picked = jnp.dot(match[...], fetched[...], preferred_element_type=F32).astype(BF)
        for q in range(block):
            dst = pl.multiple_of((b * block + q) * lane_group, lane_group)
            x[pl.ds(dst, half), :] = picked[q * half : (q + 1) * half]
        return carry

    lax.fori_loop(0, groups // block, gather, 0)
    for c in hot_copies:
        c.wait()

    def dots(i, carry):
        for u in range(UNROLL):
            g = i * UNROLL + u
            rows = pl.ds(pl.multiple_of(g * lane_group, lane_group), lane_group)
            part = pl.ds(pl.multiple_of(g * GROUP, GROUP), GROUP)
            xg = x[rows, :]
            for f in range(FEATS):
                a[part, f * width : (f + 1) * width] = xg[f * GROUP : (f + 1) * GROUP]
            gram = lax.dot_general(xg, xg, NT, preferred_element_type=F32) * scale
            own = jnp.where(i_lo == j_lo, gram, 0.0).astype(BF)
            wide = jnp.dot(own, spread, preferred_element_type=F32)
            wide = jnp.where(i_hi == j_hi, wide, 0.0)
            pairs[part, :] = jnp.sum(
                wide.reshape(FEATS, GROUP, lane_group), axis=0
            ).astype(BF)
        return carry

    lax.fori_loop(0, groups // UNROLL, dots, 0)
    for c in tail:
        c.wait()

    pre = jnp.dot(a[...], w_flat[...], preferred_element_type=F32)
    pre = pre + jnp.dot(pairs[...], w_inter[...], preferred_element_type=F32)
    pre = pre + bias[...]
    gated = jax.nn.sigmoid(pre)
    logits = jnp.sum(pre * gated * w_out[...], axis=-1, keepdims=True)
    eye = iota((samples, samples), 0) == iota((samples, samples), 1)
    target = jnp.sum(jnp.where(eye, targets[...], 0.0), axis=1, keepdims=True)
    residual = jax.nn.sigmoid(logits) - target
    slopes[...] = (residual * w_out[...] * gated * (1.0 + pre * (1.0 - gated))).astype(BF)

    inter_t = jnp.dot(swap, w_inter[...], preferred_element_type=F32).astype(BF)
    both = lax.dot_general(slopes[...], w_inter[...], NT, preferred_element_type=F32)
    both = both + lax.dot_general(slopes[...], inter_t, NT, preferred_element_type=F32)
    mirror[...] = (both * scale).astype(BF)

    def flat_back(f, carry):
        rows = pl.ds(pl.multiple_of(f * width, width), width)
        back[f] = lax.dot_general(
            slopes[...], w_flat[rows, :], NT, preferred_element_type=F32
        )
        return carry

    lax.fori_loop(0, FEATS, flat_back, 0)

    def grads(i, carry):
        for u in range(UNROLL):
            g = i * UNROLL + u
            rows = pl.ds(pl.multiple_of(g * lane_group, lane_group), lane_group)
            part = pl.ds(pl.multiple_of(g * GROUP, GROUP), GROUP)
            mine = mirror[part, :].astype(F32)
            tall = jnp.broadcast_to(mine[None], (FEATS, GROUP, lane_group)).reshape(sq)
            tall = jnp.where(i_hi == j_hi, tall, 0.0).astype(BF)
            wide = jnp.dot(tall, spread_t, preferred_element_type=F32)
            wide = jnp.where(i_lo == j_lo, wide, 0.0).astype(BF)
            total = jnp.dot(wide, x[rows, :], preferred_element_type=F32)
            total = total + back[:, part, :].reshape(lane_group, width)
            hi = total.astype(BF)
            lo = (total - hi.astype(F32)).astype(BF)
            for f in range(F_COLD):
                dst = pl.ds(pl.multiple_of(f * samples + g * GROUP, GROUP), GROUP)
                at = f * GROUP
                g_hi[dst, :] = hi[at : at + GROUP]
                g_lo[dst, :] = lo[at : at + GROUP]
                h_hi[dst, :] = hi[half + at : half + at + GROUP]
                h_lo[dst, :] = lo[half + at : half + at + GROUP]
        return carry

    lax.fori_loop(0, groups // UNROLL, grads, 0)
    outs = load_all([(h_hi, hot_hi), (h_lo, hot_lo)], sems.at[pl.ds(0, 2)])

    rows_blk = 512

    def scatter(b, carry):
        at = pl.multiple_of(b * rows_blk, rows_blk)
        subs = iota((rows_blk, samples), 0).astype(jnp.int16)
        for f in range(F_COLD):
            mine = jnp.broadcast_to(slots_t[f : f + 1, :] - at, (16, samples)).astype(jnp.int16)
            same = subs == jnp.concatenate([mine] * (rows_blk // 16), axis=0)
            match[:, f * samples : (f + 1) * samples] = as_one(same)
        total = jnp.dot(match[...], g_hi[...], preferred_element_type=F32)
        total = total + jnp.dot(match[...], g_lo[...], preferred_element_type=F32)
        fetched[pl.ds(at, rows_blk), :] = total.astype(BF)
        pltpu.make_async_copy(
            fetched.at[pl.ds(at, rows_blk), :], slot_grad.at[pl.ds(at, rows_blk), :], sems.at[3 + b]
        ).start()
        return carry

    n_out = slot_grad.shape[0] // rows_blk
    lax.fori_loop(0, n_out, scatter, 0)
    for b in range(n_out):
        pltpu.make_async_copy(
            fetched.at[pl.ds(b * rows_blk, rows_blk), :],
            slot_grad.at[pl.ds(b * rows_blk, rows_blk), :],
            sems.at[3 + b],
        ).wait()
    for c in outs:
        c.wait()


def backprop(m, fetched, xh, slots, slots_t, targets, w_flat, w_inter, bias, w_out):
    count, width = fetched.shape
    samples = slots.shape[0] // MB
    hidden = w_flat.shape[1]
    lookups = samples * F_COLD
    wide = FEATS * width
    rows = jax.ShapeDtypeStruct((lookups, width), BF)
    return pl.pallas_call(
        lambda *refs: step_kernel(m, *refs),
        in_specs=[HBM] * 9,
        out_specs=(HBM,) * 3,
        out_shape=(jax.ShapeDtypeStruct((count, width), BF), rows, rows),
        scratch_shapes=[
            pltpu.VMEM((count, width), BF),
            pltpu.VMEM((samples * FEATS, width), BF),
            pltpu.VMEM((samples, F_COLD), jnp.int32),
            pltpu.VMEM((F_COLD, samples), jnp.int32),
            pltpu.VMEM((1, samples), F32),
            pltpu.VMEM(w_flat.shape, BF),
            pltpu.VMEM(w_inter.shape, BF),
            pltpu.VMEM((1, hidden), F32),
            pltpu.VMEM((1, hidden), F32),
            pltpu.VMEM((samples, wide), BF),
            pltpu.VMEM((samples, FEATS * FEATS), BF),
            pltpu.VMEM((FEATS, samples, width), F32),
            pltpu.VMEM((samples, FEATS * FEATS), BF),
            pltpu.VMEM((lookups, width), BF),
            pltpu.VMEM((lookups, width), BF),
            pltpu.VMEM((lookups, width), BF),
            pltpu.VMEM((lookups, width), BF),
            pltpu.VMEM((512, 2048), BF),
            pltpu.VMEM((samples, hidden), BF),
            pltpu.SemaphoreType.DMA((9,)),
        ],
        compiler_params=params(48),
        name="train_step",
    )(fetched, xh, slots, slots_t, targets, w_flat, w_inter, bias, w_out)


def hot_scatter_kernel(at_ref, ids_h, hi0, lo0, hi1, lo1, *refs):
    outs = refs[:N_DP]
    ids, h0, l0, h1, l1, match, res, sems = refs[N_DP:]
    copies = load_all([(ids_h, ids), (hi0, h0), (lo0, l0), (hi1, h1), (lo1, l1)], sems)
    samples = ids.shape[1] // MB
    block = 256
    subs = iota((block, samples), 0).astype(jnp.int16)
    for c in copies:
        c.wait()

    def body(b, carry):
        at = pl.multiple_of(b * block, block)
        total = None
        for m, parts in enumerate(((h0, l0), (h1, l1))):
            for f in range(F_COLD):
                row = ids[f : f + 1, m * samples : (m + 1) * samples] - at
                mine = jnp.broadcast_to(row, (16, samples)).astype(jnp.int16)
                same = subs == jnp.concatenate([mine] * (block // 16), axis=0)
                match[m, :, f * samples : (f + 1) * samples] = as_one(same)
            for part in parts:
                term = jnp.dot(match[m], part[...], preferred_element_type=F32)
                total = term if total is None else total + term
        res[pl.ds(at, block), :] = total
        return carry

    lax.fori_loop(0, res.shape[0] // block, body, 0)
    size = res.shape[0] // N_DP
    done = []
    for k in range(N_DP):
        chunk = (at_ref[0] + k) & (N_DP - 1)
        src = res.at[pl.ds(pl.multiple_of(chunk * size, size), size), :]
        done.append(pltpu.make_async_copy(src, outs[k], sems.at[k]))
        done[-1].start()
    for c in done:
        c.wait()


def hot_scatter(dp_at, ids, hi0, lo0, hi1, lo1, count):
    rows, width = hi0.shape
    return pl.pallas_call(
        hot_scatter_kernel,
        in_specs=[SMEM] + [HBM] * 5,
        out_specs=(HBM,) * N_DP,
        out_shape=(jax.ShapeDtypeStruct((count // N_DP, width), F32),) * N_DP,
        scratch_shapes=[pltpu.VMEM(ids.shape, jnp.int32)]
        + [pltpu.VMEM((rows, width), BF)] * 4
        + [
            pltpu.VMEM((MB, 256, rows), BF),
            pltpu.VMEM((count, width), F32),
            pltpu.SemaphoreType.DMA((N_DP,)),
        ],
        compiler_params=params(32),
        name="hot_scatter",
    )(dp_at, ids, hi0, lo0, hi1, lo1)


def serve_kernel(m, with_hits, wanted, table, rows, *refs):
    if with_hits:
        hits, match, res, count_acc, sems = refs
    else:
        match, res, sems = refs
    shards, lanes = wanted.shape
    capacity = lanes // MB
    count = table.shape[0]
    per = 8
    block = per * capacity
    ids = jnp.concatenate([wanted[...], jnp.zeros((lanes - shards, lanes), jnp.int32)], axis=0)
    turned = ids.T
    names = iota((capacity, count), 1).astype(jnp.int16)
    if with_hits:
        count_acc[...] = jnp.zeros_like(count_acc)

    def ones_of(part, mb, j):
        col = part[mb * capacity : (mb + 1) * capacity, j : j + 1]
        mine = jnp.broadcast_to(col, (capacity, 128)).astype(jnp.int16)
        return as_one(names == jnp.concatenate([mine] * (count // 128), axis=1))

    def add_hits(one):
        tall = one[0:16] + one[16:32] + one[32:48] + one[48:64]
        count_acc[...] += tall

    def body(b, carry):
        part = pltpu.roll(turned, lanes - b * per, 1)
        for j in range(per):
            one = ones_of(part, m, j)
            match[j * capacity : (j + 1) * capacity, :] = one
            if with_hits:
                add_hits(one)
                for other in range(MB):
                    if other != m:
                        add_hits(ones_of(part, other, j))
        at = pl.ds(pl.multiple_of(b * block, block), block)
        res[at, :] = jnp.dot(match[...], table[...], preferred_element_type=F32).astype(BF)
        pltpu.make_async_copy(res.at[at, :], rows.at[at, :], sems.at[b]).start()
        return carry

    steps = shards // per
    lax.fori_loop(0, steps, body, 0)
    if with_hits:
        hits[...] = jnp.sum(count_acc[...].astype(F32), axis=0, keepdims=True)
    for b in range(steps):
        at = pl.ds(b * block, block)
        pltpu.make_async_copy(res.at[at, :], rows.at[at, :], sems.at[b]).wait()


def serve(m, with_hits, wanted, table):
    shards, lanes = wanted.shape
    capacity = lanes // MB
    slots = shards * capacity
    count, width = table.shape
    rows = jax.ShapeDtypeStruct((slots, width), BF)
    extra = [pltpu.VMEM((16, count), BF)] if with_hits else []
    return pl.pallas_call(
        lambda *refs: serve_kernel(m, with_hits, *refs),
        in_specs=[VMEM, VMEM],
        out_specs=(HBM, VMEM) if with_hits else HBM,
        out_shape=(rows, jax.ShapeDtypeStruct((1, count), F32)) if with_hits else rows,
        scratch_shapes=[pltpu.VMEM((512, count), BF), pltpu.VMEM((slots, width), BF)]
        + extra
        + [pltpu.SemaphoreType.DMA((shards // 8,))],
        compiler_params=params(24),
        name="serve_rows",
    )(wanted, table)


def id_tiles(wanted, m):
    ids = wanted[...]
    other = pltpu.roll(ids, 64, 1)
    left, right = (ids, other) if m == 0 else (other, ids)
    low = iota((1, 128), 1) < 64
    return [
        jnp.where(low, left[2 * i : 2 * i + 1], right[2 * i + 1 : 2 * i + 2])
        for i in range(ids.shape[0] // 2)
    ]


def owner_match(tiles, base, match, subs):
    size = match.shape[0]
    for i, tile in enumerate(tiles):
        mine = jnp.broadcast_to(tile - base, (16, 128)).astype(jnp.int16)
        same = subs == jnp.concatenate([mine] * (size // 16), axis=0)
        match[:, i * 128 : (i + 1) * 128] = as_one(same)


def owner_first_kernel(wanted, grads_h, out, grads, match, res, sems):
    load = pltpu.make_async_copy(grads_h, grads, sems.at[0])
    load.start()
    block = match.shape[0]
    tiles = id_tiles(wanted, 0)
    subs = iota((block, 128), 0).astype(jnp.int16)
    load.wait()

    def body(b, carry):
        at = pl.multiple_of(b * block, block)
        owner_match(tiles, at, match, subs)
        res[pl.ds(at, block), :] = jnp.dot(match[...], grads[...], preferred_element_type=F32)
        return carry

    lax.fori_loop(0, res.shape[0] // block, body, 0)
    done = pltpu.make_async_copy(res, out, sems.at[1])
    done.start()
    done.wait()


def owner_first(wanted, grads, count):
    slots, width = grads.shape
    return pl.pallas_call(
        owner_first_kernel,
        in_specs=[VMEM, HBM],
        out_specs=HBM,
        out_shape=jax.ShapeDtypeStruct((count, width), F32),
        scratch_shapes=[
            pltpu.VMEM((slots, width), BF),
            pltpu.VMEM((512, slots), BF),
            pltpu.VMEM((count, width), F32),
            pltpu.SemaphoreType.DMA((2,)),
        ],
        compiler_params=params(24),
        name="owner_first",
    )(wanted, grads)


def owner_second_kernel(at_ref, wanted, hits, grads_h, prev_h, *refs):
    outs = refs[:N_DP]
    grads, prev, match, res, sems = refs[N_DP:]
    size = match.shape[0]
    load = pltpu.make_async_copy(grads_h, grads, sems.at[0])
    load.start()
    load_prev = pltpu.make_async_copy(prev_h, prev, sems.at[1])
    load_prev.start()
    tiles = id_tiles(wanted, 1)
    subs = iota((size, 128), 0).astype(jnp.int16)
    for k in range(N_DP):
        chunk = (at_ref[0] + k) & (N_DP - 1)
        at = pl.multiple_of(chunk * size, size)
        owner_match(tiles, at, match, subs)
        if k == 0:
            load.wait()
        total = jnp.dot(match[...], grads[...], preferred_element_type=F32)
        if k == 0:
            load_prev.wait()
        total = total + prev[pl.ds(at, size), :]
        res[k, :size, :] = total.astype(BF)
        mine = hits[pl.ds(chunk, 1), :]
        res[k, size:, :] = jnp.broadcast_to(mine, (16, size)).astype(BF)
        pltpu.make_async_copy(res.at[k], outs[k], sems.at[2 + k]).start()
    for k in range(N_DP):
        pltpu.make_async_copy(res.at[k], outs[k], sems.at[2 + k]).wait()


def owner_second(dp_at, wanted, hits, grads, prev):
    slots, width = grads.shape
    count = prev.shape[0]
    size = count // N_DP
    return pl.pallas_call(
        owner_second_kernel,
        in_specs=[SMEM, VMEM, VMEM, HBM, HBM],
        out_specs=(HBM,) * N_DP,
        out_shape=(jax.ShapeDtypeStruct((size + 16, width), BF),) * N_DP,
        scratch_shapes=[
            pltpu.VMEM((slots, width), BF),
            pltpu.VMEM((count, width), F32),
            pltpu.VMEM((size, slots), BF),
            pltpu.VMEM((N_DP, size + 16, width), BF),
            pltpu.SemaphoreType.DMA((2 + N_DP,)),
        ],
        compiler_params=params(24),
        name="owner_second",
    )(dp_at, wanted, hits, grads, prev)


def to_col(row, eye):
    return jnp.sum(jnp.where(eye, row, 0.0), axis=1, keepdims=True)


def to_row(col, eye):
    return jnp.sum(jnp.where(eye, col, 0.0), axis=0, keepdims=True)


def adagrad(table, accum, grad):
    accum_new = accum + jnp.mean(grad * grad, axis=-1, keepdims=True)
    return table - learn_rate * grad / jnp.sqrt(accum_new), accum_new


def cold_update_kernel(at_ref, table_h, accum_h, bits_h, *refs):
    parts_h = refs[:N_DP]
    out = refs[N_DP]
    parts, table, accum, bits, res, sems = refs[N_DP + 1 :]
    size = table.shape[0]
    at = pl.multiple_of(at_ref[0] * size, size)
    copies = load_all(
        [(parts_h[k], parts.at[k]) for k in range(N_DP)]
        + [
            (table_h.at[pl.ds(at, size), :], table),
            (accum_h, accum),
            (bits_h.at[pl.ds(at, size), :], bits),
        ],
        sems,
    )
    eye = iota((size, size), 0) == iota((size, size), 1)
    for c in copies:
        c.wait()
    total = parts[0].astype(F32)
    for k in range(1, N_DP):
        total = total + parts[k].astype(F32)
    touched = to_col(total[size : size + 1], eye)
    averaged = total[:size] / jnp.maximum(touched, 1.0)
    old = to_col(accum[pl.ds(at_ref[0], 1), :], eye)
    updated, accum_new = adagrad(table[...].astype(F32), old, averaged)
    grid_step = jnp.max(jnp.abs(updated), axis=-1, keepdims=True) / 8.0
    dither = bits[...].astype(F32) * (1.0 / 65280.0) - 0.5
    res[:size, :] = jnp.where(touched > 0.5, updated + grid_step * dither, updated).astype(BF)
    row = to_row(accum_new, eye)
    high = row.astype(BF).astype(F32)
    middle = (row - high).astype(BF).astype(F32)
    low = (row - high) - middle
    which = iota((16, size), 0)
    packed = jnp.where(which == 0, high, jnp.where(which == 1, middle, low))
    res[size:, :] = packed.astype(BF)
    done = pltpu.make_async_copy(res, out, sems.at[0])
    done.start()
    done.wait()


def cold_update(dp_at, table, accum, bits, parts):
    width = table.shape[1]
    size = table.shape[0] // N_DP
    packed = parts[0].shape
    return pl.pallas_call(
        cold_update_kernel,
        in_specs=[SMEM] + [HBM] * (3 + N_DP),
        out_specs=HBM,
        out_shape=jax.ShapeDtypeStruct(packed, BF),
        scratch_shapes=[
            pltpu.VMEM((N_DP,) + packed, BF),
            pltpu.VMEM((size, width), BF),
            pltpu.VMEM(accum.shape, F32),
            pltpu.VMEM((size, width), jnp.int32),
            pltpu.VMEM(packed, BF),
            pltpu.SemaphoreType.DMA((N_DP + 3,)),
        ],
        compiler_params=params(24),
        name="cold_update",
    )(dp_at, table, accum, bits, *parts)


def cold_join_kernel(at_ref, *refs):
    parts = refs[:N_DP]
    out, accum_out, pieces, sems = refs[N_DP:]
    size = out.shape[0] // N_DP
    copies = []
    for k in range(N_DP):
        chunk = (at_ref[0] - k) & (N_DP - 1)
        dst = out.at[pl.ds(pl.multiple_of(chunk * size, size), size), :]
        copies.append(pltpu.make_async_copy(parts[k].at[pl.ds(0, size), :], dst, sems.at[k]))
        copies.append(
            pltpu.make_async_copy(
                parts[k].at[pl.ds(size, 16), :], pieces.at[chunk], sems.at[N_DP + k]
            )
        )
    for c in copies:
        c.start()
    for c in copies:
        c.wait()
    for p in range(N_DP):
        rows = pieces[p].astype(F32)
        accum_out[p : p + 1, :] = (rows[2:3] + rows[1:2]) + rows[0:1]


def cold_join(dp_at, parts):
    width = parts[0].shape[1]
    size = parts[0].shape[0] - 16
    return pl.pallas_call(
        cold_join_kernel,
        in_specs=[SMEM] + [HBM] * N_DP,
        out_specs=(HBM, VMEM),
        out_shape=(
            jax.ShapeDtypeStruct((N_DP * size, width), BF),
            jax.ShapeDtypeStruct((N_DP, size), F32),
        ),
        scratch_shapes=[
            pltpu.VMEM((N_DP, 16, width), BF),
            pltpu.SemaphoreType.DMA((2 * N_DP,)),
        ],
        compiler_params=params(16),
        name="cold_join",
    )(dp_at, *parts)


def sum_parts_kernel(*refs):
    parts_h = refs[:N_DP]
    out, parts, sems = refs[N_DP:]
    copies = load_all([(parts_h[k], parts.at[k]) for k in range(N_DP)], sems)
    for c in copies:
        c.wait()
    out[...] = jnp.sum(parts[...], axis=0)


def sum_parts(parts):
    shape = parts[0].shape
    return pl.pallas_call(
        sum_parts_kernel,
        in_specs=[HBM] * N_DP,
        out_specs=VMEM,
        out_shape=jax.ShapeDtypeStruct(shape, F32),
        scratch_shapes=[
            pltpu.VMEM((N_DP,) + shape, F32),
            pltpu.SemaphoreType.DMA((N_DP,)),
        ],
        compiler_params=params(16),
        name="sum_parts",
    )(*parts)


def hot_update_kernel(at_ref, table_h, accum_h, *refs):
    grads_h = refs[:N_DP]
    out, accum_out, table, accum, grads, res, sems = refs[N_DP:]
    size = grads.shape[1]
    copies = load_all(
        [(table_h, table), (accum_h, accum)]
        + [(grads_h[k], grads.at[k]) for k in range(N_DP)],
        sems,
    )
    eye = iota((size, size), 0) == iota((size, size), 1)
    for c in copies:
        c.wait()
    for k in range(N_DP):
        chunk = (at_ref[0] - k) & (N_DP - 1)
        rows = pl.ds(pl.multiple_of(chunk * size, size), size)
        old = to_col(accum[pl.ds(chunk, 1), :], eye)
        updated, accum_new = adagrad(table[rows, :], old, grads[k])
        res[rows, :] = updated
        accum_out[pl.ds(chunk, 1), :] = to_row(accum_new, eye)
    done = pltpu.make_async_copy(res, out, sems.at[0])
    done.start()
    done.wait()


def hot_update(dp_at, table, accum, grads):
    count, width = table.shape
    size = count // N_DP
    return pl.pallas_call(
        hot_update_kernel,
        in_specs=[SMEM] + [HBM] * (2 + N_DP),
        out_specs=(HBM, VMEM),
        out_shape=(
            jax.ShapeDtypeStruct((count, width), F32),
            jax.ShapeDtypeStruct((N_DP, size), F32),
        ),
        scratch_shapes=[
            pltpu.VMEM((count, width), F32),
            pltpu.VMEM((N_DP, size), F32),
            pltpu.VMEM((N_DP, size, width), F32),
            pltpu.VMEM((count, width), F32),
            pltpu.SemaphoreType.DMA((2 + N_DP,)),
        ],
        compiler_params=params(24),
        name="hot_update",
    )(dp_at, table, accum, *grads)


def exchange(value, axis):
    return lax.all_to_all(value, axis, split_axis=0, concat_axis=0, tiled=True)


def shift(value, k):
    return lax.ppermute(value, "dp", [(i, (i + k) % N_DP) for i in range(N_DP)])


def to_owners(parts):
    return [parts[0]] + [shift(parts[k], k) for k in range(1, N_DP)]


def to_all(part):
    return [part] + [shift(part, k) for k in range(1, N_DP)]


def step(
    cold_table,
    cold_accum,
    dither_bits,
    hot_table,
    hot_accum,
    w_flat,
    w_inter,
    hidden_bias,
    w_out,
    targets,
    hot_ids,
    cold_slots,
    requests,
    counts,
):
    shards = lax.axis_size("shard")
    capacity = requests.shape[1]
    row_count, row_width = cold_table.shape
    hot_count = hot_table.shape[0]
    slots = shards * capacity
    dp_at = lax.axis_index("dp").astype(jnp.int32).reshape(1)

    live = jnp.arange(capacity, dtype=jnp.int32) < counts[:, :, None]
    asked = jnp.where(live, requests.reshape(MB, shards, capacity), -1)
    asked = asked.transpose(1, 0, 2).reshape(shards, MB * capacity)
    wanted = exchange(asked, "shard")

    fetched = []
    for m in range(MB):
        rows = serve(m, m == 1, wanted, cold_table)
        if m == 1:
            rows, hits = rows
        rows = exchange(rows.reshape(shards, capacity, row_width), "shard")
        fetched.append(rows.reshape(slots, row_width))
    xh = hot_rows(hot_ids, hot_table)

    owned = []
    hot_parts = []
    for m in range(MB):
        slot_grad, *hot_part = backprop(
            m,
            fetched[m],
            xh,
            cold_slots,
            cold_slots.T,
            targets.reshape(1, -1),
            w_flat,
            w_inter,
            hidden_bias.reshape(1, -1),
            w_out.reshape(1, -1),
        )
        hot_parts += hot_part
        rows = exchange(slot_grad.reshape(shards, capacity, row_width), "shard")
        owned.append(rows.reshape(slots, row_width))

    hot_grads = hot_scatter(dp_at, hot_ids.T, *hot_parts, hot_count)
    hot_grads = to_owners(hot_grads)
    hot_sum = sum_parts(hot_grads)
    hot_size = hot_sum.shape[0]
    hot_sum = exchange(hot_sum.reshape(shards, hot_size // shards, row_width), "shard")
    hot_sum = jnp.sum(hot_sum, axis=0)
    hot_all = exchange(jnp.broadcast_to(hot_sum[None], (shards,) + hot_sum.shape), "shard")
    hot_all = to_all(hot_all.reshape(hot_size, row_width))
    hot_out, hot_accum_out = hot_update(
        dp_at, hot_table, hot_accum.reshape(N_DP, -1), hot_all
    )

    first = owner_first(wanted, owned[0], row_count)
    parts = owner_second(dp_at, wanted, hits.reshape(N_DP, -1), owned[1], first)
    parts = to_owners(parts)
    packed = cold_update(
        dp_at, cold_table, cold_accum.reshape(N_DP, -1), dither_bits, parts
    )
    parts = to_all(packed)
    cold_out, cold_accum_out = cold_join(dp_at, parts)
    return (cold_out, cold_accum_out.reshape(-1), hot_out, hot_accum_out.reshape(-1))


def solution(mesh):
    return jax.shard_map(
        step,
        mesh=mesh,
        in_specs=(
            P("shard", None),
            P("shard"),
            P("shard", None),
            P(),
            P(),
            P(),
            P(),
            P(),
            P(),
            P(("shard", "dp")),
            P(("shard", "dp"), None),
            P(("shard", "dp"), None),
            P(("shard", "dp"), None),
            P(("shard", "dp"), None),
        ),
        out_specs=(P("shard", None), P("shard"), P(), P()),
        check_vma=False,
    )
```

```python
import jax
import jax.numpy as jnp
from jax import lax
from jax.experimental import pallas as pl
from jax.experimental.pallas import tpu as pltpu
from jax.sharding import PartitionSpec as P


MB = 2
GROUP = 16
FEATS = 16
F_COLD = 8
BF = jnp.bfloat16
F32 = jnp.float32
NT = (((1,), (1,)), ((), ()))
HBM = pl.BlockSpec(memory_space=pltpu.HBM)
VMEM = pl.BlockSpec(memory_space=pltpu.VMEM)
SMEM = pl.BlockSpec(memory_space=pltpu.SMEM)
N_DP = 8
VMEM_LIMIT = (64 << 20) - (64 << 10)
learn_rate = 0.3
UNROLL = 4


def iota(shape, axis):
    return lax.broadcasted_iota(jnp.int32, shape, axis)


def as_one(same):
    return jnp.where(same, jnp.ones(same.shape, BF), jnp.zeros(same.shape, BF))


def params():
    return pltpu.CompilerParams(vmem_limit_bytes=VMEM_LIMIT)


def load_all(pairs, sems):
    copies = [pltpu.make_async_copy(s, d, sems.at[i]) for i, (s, d) in enumerate(pairs)]
    for c in copies:
        c.start()
    return copies


def match_rows(ids, match, at, count):
    lanes = iota((GROUP, count), 1).astype(jnp.int16)
    for f in range(F_COLD):
        mine = jnp.broadcast_to(ids[:, f : f + 1], (GROUP, 128)).astype(jnp.int16)
        same = lanes == jnp.concatenate([mine] * (count // 128), axis=1)
        match[pl.ds(at + f * GROUP, GROUP), :count] = as_one(same)


def hot_rows_kernel(hot_ids, table, out, ids, src, match, res, sems):
    copies = load_all([(hot_ids, ids), (table, src)], sems)
    for c in copies:
        c.wait()
    source = src[...].astype(BF)
    half = F_COLD * GROUP
    block = 4
    steps = ids.shape[0] // GROUP // block

    def body(b, carry):
        for q in range(block):
            part = pl.ds(pl.multiple_of((b * block + q) * GROUP, GROUP), GROUP)
            match_rows(ids[part, :], match, q * half, source.shape[0])
        rows = pl.ds(pl.multiple_of(b * block * half, block * half), block * half)
        res[rows, :] = jnp.dot(match[...], source, preferred_element_type=F32).astype(BF)
        return carry

    lax.fori_loop(0, steps, body, 0)
    done = pltpu.make_async_copy(res, out, sems.at[2])
    done.start()
    done.wait()


def hot_rows(hot_ids, table):
    count, width = table.shape
    rows = hot_ids.shape[0] * F_COLD
    return pl.pallas_call(
        hot_rows_kernel,
        in_specs=[HBM, HBM],
        out_specs=HBM,
        out_shape=jax.ShapeDtypeStruct((rows, width), BF),
        scratch_shapes=[
            pltpu.VMEM(hot_ids.shape, jnp.int32),
            pltpu.VMEM(table.shape, F32),
            pltpu.VMEM((512, count), BF),
            pltpu.VMEM((rows, width), BF),
            pltpu.SemaphoreType.DMA((3,)),
        ],
        compiler_params=params(),
        name="hot_rows",
    )(hot_ids, table)


def step_kernel(m, *refs):
    (
        fetched_h, xh_h, slots_h, slots_t_h, targets_h, flat_h, inter_h, bias_h, w_out_h,
        slot_grad, hot_hi, hot_lo,
        fetched, x, slots, slots_t, targets, w_flat, w_inter, bias, w_out,
        a, pairs, back, mirror, g_hi, g_lo, h_hi, h_lo, match, slopes, sems,
    ) = refs
    width = fetched.shape[1]
    samples = targets.shape[1]
    groups = samples // GROUP
    lane_group = FEATS * GROUP
    half = F_COLD * GROUP
    scale = width ** (-0.5)
    block = 4
    first = m * samples

    head = load_all(
        [
            (slots_h.at[pl.ds(first, samples), :], slots),
            (fetched_h, fetched),
        ],
        sems,
    )
    hot_copies = [
        pltpu.make_async_copy(
            xh_h.at[pl.ds((m * groups + g) * half, half), :],
            x.at[pl.ds(g * lane_group + half, half), :],
            sems.at[2],
        )
        for g in range(groups)
    ]
    for c in hot_copies:
        c.start()
    tail = load_all(
        [
            (flat_h, w_flat),
            (inter_h, w_inter),
            (bias_h, bias),
            (w_out_h, w_out),
            (targets_h.at[:, pl.ds(first, samples)], targets),
            (slots_t_h.at[:, pl.ds(first, samples)], slots_t),
        ],
        sems.at[pl.ds(3, 6)],
    )

    sq = (lane_group, lane_group)
    i_hi = iota(sq, 0) >> 4
    i_lo = iota(sq, 0) & 15
    j_hi = iota(sq, 1) >> 4
    j_lo = iota(sq, 1) & 15
    spread = jnp.where(i_hi == j_lo, 1.0, 0.0).astype(BF)
    spread_t = jnp.where(i_lo == j_hi, 1.0, 0.0).astype(BF)
    swap = jnp.where((i_hi == j_lo) & (i_lo == j_hi), 1.0, 0.0).astype(BF)

    for c in head:
        c.wait()

    def gather(b, carry):
        for q in range(block):
            part = pl.ds(pl.multiple_of((b * block + q) * GROUP, GROUP), GROUP)
            match_rows(slots[part, :], match, q * half, fetched.shape[0])
        picked = jnp.dot(match[...], fetched[...], preferred_element_type=F32).astype(BF)
        for q in range(block):
            dst = pl.multiple_of((b * block + q) * lane_group, lane_group)
            x[pl.ds(dst, half), :] = picked[q * half : (q + 1) * half]
        return carry

    lax.fori_loop(0, groups // block, gather, 0)
    for c in hot_copies:
        c.wait()

    def dots(i, carry):
        for u in range(UNROLL):
            g = i * UNROLL + u
            rows = pl.ds(pl.multiple_of(g * lane_group, lane_group), lane_group)
            part = pl.ds(pl.multiple_of(g * GROUP, GROUP), GROUP)
            xg = x[rows, :]
            for f in range(FEATS):
                a[part, f * width : (f + 1) * width] = xg[f * GROUP : (f + 1) * GROUP]
            gram = lax.dot_general(xg, xg, NT, preferred_element_type=F32) * scale
            own = jnp.where(i_lo == j_lo, gram, 0.0).astype(BF)
            wide = jnp.dot(own, spread, preferred_element_type=F32)
            wide = jnp.where(i_hi == j_hi, wide, 0.0)
            pairs[part, :] = jnp.sum(
                wide.reshape(FEATS, GROUP, lane_group), axis=0
            ).astype(BF)
        return carry

    lax.fori_loop(0, groups // UNROLL, dots, 0)
    for c in tail:
        c.wait()

    pre = jnp.dot(a[...], w_flat[...], preferred_element_type=F32)
    pre = pre + jnp.dot(pairs[...], w_inter[...], preferred_element_type=F32)
    pre = pre + bias[...]
    gated = jax.nn.sigmoid(pre)
    logits = jnp.sum(pre * gated * w_out[...], axis=-1, keepdims=True)
    eye = iota((samples, samples), 0) == iota((samples, samples), 1)
    target = jnp.sum(jnp.where(eye, targets[...], 0.0), axis=1, keepdims=True)
    residual = jax.nn.sigmoid(logits) - target
    slopes[...] = (residual * w_out[...] * gated * (1.0 + pre * (1.0 - gated))).astype(BF)

    inter_t = jnp.dot(swap, w_inter[...], preferred_element_type=F32).astype(BF)
    both = lax.dot_general(slopes[...], w_inter[...], NT, preferred_element_type=F32)
    both = both + lax.dot_general(slopes[...], inter_t, NT, preferred_element_type=F32)
    mirror[...] = (both * scale).astype(BF)

    def flat_back(f, carry):
        rows = pl.ds(pl.multiple_of(f * width, width), width)
        back[f] = lax.dot_general(
            slopes[...], w_flat[rows, :], NT, preferred_element_type=F32
        )
        return carry

    lax.fori_loop(0, FEATS, flat_back, 0)

    def grads(i, carry):
        for u in range(UNROLL):
            g = i * UNROLL + u
            rows = pl.ds(pl.multiple_of(g * lane_group, lane_group), lane_group)
            part = pl.ds(pl.multiple_of(g * GROUP, GROUP), GROUP)
            mine = mirror[part, :].astype(F32)
            tall = jnp.broadcast_to(mine[None], (FEATS, GROUP, lane_group)).reshape(sq)
            tall = jnp.where(i_hi == j_hi, tall, 0.0).astype(BF)
            wide = jnp.dot(tall, spread_t, preferred_element_type=F32)
            wide = jnp.where(i_lo == j_lo, wide, 0.0).astype(BF)
            total = jnp.dot(wide, x[rows, :], preferred_element_type=F32)
            total = total + back[:, part, :].reshape(lane_group, width)
            hi = total.astype(BF)
            lo = (total - hi.astype(F32)).astype(BF)
            for f in range(F_COLD):
                dst = pl.ds(pl.multiple_of(f * samples + g * GROUP, GROUP), GROUP)
                at = f * GROUP
                g_hi[dst, :] = hi[at : at + GROUP]
                g_lo[dst, :] = lo[at : at + GROUP]
                h_hi[dst, :] = hi[half + at : half + at + GROUP]
                h_lo[dst, :] = lo[half + at : half + at + GROUP]
        return carry

    lax.fori_loop(0, groups // UNROLL, grads, 0)
    outs = load_all([(h_hi, hot_hi), (h_lo, hot_lo)], sems.at[pl.ds(0, 2)])

    rows_blk = 512

    def scatter(b, carry):
        at = pl.multiple_of(b * rows_blk, rows_blk)
        subs = iota((rows_blk, samples), 0).astype(jnp.int16)
        for f in range(F_COLD):
            mine = jnp.broadcast_to(slots_t[f : f + 1, :] - at, (16, samples)).astype(jnp.int16)
            same = subs == jnp.concatenate([mine] * (rows_blk // 16), axis=0)
            match[:, f * samples : (f + 1) * samples] = as_one(same)
        total = jnp.dot(match[...], g_hi[...], preferred_element_type=F32)
        total = total + jnp.dot(match[...], g_lo[...], preferred_element_type=F32)
        fetched[pl.ds(at, rows_blk), :] = total.astype(BF)
        pltpu.make_async_copy(
            fetched.at[pl.ds(at, rows_blk), :], slot_grad.at[pl.ds(at, rows_blk), :], sems.at[3 + b]
        ).start()
        return carry

    n_out = slot_grad.shape[0] // rows_blk
    lax.fori_loop(0, n_out, scatter, 0)
    for b in range(n_out):
        pltpu.make_async_copy(
            fetched.at[pl.ds(b * rows_blk, rows_blk), :],
            slot_grad.at[pl.ds(b * rows_blk, rows_blk), :],
            sems.at[3 + b],
        ).wait()
    for c in outs:
        c.wait()


def backprop(m, fetched, xh, slots, slots_t, targets, w_flat, w_inter, bias, w_out):
    count, width = fetched.shape
    samples = slots.shape[0] // MB
    hidden = w_flat.shape[1]
    lookups = samples * F_COLD
    wide = FEATS * width
    rows = jax.ShapeDtypeStruct((lookups, width), BF)
    return pl.pallas_call(
        lambda *refs: step_kernel(m, *refs),
        in_specs=[HBM] * 9,
        out_specs=(HBM,) * 3,
        out_shape=(jax.ShapeDtypeStruct((count, width), BF), rows, rows),
        scratch_shapes=[
            pltpu.VMEM((count, width), BF),
            pltpu.VMEM((samples * FEATS, width), BF),
            pltpu.VMEM((samples, F_COLD), jnp.int32),
            pltpu.VMEM((F_COLD, samples), jnp.int32),
            pltpu.VMEM((1, samples), F32),
            pltpu.VMEM(w_flat.shape, BF),
            pltpu.VMEM(w_inter.shape, BF),
            pltpu.VMEM((1, hidden), F32),
            pltpu.VMEM((1, hidden), F32),
            pltpu.VMEM((samples, wide), BF),
            pltpu.VMEM((samples, FEATS * FEATS), BF),
            pltpu.VMEM((FEATS, samples, width), F32),
            pltpu.VMEM((samples, FEATS * FEATS), BF),
            pltpu.VMEM((lookups, width), BF),
            pltpu.VMEM((lookups, width), BF),
            pltpu.VMEM((lookups, width), BF),
            pltpu.VMEM((lookups, width), BF),
            pltpu.VMEM((512, 2048), BF),
            pltpu.VMEM((samples, hidden), BF),
            pltpu.SemaphoreType.DMA((9,)),
        ],
        compiler_params=params(),
        name="train_step",
    )(fetched, xh, slots, slots_t, targets, w_flat, w_inter, bias, w_out)


def hot_scatter_kernel(at_ref, ids_h, hi0, lo0, hi1, lo1, *refs):
    outs = refs[:N_DP]
    ids, h0, l0, h1, l1, match, res, sems = refs[N_DP:]
    copies = load_all([(ids_h, ids), (hi0, h0), (lo0, l0), (hi1, h1), (lo1, l1)], sems)
    samples = ids.shape[1] // MB
    block = 256
    subs = iota((block, samples), 0).astype(jnp.int16)
    for c in copies:
        c.wait()

    def body(b, carry):
        at = pl.multiple_of(b * block, block)
        total = None
        for m, parts in enumerate(((h0, l0), (h1, l1))):
            for f in range(F_COLD):
                row = ids[f : f + 1, m * samples : (m + 1) * samples] - at
                mine = jnp.broadcast_to(row, (16, samples)).astype(jnp.int16)
                same = subs == jnp.concatenate([mine] * (block // 16), axis=0)
                match[m, :, f * samples : (f + 1) * samples] = as_one(same)
            for part in parts:
                term = jnp.dot(match[m], part[...], preferred_element_type=F32)
                total = term if total is None else total + term
        res[pl.ds(at, block), :] = total
        return carry

    lax.fori_loop(0, res.shape[0] // block, body, 0)
    size = res.shape[0] // N_DP
    done = []
    for k in range(N_DP):
        chunk = (at_ref[0] + k) & (N_DP - 1)
        src = res.at[pl.ds(pl.multiple_of(chunk * size, size), size), :]
        done.append(pltpu.make_async_copy(src, outs[k], sems.at[k]))
        done[-1].start()
    for c in done:
        c.wait()


def hot_scatter(dp_at, ids, hi0, lo0, hi1, lo1, count):
    rows, width = hi0.shape
    return pl.pallas_call(
        hot_scatter_kernel,
        in_specs=[SMEM] + [HBM] * 5,
        out_specs=(HBM,) * N_DP,
        out_shape=(jax.ShapeDtypeStruct((count // N_DP, width), F32),) * N_DP,
        scratch_shapes=[pltpu.VMEM(ids.shape, jnp.int32)]
        + [pltpu.VMEM((rows, width), BF)] * 4
        + [
            pltpu.VMEM((MB, 256, rows), BF),
            pltpu.VMEM((count, width), F32),
            pltpu.SemaphoreType.DMA((N_DP,)),
        ],
        compiler_params=params(),
        name="hot_scatter",
    )(dp_at, ids, hi0, lo0, hi1, lo1)


def serve_kernel(m, with_hits, wanted, table, rows, *refs):
    if with_hits:
        hits, match, res, count_acc, sems = refs
    else:
        match, res, sems = refs
    shards, lanes = wanted.shape
    capacity = lanes // MB
    count = table.shape[0]
    per = 8
    block = per * capacity
    ids = jnp.concatenate([wanted[...], jnp.zeros((lanes - shards, lanes), jnp.int32)], axis=0)
    turned = ids.T
    names = iota((capacity, count), 1).astype(jnp.int16)
    if with_hits:
        count_acc[...] = jnp.zeros_like(count_acc)

    def ones_of(part, mb, j):
        col = part[mb * capacity : (mb + 1) * capacity, j : j + 1]
        mine = jnp.broadcast_to(col, (capacity, 128)).astype(jnp.int16)
        return as_one(names == jnp.concatenate([mine] * (count // 128), axis=1))

    def add_hits(one):
        tall = one[0:16] + one[16:32] + one[32:48] + one[48:64]
        count_acc[...] += tall

    def body(b, carry):
        part = pltpu.roll(turned, lanes - b * per, 1)
        for j in range(per):
            one = ones_of(part, m, j)
            match[j * capacity : (j + 1) * capacity, :] = one
            if with_hits:
                add_hits(one)
                for other in range(MB):
                    if other != m:
                        add_hits(ones_of(part, other, j))
        at = pl.ds(pl.multiple_of(b * block, block), block)
        res[at, :] = jnp.dot(match[...], table[...], preferred_element_type=F32).astype(BF)
        pltpu.make_async_copy(res.at[at, :], rows.at[at, :], sems.at[b]).start()
        return carry

    steps = shards // per
    lax.fori_loop(0, steps, body, 0)
    if with_hits:
        hits[...] = jnp.sum(count_acc[...].astype(F32), axis=0, keepdims=True)
    for b in range(steps):
        at = pl.ds(b * block, block)
        pltpu.make_async_copy(res.at[at, :], rows.at[at, :], sems.at[b]).wait()


def serve(m, with_hits, wanted, table):
    shards, lanes = wanted.shape
    capacity = lanes // MB
    slots = shards * capacity
    count, width = table.shape
    rows = jax.ShapeDtypeStruct((slots, width), BF)
    extra = [pltpu.VMEM((16, count), BF)] if with_hits else []
    return pl.pallas_call(
        lambda *refs: serve_kernel(m, with_hits, *refs),
        in_specs=[VMEM, VMEM],
        out_specs=(HBM, VMEM) if with_hits else HBM,
        out_shape=(rows, jax.ShapeDtypeStruct((1, count), F32)) if with_hits else rows,
        scratch_shapes=[pltpu.VMEM((512, count), BF), pltpu.VMEM((slots, width), BF)]
        + extra
        + [pltpu.SemaphoreType.DMA((shards // 8,))],
        compiler_params=params(),
        name="serve_rows",
    )(wanted, table)


def id_tiles(wanted, m):
    ids = wanted[...]
    other = pltpu.roll(ids, 64, 1)
    left, right = (ids, other) if m == 0 else (other, ids)
    low = iota((1, 128), 1) < 64
    return [
        jnp.where(low, left[2 * i : 2 * i + 1], right[2 * i + 1 : 2 * i + 2])
        for i in range(ids.shape[0] // 2)
    ]


def owner_match(tiles, base, match, subs):
    size = match.shape[0]
    for i, tile in enumerate(tiles):
        mine = jnp.broadcast_to(tile - base, (16, 128)).astype(jnp.int16)
        same = subs == jnp.concatenate([mine] * (size // 16), axis=0)
        match[:, i * 128 : (i + 1) * 128] = as_one(same)


def owner_first_kernel(wanted, grads_h, out, grads, match, res, sems):
    load = pltpu.make_async_copy(grads_h, grads, sems.at[0])
    load.start()
    block = match.shape[0]
    tiles = id_tiles(wanted, 0)
    subs = iota((block, 128), 0).astype(jnp.int16)
    load.wait()

    def body(b, carry):
        at = pl.multiple_of(b * block, block)
        owner_match(tiles, at, match, subs)
        res[pl.ds(at, block), :] = jnp.dot(match[...], grads[...], preferred_element_type=F32)
        return carry

    lax.fori_loop(0, res.shape[0] // block, body, 0)
    done = pltpu.make_async_copy(res, out, sems.at[1])
    done.start()
    done.wait()


def owner_first(wanted, grads, count):
    slots, width = grads.shape
    return pl.pallas_call(
        owner_first_kernel,
        in_specs=[VMEM, HBM],
        out_specs=HBM,
        out_shape=jax.ShapeDtypeStruct((count, width), F32),
        scratch_shapes=[
            pltpu.VMEM((slots, width), BF),
            pltpu.VMEM((512, slots), BF),
            pltpu.VMEM((count, width), F32),
            pltpu.SemaphoreType.DMA((2,)),
        ],
        compiler_params=params(),
        name="owner_first",
    )(wanted, grads)


def owner_second_kernel(at_ref, wanted, hits, grads_h, prev_h, *refs):
    outs = refs[:N_DP]
    grads, prev, match, res, sems = refs[N_DP:]
    size = match.shape[0]
    load = pltpu.make_async_copy(grads_h, grads, sems.at[0])
    load.start()
    load_prev = pltpu.make_async_copy(prev_h, prev, sems.at[1])
    load_prev.start()
    tiles = id_tiles(wanted, 1)
    subs = iota((size, 128), 0).astype(jnp.int16)
    load.wait()
    load_prev.wait()

    def body(k, carry):
        chunk = (at_ref[0] + k) & (N_DP - 1)
        at = pl.multiple_of(chunk * size, size)
        owner_match(tiles, at, match, subs)
        total = jnp.dot(match[...], grads[...], preferred_element_type=F32)
        total = total + prev[pl.ds(at, size), :]
        res[k, :size, :] = total.astype(BF)
        mine = hits[pl.ds(chunk, 1), :]
        res[k, size:, :] = jnp.broadcast_to(mine, (16, size)).astype(BF)
        return carry

    lax.fori_loop(0, N_DP, body, 0)
    done = load_all([(res.at[k], outs[k]) for k in range(N_DP)], sems)
    for c in done:
        c.wait()


def owner_second(dp_at, wanted, hits, grads, prev):
    slots, width = grads.shape
    count = prev.shape[0]
    size = count // N_DP
    return pl.pallas_call(
        owner_second_kernel,
        in_specs=[SMEM, VMEM, VMEM, HBM, HBM],
        out_specs=(HBM,) * N_DP,
        out_shape=(jax.ShapeDtypeStruct((size + 16, width), BF),) * N_DP,
        scratch_shapes=[
            pltpu.VMEM((slots, width), BF),
            pltpu.VMEM((count, width), F32),
            pltpu.VMEM((size, slots), BF),
            pltpu.VMEM((N_DP, size + 16, width), BF),
            pltpu.SemaphoreType.DMA((2 + N_DP,)),
        ],
        compiler_params=params(),
        name="owner_second",
    )(dp_at, wanted, hits, grads, prev)


def to_col(row, eye):
    return jnp.sum(jnp.where(eye, row, 0.0), axis=1, keepdims=True)


def to_row(col, eye):
    return jnp.sum(jnp.where(eye, col, 0.0), axis=0, keepdims=True)


def adagrad(table, accum, grad):
    accum_new = accum + jnp.mean(grad * grad, axis=-1, keepdims=True)
    return table - learn_rate * grad / jnp.sqrt(accum_new), accum_new


def cold_update_kernel(at_ref, table_h, accum_h, bits_h, *refs):
    parts_h = refs[:N_DP]
    out = refs[N_DP]
    parts, table, accum, bits, res, sems = refs[N_DP + 1 :]
    size = table.shape[0]
    at = pl.multiple_of(at_ref[0] * size, size)
    copies = load_all(
        [(parts_h[k], parts.at[k]) for k in range(N_DP)]
        + [
            (table_h.at[pl.ds(at, size), :], table),
            (accum_h, accum),
            (bits_h.at[pl.ds(at, size), :], bits),
        ],
        sems,
    )
    eye = iota((size, size), 0) == iota((size, size), 1)
    for c in copies:
        c.wait()
    total = parts[0].astype(F32)
    for k in range(1, N_DP):
        total = total + parts[k].astype(F32)
    touched = to_col(total[size : size + 1], eye)
    averaged = total[:size] / jnp.maximum(touched, 1.0)
    old = to_col(accum[pl.ds(at_ref[0], 1), :], eye)
    updated, accum_new = adagrad(table[...].astype(F32), old, averaged)
    grid_step = jnp.max(jnp.abs(updated), axis=-1, keepdims=True) / 8.0
    dither = bits[...].astype(F32) * (1.0 / 65280.0) - 0.5
    res[:size, :] = jnp.where(touched > 0.5, updated + grid_step * dither, updated).astype(BF)
    row = to_row(accum_new, eye)
    high = row.astype(BF).astype(F32)
    middle = (row - high).astype(BF).astype(F32)
    low = (row - high) - middle
    which = iota((16, size), 0)
    packed = jnp.where(which == 0, high, jnp.where(which == 1, middle, low))
    res[size:, :] = packed.astype(BF)
    done = pltpu.make_async_copy(res, out, sems.at[0])
    done.start()
    done.wait()


def cold_update(dp_at, table, accum, bits, parts):
    width = table.shape[1]
    size = table.shape[0] // N_DP
    packed = parts[0].shape
    return pl.pallas_call(
        cold_update_kernel,
        in_specs=[SMEM] + [HBM] * (3 + N_DP),
        out_specs=HBM,
        out_shape=jax.ShapeDtypeStruct(packed, BF),
        scratch_shapes=[
            pltpu.VMEM((N_DP,) + packed, BF),
            pltpu.VMEM((size, width), BF),
            pltpu.VMEM(accum.shape, F32),
            pltpu.VMEM((size, width), jnp.int32),
            pltpu.VMEM(packed, BF),
            pltpu.SemaphoreType.DMA((N_DP + 3,)),
        ],
        compiler_params=params(),
        name="cold_update",
    )(dp_at, table, accum, bits, *parts)


def cold_join_kernel(at_ref, *refs):
    parts = refs[:N_DP]
    out, accum_out, pieces, sems = refs[N_DP:]
    size = out.shape[0] // N_DP
    copies = []
    for k in range(N_DP):
        chunk = (at_ref[0] - k) & (N_DP - 1)
        dst = out.at[pl.ds(pl.multiple_of(chunk * size, size), size), :]
        copies.append(pltpu.make_async_copy(parts[k].at[pl.ds(0, size), :], dst, sems.at[k]))
        copies.append(
            pltpu.make_async_copy(
                parts[k].at[pl.ds(size, 16), :], pieces.at[chunk], sems.at[N_DP + k]
            )
        )
    for c in copies:
        c.start()
    for c in copies:
        c.wait()
    for p in range(N_DP):
        rows = pieces[p].astype(F32)
        accum_out[p : p + 1, :] = (rows[2:3] + rows[1:2]) + rows[0:1]


def cold_join(dp_at, parts):
    width = parts[0].shape[1]
    size = parts[0].shape[0] - 16
    return pl.pallas_call(
        cold_join_kernel,
        in_specs=[SMEM] + [HBM] * N_DP,
        out_specs=(HBM, VMEM),
        out_shape=(
            jax.ShapeDtypeStruct((N_DP * size, width), BF),
            jax.ShapeDtypeStruct((N_DP, size), F32),
        ),
        scratch_shapes=[
            pltpu.VMEM((N_DP, 16, width), BF),
            pltpu.SemaphoreType.DMA((2 * N_DP,)),
        ],
        compiler_params=params(),
        name="cold_join",
    )(dp_at, *parts)


def sum_parts_kernel(*refs):
    parts_h = refs[:N_DP]
    out, parts, sems = refs[N_DP:]
    copies = load_all([(parts_h[k], parts.at[k]) for k in range(N_DP)], sems)
    for c in copies:
        c.wait()
    out[...] = jnp.sum(parts[...], axis=0)


def sum_parts(parts):
    shape = parts[0].shape
    return pl.pallas_call(
        sum_parts_kernel,
        in_specs=[HBM] * N_DP,
        out_specs=VMEM,
        out_shape=jax.ShapeDtypeStruct(shape, F32),
        scratch_shapes=[
            pltpu.VMEM((N_DP,) + shape, F32),
            pltpu.SemaphoreType.DMA((N_DP,)),
        ],
        compiler_params=params(),
        name="sum_parts",
    )(*parts)


def hot_update_kernel(at_ref, table_h, accum_h, *refs):
    grads_h = refs[:N_DP]
    out, accum_out, table, accum, grads, res, sems = refs[N_DP:]
    size = grads.shape[1]
    copies = load_all(
        [(table_h, table), (accum_h, accum)]
        + [(grads_h[k], grads.at[k]) for k in range(N_DP)],
        sems,
    )
    eye = iota((size, size), 0) == iota((size, size), 1)
    for c in copies:
        c.wait()
    for k in range(N_DP):
        chunk = (at_ref[0] - k) & (N_DP - 1)
        rows = pl.ds(pl.multiple_of(chunk * size, size), size)
        old = to_col(accum[pl.ds(chunk, 1), :], eye)
        updated, accum_new = adagrad(table[rows, :], old, grads[k])
        res[rows, :] = updated
        accum_out[pl.ds(chunk, 1), :] = to_row(accum_new, eye)
    done = pltpu.make_async_copy(res, out, sems.at[0])
    done.start()
    done.wait()


def hot_update(dp_at, table, accum, grads):
    count, width = table.shape
    size = count // N_DP
    return pl.pallas_call(
        hot_update_kernel,
        in_specs=[SMEM] + [HBM] * (2 + N_DP),
        out_specs=(HBM, VMEM),
        out_shape=(
            jax.ShapeDtypeStruct((count, width), F32),
            jax.ShapeDtypeStruct((N_DP, size), F32),
        ),
        scratch_shapes=[
            pltpu.VMEM((count, width), F32),
            pltpu.VMEM((N_DP, size), F32),
            pltpu.VMEM((N_DP, size, width), F32),
            pltpu.VMEM((count, width), F32),
            pltpu.SemaphoreType.DMA((2 + N_DP,)),
        ],
        compiler_params=params(),
        name="hot_update",
    )(dp_at, table, accum, *grads)


def exchange(value, axis):
    return lax.all_to_all(value, axis, split_axis=0, concat_axis=0, tiled=True)


def shift(value, k):
    return lax.ppermute(value, "dp", [(i, (i + k) % N_DP) for i in range(N_DP)])


def to_owners(parts):
    return [parts[0]] + [shift(parts[k], k) for k in range(1, N_DP)]


def to_all(part):
    return [part] + [shift(part, k) for k in range(1, N_DP)]


def step(
    cold_table,
    cold_accum,
    dither_bits,
    hot_table,
    hot_accum,
    w_flat,
    w_inter,
    hidden_bias,
    w_out,
    targets,
    hot_ids,
    cold_slots,
    requests,
    counts,
):
    shards = lax.axis_size("shard")
    capacity = requests.shape[1]
    row_count, row_width = cold_table.shape
    hot_count = hot_table.shape[0]
    slots = shards * capacity
    dp_at = lax.axis_index("dp").astype(jnp.int32).reshape(1)

    live = jnp.arange(capacity, dtype=jnp.int32) < counts[:, :, None]
    asked = jnp.where(live, requests.reshape(MB, shards, capacity), -1)
    asked = asked.transpose(1, 0, 2).reshape(shards, MB * capacity)
    wanted = exchange(asked, "shard")

    fetched = []
    for m in range(MB):
        rows = serve(m, m == 1, wanted, cold_table)
        if m == 1:
            rows, hits = rows
        rows = exchange(rows.reshape(shards, capacity, row_width), "shard")
        fetched.append(rows.reshape(slots, row_width))
    xh = hot_rows(hot_ids, hot_table)

    owned = []
    hot_parts = []
    for m in range(MB):
        slot_grad, *hot_part = backprop(
            m,
            fetched[m],
            xh,
            cold_slots,
            cold_slots.T,
            targets.reshape(1, -1),
            w_flat,
            w_inter,
            hidden_bias.reshape(1, -1),
            w_out.reshape(1, -1),
        )
        hot_parts += hot_part
        rows = exchange(slot_grad.reshape(shards, capacity, row_width), "shard")
        owned.append(rows.reshape(slots, row_width))

    hot_grads = hot_scatter(dp_at, hot_ids.T, *hot_parts, hot_count)
    hot_grads = to_owners(hot_grads)
    hot_sum = sum_parts(hot_grads)
    hot_size = hot_sum.shape[0]
    hot_sum = exchange(hot_sum.reshape(shards, hot_size // shards, row_width), "shard")
    hot_sum = jnp.sum(hot_sum, axis=0)
    hot_all = exchange(jnp.broadcast_to(hot_sum[None], (shards,) + hot_sum.shape), "shard")
    hot_all = to_all(hot_all.reshape(hot_size, row_width))
    hot_out, hot_accum_out = hot_update(
        dp_at, hot_table, hot_accum.reshape(N_DP, -1), hot_all
    )

    first = owner_first(wanted, owned[0], row_count)
    parts = owner_second(dp_at, wanted, hits.reshape(N_DP, -1), owned[1], first)
    parts = to_owners(parts)
    packed = cold_update(
        dp_at, cold_table, cold_accum.reshape(N_DP, -1), dither_bits, parts
    )
    parts = to_all(packed)
    cold_out, cold_accum_out = cold_join(dp_at, parts)
    return (cold_out, cold_accum_out.reshape(-1), hot_out, hot_accum_out.reshape(-1))


def solution(mesh):
    return jax.shard_map(
        step,
        mesh=mesh,
        in_specs=(
            P("shard", None),
            P("shard"),
            P("shard", None),
            P(),
            P(),
            P(),
            P(),
            P(),
            P(),
            P(("shard", "dp")),
            P(("shard", "dp"), None),
            P(("shard", "dp"), None),
            P(("shard", "dp"), None),
            P(("shard", "dp"), None),
        ),
        out_specs=(P("shard", None), P("shard"), P(), P()),
        check_vma=False,
    )
```

```python
import jax
import jax.numpy as jnp
from jax import lax
from jax.experimental import pallas as pl
from jax.experimental.pallas import tpu as pltpu
from jax.sharding import PartitionSpec as P


MB = 2
GROUP = 16
FEATS = 16
F_COLD = 8
BF = jnp.bfloat16
F32 = jnp.float32
NT = (((1,), (1,)), ((), ()))
HBM = pl.BlockSpec(memory_space=pltpu.HBM)
VMEM = pl.BlockSpec(memory_space=pltpu.VMEM)
SMEM = pl.BlockSpec(memory_space=pltpu.SMEM)
N_DP = 8
VMEM_LIMIT = (64 << 20) - (64 << 10)
learn_rate = 0.3
UNROLL = 4


def iota(shape, axis):
    return lax.broadcasted_iota(jnp.int32, shape, axis)


def as_one(same):
    return jnp.where(same, jnp.ones(same.shape, BF), jnp.zeros(same.shape, BF))


def chunk_of(at, i):
    x = ((at >> 1) - (i & 3)) & 3
    return x * 2 + ((at & 1) ^ (i >> 2))


def params():
    return pltpu.CompilerParams(vmem_limit_bytes=VMEM_LIMIT)


def load_all(pairs, sems):
    copies = [pltpu.make_async_copy(s, d, sems.at[i]) for i, (s, d) in enumerate(pairs)]
    for c in copies:
        c.start()
    return copies


def match_rows(ids, match, at, count):
    lanes = iota((GROUP, count), 1).astype(jnp.int16)
    for f in range(F_COLD):
        mine = jnp.broadcast_to(ids[:, f : f + 1], (GROUP, 128)).astype(jnp.int16)
        same = lanes == jnp.concatenate([mine] * (count // 128), axis=1)
        match[pl.ds(at + f * GROUP, GROUP), :count] = as_one(same)


def hot_rows_kernel(hot_ids, table, out, ids, src, match, res, sems):
    copies = load_all([(hot_ids, ids), (table, src)], sems)
    for c in copies:
        c.wait()
    source = src[...].astype(BF)
    half = F_COLD * GROUP
    block = 4
    steps = ids.shape[0] // GROUP // block

    def body(b, carry):
        for q in range(block):
            part = pl.ds(pl.multiple_of((b * block + q) * GROUP, GROUP), GROUP)
            match_rows(ids[part, :], match, q * half, source.shape[0])
        rows = pl.ds(pl.multiple_of(b * block * half, block * half), block * half)
        res[rows, :] = jnp.dot(match[...], source, preferred_element_type=F32).astype(BF)
        return carry

    lax.fori_loop(0, steps, body, 0)
    done = pltpu.make_async_copy(res, out, sems.at[2])
    done.start()
    done.wait()


def hot_rows(hot_ids, table):
    count, width = table.shape
    rows = hot_ids.shape[0] * F_COLD
    return pl.pallas_call(
        hot_rows_kernel,
        in_specs=[HBM, HBM],
        out_specs=HBM,
        out_shape=jax.ShapeDtypeStruct((rows, width), BF),
        scratch_shapes=[
            pltpu.VMEM(hot_ids.shape, jnp.int32),
            pltpu.VMEM(table.shape, F32),
            pltpu.VMEM((512, count), BF),
            pltpu.VMEM((rows, width), BF),
            pltpu.SemaphoreType.DMA((3,)),
        ],
        compiler_params=params(),
        name="hot_rows",
    )(hot_ids, table)


def step_kernel(m, *refs):
    (
        fetched_h, xh_h, slots_h, slots_t_h, targets_h, flat_h, inter_h, bias_h, w_out_h,
        slot_grad, hot_hi, hot_lo,
        fetched, x, slots, slots_t, targets, w_flat, w_inter, bias, w_out,
        a, pairs, back, mirror, g_hi, g_lo, h_hi, h_lo, match, slopes, sems,
    ) = refs
    width = fetched.shape[1]
    samples = targets.shape[1]
    groups = samples // GROUP
    lane_group = FEATS * GROUP
    half = F_COLD * GROUP
    scale = width ** (-0.5)
    block = 4
    first = m * samples

    head = load_all(
        [
            (slots_h.at[pl.ds(first, samples), :], slots),
            (fetched_h, fetched),
        ],
        sems,
    )
    hot_copies = [
        pltpu.make_async_copy(
            xh_h.at[pl.ds((m * groups + g) * half, half), :],
            x.at[pl.ds(g * lane_group + half, half), :],
            sems.at[2],
        )
        for g in range(groups)
    ]
    for c in hot_copies:
        c.start()
    tail = load_all(
        [
            (flat_h, w_flat),
            (inter_h, w_inter),
            (bias_h, bias),
            (w_out_h, w_out),
            (targets_h.at[:, pl.ds(first, samples)], targets),
            (slots_t_h.at[:, pl.ds(first, samples)], slots_t),
        ],
        sems.at[pl.ds(3, 6)],
    )

    sq = (lane_group, lane_group)
    i_hi = iota(sq, 0) >> 4
    i_lo = iota(sq, 0) & 15
    j_hi = iota(sq, 1) >> 4
    j_lo = iota(sq, 1) & 15
    spread = jnp.where(i_hi == j_lo, 1.0, 0.0).astype(BF)
    spread_t = jnp.where(i_lo == j_hi, 1.0, 0.0).astype(BF)
    swap = jnp.where((i_hi == j_lo) & (i_lo == j_hi), 1.0, 0.0).astype(BF)

    for c in head:
        c.wait()

    def gather(b, carry):
        for q in range(block):
            part = pl.ds(pl.multiple_of((b * block + q) * GROUP, GROUP), GROUP)
            match_rows(slots[part, :], match, q * half, fetched.shape[0])
        picked = jnp.dot(match[...], fetched[...], preferred_element_type=F32).astype(BF)
        for q in range(block):
            dst = pl.multiple_of((b * block + q) * lane_group, lane_group)
            x[pl.ds(dst, half), :] = picked[q * half : (q + 1) * half]
        return carry

    lax.fori_loop(0, groups // block, gather, 0)
    for c in hot_copies:
        c.wait()

    def dots(i, carry):
        for u in range(UNROLL):
            g = i * UNROLL + u
            rows = pl.ds(pl.multiple_of(g * lane_group, lane_group), lane_group)
            part = pl.ds(pl.multiple_of(g * GROUP, GROUP), GROUP)
            xg = x[rows, :]
            for f in range(FEATS):
                a[part, f * width : (f + 1) * width] = xg[f * GROUP : (f + 1) * GROUP]
            gram = lax.dot_general(xg, xg, NT, preferred_element_type=F32) * scale
            own = jnp.where(i_lo == j_lo, gram, 0.0).astype(BF)
            wide = jnp.dot(own, spread, preferred_element_type=F32)
            wide = jnp.where(i_hi == j_hi, wide, 0.0)
            pairs[part, :] = jnp.sum(
                wide.reshape(FEATS, GROUP, lane_group), axis=0
            ).astype(BF)
        return carry

    lax.fori_loop(0, groups // UNROLL, dots, 0)
    for c in tail:
        c.wait()

    pre = jnp.dot(a[...], w_flat[...], preferred_element_type=F32)
    pre = pre + jnp.dot(pairs[...], w_inter[...], preferred_element_type=F32)
    pre = pre + bias[...]
    gated = jax.nn.sigmoid(pre)
    logits = jnp.sum(pre * gated * w_out[...], axis=-1, keepdims=True)
    eye = iota((samples, samples), 0) == iota((samples, samples), 1)
    target = jnp.sum(jnp.where(eye, targets[...], 0.0), axis=1, keepdims=True)
    residual = jax.nn.sigmoid(logits) - target
    slopes[...] = (residual * w_out[...] * gated * (1.0 + pre * (1.0 - gated))).astype(BF)

    inter_t = jnp.dot(swap, w_inter[...], preferred_element_type=F32).astype(BF)
    both = lax.dot_general(slopes[...], w_inter[...], NT, preferred_element_type=F32)
    both = both + lax.dot_general(slopes[...], inter_t, NT, preferred_element_type=F32)
    mirror[...] = (both * scale).astype(BF)

    def flat_back(f, carry):
        rows = pl.ds(pl.multiple_of(f * width, width), width)
        back[f] = lax.dot_general(
            slopes[...], w_flat[rows, :], NT, preferred_element_type=F32
        )
        return carry

    lax.fori_loop(0, FEATS, flat_back, 0)

    def grads(i, carry):
        for u in range(UNROLL):
            g = i * UNROLL + u
            rows = pl.ds(pl.multiple_of(g * lane_group, lane_group), lane_group)
            part = pl.ds(pl.multiple_of(g * GROUP, GROUP), GROUP)
            mine = mirror[part, :].astype(F32)
            tall = jnp.broadcast_to(mine[None], (FEATS, GROUP, lane_group)).reshape(sq)
            tall = jnp.where(i_hi == j_hi, tall, 0.0).astype(BF)
            wide = jnp.dot(tall, spread_t, preferred_element_type=F32)
            wide = jnp.where(i_lo == j_lo, wide, 0.0).astype(BF)
            total = jnp.dot(wide, x[rows, :], preferred_element_type=F32)
            total = total + back[:, part, :].reshape(lane_group, width)
            hi = total.astype(BF)
            lo = (total - hi.astype(F32)).astype(BF)
            for f in range(F_COLD):
                dst = pl.ds(pl.multiple_of(f * samples + g * GROUP, GROUP), GROUP)
                at = f * GROUP
                g_hi[dst, :] = hi[at : at + GROUP]
                g_lo[dst, :] = lo[at : at + GROUP]
                h_hi[dst, :] = hi[half + at : half + at + GROUP]
                h_lo[dst, :] = lo[half + at : half + at + GROUP]
        return carry

    lax.fori_loop(0, groups // UNROLL, grads, 0)
    outs = load_all([(h_hi, hot_hi), (h_lo, hot_lo)], sems.at[pl.ds(0, 2)])

    rows_blk = 512

    def scatter(b, carry):
        at = pl.multiple_of(b * rows_blk, rows_blk)
        subs = iota((rows_blk, samples), 0).astype(jnp.int16)
        for f in range(F_COLD):
            mine = jnp.broadcast_to(slots_t[f : f + 1, :] - at, (16, samples)).astype(jnp.int16)
            same = subs == jnp.concatenate([mine] * (rows_blk // 16), axis=0)
            match[:, f * samples : (f + 1) * samples] = as_one(same)
        total = jnp.dot(match[...], g_hi[...], preferred_element_type=F32)
        total = total + jnp.dot(match[...], g_lo[...], preferred_element_type=F32)
        fetched[pl.ds(at, rows_blk), :] = total.astype(BF)
        pltpu.make_async_copy(
            fetched.at[pl.ds(at, rows_blk), :], slot_grad.at[pl.ds(at, rows_blk), :], sems.at[3 + b]
        ).start()
        return carry

    n_out = slot_grad.shape[0] // rows_blk
    lax.fori_loop(0, n_out, scatter, 0)
    for b in range(n_out):
        pltpu.make_async_copy(
            fetched.at[pl.ds(b * rows_blk, rows_blk), :],
            slot_grad.at[pl.ds(b * rows_blk, rows_blk), :],
            sems.at[3 + b],
        ).wait()
    for c in outs:
        c.wait()


def backprop(m, fetched, xh, slots, slots_t, targets, w_flat, w_inter, bias, w_out):
    count, width = fetched.shape
    samples = slots.shape[0] // MB
    hidden = w_flat.shape[1]
    lookups = samples * F_COLD
    wide = FEATS * width
    rows = jax.ShapeDtypeStruct((lookups, width), BF)
    return pl.pallas_call(
        lambda *refs: step_kernel(m, *refs),
        in_specs=[HBM] * 9,
        out_specs=(HBM,) * 3,
        out_shape=(jax.ShapeDtypeStruct((count, width), BF), rows, rows),
        scratch_shapes=[
            pltpu.VMEM((count, width), BF),
            pltpu.VMEM((samples * FEATS, width), BF),
            pltpu.VMEM((samples, F_COLD), jnp.int32),
            pltpu.VMEM((F_COLD, samples), jnp.int32),
            pltpu.VMEM((1, samples), F32),
            pltpu.VMEM(w_flat.shape, BF),
            pltpu.VMEM(w_inter.shape, BF),
            pltpu.VMEM((1, hidden), F32),
            pltpu.VMEM((1, hidden), F32),
            pltpu.VMEM((samples, wide), BF),
            pltpu.VMEM((samples, FEATS * FEATS), BF),
            pltpu.VMEM((FEATS, samples, width), F32),
            pltpu.VMEM((samples, FEATS * FEATS), BF),
            pltpu.VMEM((lookups, width), BF),
            pltpu.VMEM((lookups, width), BF),
            pltpu.VMEM((lookups, width), BF),
            pltpu.VMEM((lookups, width), BF),
            pltpu.VMEM((512, 2048), BF),
            pltpu.VMEM((samples, hidden), BF),
            pltpu.SemaphoreType.DMA((9,)),
        ],
        compiler_params=params(),
        name="train_step",
    )(fetched, xh, slots, slots_t, targets, w_flat, w_inter, bias, w_out)


def hot_sums(m, ids, hi, lo, prev, match, res):
    samples = ids.shape[1] // MB
    block = match.shape[0]
    subs = iota((block, samples), 0).astype(jnp.int16)

    def body(b, carry):
        at = pl.multiple_of(b * block, block)
        for f in range(F_COLD):
            row = ids[f : f + 1, m * samples : (m + 1) * samples] - at
            mine = jnp.broadcast_to(row, (16, samples)).astype(jnp.int16)
            same = subs == jnp.concatenate([mine] * (block // 16), axis=0)
            match[:, f * samples : (f + 1) * samples] = as_one(same)
        total = jnp.dot(match[...], hi[...], preferred_element_type=F32)
        total = total + jnp.dot(match[...], lo[...], preferred_element_type=F32)
        if prev is not None:
            total = total + prev[pl.ds(at, block), :]
        res[pl.ds(at, block), :] = total
        return carry

    lax.fori_loop(0, res.shape[0] // block, body, 0)


def hot_first_kernel(ids_h, hi_h, lo_h, out, ids, hi, lo, match, res, sems):
    copies = load_all([(ids_h, ids), (hi_h, hi), (lo_h, lo)], sems)
    for c in copies:
        c.wait()
    hot_sums(0, ids, hi, lo, None, match, res)
    done = pltpu.make_async_copy(res, out, sems.at[0])
    done.start()
    done.wait()


def hot_second_kernel(at_ref, ids_h, hi_h, lo_h, prev_h, *refs):
    outs = refs[:N_DP]
    ids, hi, lo, prev, match, res, sems = refs[N_DP:]
    copies = load_all([(ids_h, ids), (hi_h, hi), (lo_h, lo), (prev_h, prev)], sems)
    for c in copies:
        c.wait()
    hot_sums(1, ids, hi, lo, prev, match, res)
    size = res.shape[0] // N_DP
    done = []
    for k in range(N_DP):
        chunk = (at_ref[0] + k) & (N_DP - 1)
        src = res.at[pl.ds(pl.multiple_of(chunk * size, size), size), :]
        done.append(pltpu.make_async_copy(src, outs[k], sems.at[k]))
        done[-1].start()
    for c in done:
        c.wait()


def hot_scatter(m, dp_at, ids, hi, lo, prev, count):
    rows, width = hi.shape
    scratch = [
        pltpu.VMEM(ids.shape, jnp.int32),
        pltpu.VMEM((rows, width), BF),
        pltpu.VMEM((rows, width), BF),
    ]
    tail = [
        pltpu.VMEM((256, rows), BF),
        pltpu.VMEM((count, width), F32),
        pltpu.SemaphoreType.DMA((N_DP,)),
    ]
    whole = jax.ShapeDtypeStruct((count, width), F32)
    if m == 0:
        return pl.pallas_call(
            hot_first_kernel,
            in_specs=[HBM] * 3,
            out_specs=HBM,
            out_shape=whole,
            scratch_shapes=scratch + tail,
            compiler_params=params(),
            name="hot_first",
        )(ids, hi, lo)
    return pl.pallas_call(
        hot_second_kernel,
        in_specs=[SMEM] + [HBM] * 4,
        out_specs=(HBM,) * N_DP,
        out_shape=(jax.ShapeDtypeStruct((count // N_DP, width), F32),) * N_DP,
        scratch_shapes=scratch + [pltpu.VMEM((count, width), F32)] + tail,
        compiler_params=params(),
        name="hot_second",
    )(dp_at, ids, hi, lo, prev)


def serve_kernel(m, with_hits, wanted, table, rows, *refs):
    if with_hits:
        hits, match, res, count_acc, sems = refs
    else:
        match, res, sems = refs
    shards, lanes = wanted.shape
    capacity = lanes // MB
    count = table.shape[0]
    per = 8
    block = per * capacity
    ids = jnp.concatenate([wanted[...], jnp.zeros((lanes - shards, lanes), jnp.int32)], axis=0)
    turned = ids.T
    names = iota((capacity, count), 1).astype(jnp.int16)
    if with_hits:
        count_acc[...] = jnp.zeros_like(count_acc)

    def ones_of(part, mb, j):
        col = part[mb * capacity : (mb + 1) * capacity, j : j + 1]
        mine = jnp.broadcast_to(col, (capacity, 128)).astype(jnp.int16)
        return as_one(names == jnp.concatenate([mine] * (count // 128), axis=1))

    def add_hits(one):
        tall = one[0:16] + one[16:32] + one[32:48] + one[48:64]
        count_acc[...] += tall

    def body(b, carry):
        part = pltpu.roll(turned, lanes - b * per, 1)
        for j in range(per):
            one = ones_of(part, m, j)
            match[j * capacity : (j + 1) * capacity, :] = one
            if with_hits:
                add_hits(one)
                for other in range(MB):
                    if other != m:
                        add_hits(ones_of(part, other, j))
        at = pl.ds(pl.multiple_of(b * block, block), block)
        res[at, :] = jnp.dot(match[...], table[...], preferred_element_type=F32).astype(BF)
        pltpu.make_async_copy(res.at[at, :], rows.at[at, :], sems.at[b]).start()
        return carry

    steps = shards // per
    lax.fori_loop(0, steps, body, 0)
    if with_hits:
        hits[...] = jnp.sum(count_acc[...].astype(F32), axis=0, keepdims=True)
    for b in range(steps):
        at = pl.ds(b * block, block)
        pltpu.make_async_copy(res.at[at, :], rows.at[at, :], sems.at[b]).wait()


def serve(m, with_hits, wanted, table):
    shards, lanes = wanted.shape
    capacity = lanes // MB
    slots = shards * capacity
    count, width = table.shape
    rows = jax.ShapeDtypeStruct((slots, width), BF)
    extra = [pltpu.VMEM((16, count), BF)] if with_hits else []
    return pl.pallas_call(
        lambda *refs: serve_kernel(m, with_hits, *refs),
        in_specs=[VMEM, VMEM],
        out_specs=(HBM, VMEM) if with_hits else HBM,
        out_shape=(rows, jax.ShapeDtypeStruct((1, count), F32)) if with_hits else rows,
        scratch_shapes=[pltpu.VMEM((512, count), BF), pltpu.VMEM((slots, width), BF)]
        + extra
        + [pltpu.SemaphoreType.DMA((shards // 8,))],
        compiler_params=params(),
        name="serve_rows",
    )(wanted, table)


def id_tiles(wanted, m):
    ids = wanted[...]
    other = pltpu.roll(ids, 64, 1)
    left, right = (ids, other) if m == 0 else (other, ids)
    low = iota((1, 128), 1) < 64
    return [
        jnp.where(low, left[2 * i : 2 * i + 1], right[2 * i + 1 : 2 * i + 2])
        for i in range(ids.shape[0] // 2)
    ]


def owner_match(tiles, base, match, subs):
    size = match.shape[0]
    for i, tile in enumerate(tiles):
        mine = jnp.broadcast_to(tile - base, (16, 128)).astype(jnp.int16)
        same = subs == jnp.concatenate([mine] * (size // 16), axis=0)
        match[:, i * 128 : (i + 1) * 128] = as_one(same)


def owner_first_kernel(wanted, grads_h, out, grads, match, res, sems):
    load = pltpu.make_async_copy(grads_h, grads, sems.at[0])
    load.start()
    block = match.shape[0]
    tiles = id_tiles(wanted, 0)
    subs = iota((block, 128), 0).astype(jnp.int16)
    load.wait()

    def body(b, carry):
        at = pl.multiple_of(b * block, block)
        owner_match(tiles, at, match, subs)
        res[pl.ds(at, block), :] = jnp.dot(match[...], grads[...], preferred_element_type=F32)
        return carry

    lax.fori_loop(0, res.shape[0] // block, body, 0)
    done = pltpu.make_async_copy(res, out, sems.at[1])
    done.start()
    done.wait()


def owner_first(wanted, grads, count):
    slots, width = grads.shape
    return pl.pallas_call(
        owner_first_kernel,
        in_specs=[VMEM, HBM],
        out_specs=HBM,
        out_shape=jax.ShapeDtypeStruct((count, width), F32),
        scratch_shapes=[
            pltpu.VMEM((slots, width), BF),
            pltpu.VMEM((256, slots), BF),
            pltpu.VMEM((count, width), F32),
            pltpu.SemaphoreType.DMA((2,)),
        ],
        compiler_params=params(),
        name="owner_first",
    )(wanted, grads)


def owner_second_kernel(at_ref, wanted, hits, grads_h, prev_h, *refs):
    outs = refs[:N_DP]
    grads, prev, match, res, sems = refs[N_DP:]
    size = match.shape[0]
    load = pltpu.make_async_copy(grads_h, grads, sems.at[0])
    load.start()
    load_prev = pltpu.make_async_copy(prev_h, prev, sems.at[1])
    load_prev.start()
    tiles = id_tiles(wanted, 1)
    subs = iota((size, 128), 0).astype(jnp.int16)
    load.wait()
    load_prev.wait()

    def body(k, carry):
        chunk = (at_ref[0] + k) & (N_DP - 1)
        at = pl.multiple_of(chunk * size, size)
        owner_match(tiles, at, match, subs)
        total = jnp.dot(match[...], grads[...], preferred_element_type=F32)
        total = total + prev[pl.ds(at, size), :]
        res[k, :size, :] = total.astype(BF)
        mine = hits[pl.ds(chunk, 1), :]
        res[k, size:, :] = jnp.broadcast_to(mine, (16, size)).astype(BF)
        return carry

    lax.fori_loop(0, N_DP, body, 0)
    done = load_all([(res.at[k], outs[k]) for k in range(N_DP)], sems)
    for c in done:
        c.wait()


def owner_second(dp_at, wanted, hits, grads, prev):
    slots, width = grads.shape
    count = prev.shape[0]
    size = count // N_DP
    return pl.pallas_call(
        owner_second_kernel,
        in_specs=[SMEM, VMEM, VMEM, HBM, HBM],
        out_specs=(HBM,) * N_DP,
        out_shape=(jax.ShapeDtypeStruct((size + 16, width), BF),) * N_DP,
        scratch_shapes=[
            pltpu.VMEM((slots, width), BF),
            pltpu.VMEM((count, width), F32),
            pltpu.VMEM((size, slots), BF),
            pltpu.VMEM((N_DP, size + 16, width), BF),
            pltpu.SemaphoreType.DMA((2 + N_DP,)),
        ],
        compiler_params=params(),
        name="owner_second",
    )(dp_at, wanted, hits, grads, prev)


def to_col(row, eye):
    return jnp.sum(jnp.where(eye, row, 0.0), axis=1, keepdims=True)


def to_row(col, eye):
    return jnp.sum(jnp.where(eye, col, 0.0), axis=0, keepdims=True)


def adagrad(table, accum, grad):
    accum_new = accum + jnp.mean(grad * grad, axis=-1, keepdims=True)
    return table - learn_rate * grad / jnp.sqrt(accum_new), accum_new


def cold_update_kernel(at_ref, table_h, accum_h, bits_h, *refs):
    parts_h = refs[:N_DP]
    out = refs[N_DP]
    parts, table, accum, bits, res, sems = refs[N_DP + 1 :]
    size = table.shape[0]
    at = pl.multiple_of(at_ref[0] * size, size)
    copies = load_all(
        [(parts_h[k], parts.at[k]) for k in range(N_DP)]
        + [
            (table_h.at[pl.ds(at, size), :], table),
            (accum_h, accum),
            (bits_h.at[pl.ds(at, size), :], bits),
        ],
        sems,
    )
    eye = iota((size, size), 0) == iota((size, size), 1)
    for c in copies:
        c.wait()
    total = parts[0].astype(F32)
    for k in range(1, N_DP):
        total = total + parts[k].astype(F32)
    touched = to_col(total[size : size + 1], eye)
    averaged = total[:size] / jnp.maximum(touched, 1.0)
    old = to_col(accum[pl.ds(at_ref[0], 1), :], eye)
    updated, accum_new = adagrad(table[...].astype(F32), old, averaged)
    grid_step = jnp.max(jnp.abs(updated), axis=-1, keepdims=True) / 8.0
    dither = bits[...].astype(F32) * (1.0 / 65280.0) - 0.5
    res[:size, :] = jnp.where(touched > 0.5, updated + grid_step * dither, updated).astype(BF)
    row = to_row(accum_new, eye)
    high = row.astype(BF).astype(F32)
    middle = (row - high).astype(BF).astype(F32)
    low = (row - high) - middle
    which = iota((16, size), 0)
    packed = jnp.where(which == 0, high, jnp.where(which == 1, middle, low))
    res[size:, :] = packed.astype(BF)
    done = pltpu.make_async_copy(res, out, sems.at[0])
    done.start()
    done.wait()


def cold_update(dp_at, table, accum, bits, parts):
    width = table.shape[1]
    size = table.shape[0] // N_DP
    packed = parts[0].shape
    return pl.pallas_call(
        cold_update_kernel,
        in_specs=[SMEM] + [HBM] * (3 + N_DP),
        out_specs=HBM,
        out_shape=jax.ShapeDtypeStruct(packed, BF),
        scratch_shapes=[
            pltpu.VMEM((N_DP,) + packed, BF),
            pltpu.VMEM((size, width), BF),
            pltpu.VMEM(accum.shape, F32),
            pltpu.VMEM((size, width), jnp.int32),
            pltpu.VMEM(packed, BF),
            pltpu.SemaphoreType.DMA((N_DP + 3,)),
        ],
        compiler_params=params(),
        name="cold_update",
    )(dp_at, table, accum, bits, *parts)


def cold_join_kernel(at_ref, *refs):
    parts = refs[:N_DP]
    out, accum_out, pieces, sems = refs[N_DP:]
    size = out.shape[0] // N_DP
    copies = load_all([(parts[i], pieces.at[i]) for i in range(N_DP)], sems)
    done = []
    for i in range(N_DP):
        copies[i].wait()
        chunk = chunk_of(at_ref[0], i)
        dst = out.at[pl.ds(pl.multiple_of(chunk * size, size), size), :]
        done.append(pltpu.make_async_copy(pieces.at[i, pl.ds(0, size), :], dst, sems.at[N_DP + i]))
        done[i].start()
        rows = pieces[i, size:, :].astype(F32)
        accum_out[pl.ds(chunk, 1), :] = (rows[2:3] + rows[1:2]) + rows[0:1]
    for c in done:
        c.wait()


def cold_join(dp_at, parts):
    width = parts[0].shape[1]
    size = parts[0].shape[0] - 16
    return pl.pallas_call(
        cold_join_kernel,
        in_specs=[SMEM] + [HBM] * N_DP,
        out_specs=(HBM, VMEM),
        out_shape=(
            jax.ShapeDtypeStruct((N_DP * size, width), BF),
            jax.ShapeDtypeStruct((N_DP, size), F32),
        ),
        scratch_shapes=[
            pltpu.VMEM((N_DP,) + parts[0].shape, BF),
            pltpu.SemaphoreType.DMA((2 * N_DP,)),
        ],
        compiler_params=params(),
        name="cold_join",
    )(dp_at, *parts)


def sum_parts_kernel(*refs):
    parts_h = refs[:N_DP]
    out, parts, sems = refs[N_DP:]
    copies = load_all([(parts_h[k], parts.at[k]) for k in range(N_DP)], sems)
    for c in copies:
        c.wait()
    out[...] = jnp.sum(parts[...], axis=0)


def sum_parts(parts):
    shape = parts[0].shape
    return pl.pallas_call(
        sum_parts_kernel,
        in_specs=[HBM] * N_DP,
        out_specs=VMEM,
        out_shape=jax.ShapeDtypeStruct(shape, F32),
        scratch_shapes=[
            pltpu.VMEM((N_DP,) + shape, F32),
            pltpu.SemaphoreType.DMA((N_DP,)),
        ],
        compiler_params=params(),
        name="sum_parts",
    )(*parts)


def hot_update_kernel(at_ref, table_h, accum_h, *refs):
    grads_h = refs[:N_DP]
    out, accum_out, table, accum, grads, res, sems = refs[N_DP:]
    size = grads.shape[1]
    copies = load_all(
        [(table_h, table), (accum_h, accum)]
        + [(grads_h[k], grads.at[k]) for k in range(N_DP)],
        sems,
    )
    eye = iota((size, size), 0) == iota((size, size), 1)
    for c in copies:
        c.wait()
    for k in range(N_DP):
        chunk = chunk_of(at_ref[0], k)
        rows = pl.ds(pl.multiple_of(chunk * size, size), size)
        old = to_col(accum[pl.ds(chunk, 1), :], eye)
        updated, accum_new = adagrad(table[rows, :], old, grads[k])
        res[rows, :] = updated
        accum_out[pl.ds(chunk, 1), :] = to_row(accum_new, eye)
    done = pltpu.make_async_copy(res, out, sems.at[0])
    done.start()
    done.wait()


def hot_update(dp_at, table, accum, grads):
    count, width = table.shape
    size = count // N_DP
    return pl.pallas_call(
        hot_update_kernel,
        in_specs=[SMEM] + [HBM] * (2 + N_DP),
        out_specs=(HBM, VMEM),
        out_shape=(
            jax.ShapeDtypeStruct((count, width), F32),
            jax.ShapeDtypeStruct((N_DP, size), F32),
        ),
        scratch_shapes=[
            pltpu.VMEM((count, width), F32),
            pltpu.VMEM((N_DP, size), F32),
            pltpu.VMEM((N_DP, size, width), F32),
            pltpu.VMEM((count, width), F32),
            pltpu.SemaphoreType.DMA((2 + N_DP,)),
        ],
        compiler_params=params(),
        name="hot_update",
    )(dp_at, table, accum, *grads)


def exchange(value, axis):
    return lax.all_to_all(value, axis, split_axis=0, concat_axis=0, tiled=True)


def shift(value, k):
    return lax.ppermute(value, "dp", [(i, (i + k) % N_DP) for i in range(N_DP)])


def to_owners(parts):
    return [parts[0]] + [shift(parts[k], k) for k in range(1, N_DP)]


def to_all(part):
    along = [part]
    for k in range(1, 4):
        perm = [(i, ((i // 2 + k) % 4) * 2 + i % 2) for i in range(N_DP)]
        along.append(lax.ppermute(part, "dp", perm))
    partner = [(i, i ^ 1) for i in range(N_DP)]
    return along + [lax.ppermute(value, "dp", partner) for value in along]


def step(
    cold_table,
    cold_accum,
    dither_bits,
    hot_table,
    hot_accum,
    w_flat,
    w_inter,
    hidden_bias,
    w_out,
    targets,
    hot_ids,
    cold_slots,
    requests,
    counts,
):
    shards = lax.axis_size("shard")
    capacity = requests.shape[1]
    row_count, row_width = cold_table.shape
    hot_count = hot_table.shape[0]
    slots = shards * capacity
    dp_at = lax.axis_index("dp").astype(jnp.int32).reshape(1)

    live = jnp.arange(capacity, dtype=jnp.int32) < counts[:, :, None]
    asked = jnp.where(live, requests.reshape(MB, shards, capacity), -1)
    asked = asked.transpose(1, 0, 2).reshape(shards, MB * capacity)
    wanted = exchange(asked, "shard")

    fetched = []
    for m in range(MB):
        rows = serve(m, m == 1, wanted, cold_table)
        if m == 1:
            rows, hits = rows
        rows = exchange(rows.reshape(shards, capacity, row_width), "shard")
        fetched.append(rows.reshape(slots, row_width))
    xh = hot_rows(hot_ids, hot_table)

    owned = []
    hot_parts = []
    for m in range(MB):
        slot_grad, *hot_part = backprop(
            m,
            fetched[m],
            xh,
            cold_slots,
            cold_slots.T,
            targets.reshape(1, -1),
            w_flat,
            w_inter,
            hidden_bias.reshape(1, -1),
            w_out.reshape(1, -1),
        )
        hot_parts += hot_part
        rows = exchange(slot_grad.reshape(shards, capacity, row_width), "shard")
        owned.append(rows.reshape(slots, row_width))

    hot_grads = hot_scatter(0, dp_at, hot_ids.T, *hot_parts[:2], None, hot_count)
    hot_grads = hot_scatter(1, dp_at, hot_ids.T, *hot_parts[2:], hot_grads, hot_count)
    hot_grads = to_owners(hot_grads)
    hot_all = sum_parts(hot_grads)
    step_bit = 1
    while step_bit < shards:
        perm = [(i, i ^ step_bit) for i in range(shards)]
        hot_all = hot_all + lax.ppermute(hot_all, "shard", perm)
        step_bit *= 2
    hot_all = to_all(hot_all)
    hot_out, hot_accum_out = hot_update(
        dp_at, hot_table, hot_accum.reshape(N_DP, -1), hot_all
    )

    first = owner_first(wanted, owned[0], row_count)
    parts = owner_second(dp_at, wanted, hits.reshape(N_DP, -1), owned[1], first)
    parts = to_owners(parts)
    packed = cold_update(
        dp_at, cold_table, cold_accum.reshape(N_DP, -1), dither_bits, parts
    )
    parts = to_all(packed)
    cold_out, cold_accum_out = cold_join(dp_at, parts)
    return (cold_out, cold_accum_out.reshape(-1), hot_out, hot_accum_out.reshape(-1))


def solution(mesh):
    return jax.shard_map(
        step,
        mesh=mesh,
        in_specs=(
            P("shard", None),
            P("shard"),
            P("shard", None),
            P(),
            P(),
            P(),
            P(),
            P(),
            P(),
            P(("shard", "dp")),
            P(("shard", "dp"), None),
            P(("shard", "dp"), None),
            P(("shard", "dp"), None),
            P(("shard", "dp"), None),
        ),
        out_specs=(P("shard", None), P("shard"), P(), P()),
        check_vma=False,
    )
```

```python
import jax
import jax.numpy as jnp
from jax import lax
from jax.experimental import pallas as pl
from jax.experimental.pallas import tpu as pltpu
from jax.sharding import PartitionSpec as P


MB = 2
GROUP = 16
FEATS = 16
F_COLD = 8
BF = jnp.bfloat16
F32 = jnp.float32
NT = (((1,), (1,)), ((), ()))
HBM = pl.BlockSpec(memory_space=pltpu.HBM)
VMEM = pl.BlockSpec(memory_space=pltpu.VMEM)
SMEM = pl.BlockSpec(memory_space=pltpu.SMEM)
N_DP = 8
N_X = 4
VMEM_LIMIT = 64 << 20
learn_rate = 0.3
UNROLL = 4


def iota(shape, axis):
    return lax.broadcasted_iota(jnp.int32, shape, axis)


def as_one(same):
    return jnp.where(same, jnp.ones(same.shape, BF), jnp.zeros(same.shape, BF))


def chunk_of(at, i):
    x = ((at >> 1) - (i & 3)) & 3
    return x * 2 + ((at & 1) ^ (i >> 2))


def params():
    return pltpu.CompilerParams(vmem_limit_bytes=VMEM_LIMIT)


def small_params():
    return pltpu.CompilerParams(vmem_limit_bytes=20 << 20)


def load_all(pairs, sems):
    copies = [pltpu.make_async_copy(s, d, sems.at[i]) for i, (s, d) in enumerate(pairs)]
    for c in copies:
        c.start()
    return copies


def match_rows(ids, match, at, count):
    lanes = iota((GROUP, count), 1).astype(jnp.int16)
    for f in range(F_COLD):
        mine = jnp.broadcast_to(ids[:, f : f + 1], (GROUP, 128)).astype(jnp.int16)
        same = lanes == jnp.concatenate([mine] * (count // 128), axis=1)
        match[pl.ds(at + f * GROUP, GROUP), :count] = as_one(same)


def hot_rows_kernel(hot_ids, table, later, out, ids, src, match, res, sems):
    copies = load_all([(hot_ids, ids), (table, src)], sems)
    for c in copies:
        c.wait()
    source = src[...].astype(BF)
    half = F_COLD * GROUP
    block = 4
    steps = ids.shape[0] // GROUP // block

    def body(b, carry):
        for q in range(block):
            part = pl.ds(pl.multiple_of((b * block + q) * GROUP, GROUP), GROUP)
            match_rows(ids[part, :], match, q * half, source.shape[0])
        rows = pl.ds(pl.multiple_of(b * block * half, block * half), block * half)
        res[rows, :] = jnp.dot(match[...], source, preferred_element_type=F32).astype(BF)
        return carry

    lax.fori_loop(0, steps, body, 0)
    done = pltpu.make_async_copy(res, out, sems.at[2])
    done.start()
    done.wait()


def hot_rows(hot_ids, table, later):
    count, width = table.shape
    rows = hot_ids.shape[0] * F_COLD
    return pl.pallas_call(
        hot_rows_kernel,
        in_specs=[HBM] * 3,
        out_specs=HBM,
        out_shape=jax.ShapeDtypeStruct((rows, width), BF),
        scratch_shapes=[
            pltpu.VMEM(hot_ids.shape, jnp.int32),
            pltpu.VMEM(table.shape, F32),
            pltpu.VMEM((512, count), BF),
            pltpu.VMEM((rows, width), BF),
            pltpu.SemaphoreType.DMA((3,)),
        ],
        compiler_params=params(),
        name="hot_rows",
    )(hot_ids, table, later)


def step_kernel(m, *refs):
    (
        fetched_h, xh_h, slots_h, slots_t_h, targets_h, flat_h, inter_h, bias_h, w_out_h,
        slot_grad, hot_hi, hot_lo,
        fetched, x, slots, slots_t, targets, w_flat, w_inter, bias, w_out,
        a, pairs, back, mirror, g_hi, g_lo, h_hi, h_lo, match, slopes, sems,
    ) = refs
    width = fetched.shape[1]
    samples = targets.shape[1]
    groups = samples // GROUP
    lane_group = FEATS * GROUP
    half = F_COLD * GROUP
    scale = width ** (-0.5)
    block = 4
    first = m * samples

    head = load_all(
        [
            (slots_h.at[pl.ds(first, samples), :], slots),
            (fetched_h, fetched),
        ],
        sems,
    )
    hot_copies = [
        pltpu.make_async_copy(
            xh_h.at[pl.ds((m * groups + g) * half, half), :],
            x.at[pl.ds(g * lane_group + half, half), :],
            sems.at[2],
        )
        for g in range(groups)
    ]
    for c in hot_copies:
        c.start()
    tail = load_all(
        [
            (flat_h, w_flat),
            (inter_h, w_inter),
            (bias_h, bias),
            (w_out_h, w_out),
            (targets_h.at[:, pl.ds(first, samples)], targets),
            (slots_t_h.at[:, pl.ds(first, samples)], slots_t),
        ],
        sems.at[pl.ds(3, 6)],
    )

    sq = (lane_group, lane_group)
    i_hi = iota(sq, 0) >> 4
    i_lo = iota(sq, 0) & 15
    j_hi = iota(sq, 1) >> 4
    j_lo = iota(sq, 1) & 15
    spread = jnp.where(i_hi == j_lo, 1.0, 0.0).astype(BF)
    spread_t = jnp.where(i_lo == j_hi, 1.0, 0.0).astype(BF)
    swap = jnp.where((i_hi == j_lo) & (i_lo == j_hi), 1.0, 0.0).astype(BF)

    for c in head:
        c.wait()

    def gather(b, carry):
        for q in range(block):
            part = pl.ds(pl.multiple_of((b * block + q) * GROUP, GROUP), GROUP)
            match_rows(slots[part, :], match, q * half, fetched.shape[0])
        picked = jnp.dot(match[...], fetched[...], preferred_element_type=F32).astype(BF)
        for q in range(block):
            dst = pl.multiple_of((b * block + q) * lane_group, lane_group)
            x[pl.ds(dst, half), :] = picked[q * half : (q + 1) * half]
        return carry

    lax.fori_loop(0, groups // block, gather, 0)
    for c in hot_copies:
        c.wait()

    def dots(i, carry):
        for u in range(UNROLL):
            g = i * UNROLL + u
            rows = pl.ds(pl.multiple_of(g * lane_group, lane_group), lane_group)
            part = pl.ds(pl.multiple_of(g * GROUP, GROUP), GROUP)
            xg = x[rows, :]
            for f in range(FEATS):
                a[part, f * width : (f + 1) * width] = xg[f * GROUP : (f + 1) * GROUP]
            gram = lax.dot_general(xg, xg, NT, preferred_element_type=F32) * scale
            own = jnp.where(i_lo == j_lo, gram, 0.0).astype(BF)
            wide = jnp.dot(own, spread, preferred_element_type=F32)
            wide = jnp.where(i_hi == j_hi, wide, 0.0)
            pairs[part, :] = jnp.sum(
                wide.reshape(FEATS, GROUP, lane_group), axis=0
            ).astype(BF)
        return carry

    lax.fori_loop(0, groups // UNROLL, dots, 0)
    for c in tail:
        c.wait()

    pre = jnp.dot(a[...], w_flat[...], preferred_element_type=F32)
    pre = pre + jnp.dot(pairs[...], w_inter[...], preferred_element_type=F32)
    pre = pre + bias[...]
    gated = jax.nn.sigmoid(pre)
    logits = jnp.sum(pre * gated * w_out[...], axis=-1, keepdims=True)
    eye = iota((samples, samples), 0) == iota((samples, samples), 1)
    target = jnp.sum(jnp.where(eye, targets[...], 0.0), axis=1, keepdims=True)
    residual = jax.nn.sigmoid(logits) - target
    slopes[...] = (residual * w_out[...] * gated * (1.0 + pre * (1.0 - gated))).astype(BF)

    inter_t = jnp.dot(swap, w_inter[...], preferred_element_type=F32).astype(BF)
    both = lax.dot_general(slopes[...], w_inter[...], NT, preferred_element_type=F32)
    both = both + lax.dot_general(slopes[...], inter_t, NT, preferred_element_type=F32)
    mirror[...] = (both * scale).astype(BF)

    def flat_back(f, carry):
        rows = pl.ds(pl.multiple_of(f * width, width), width)
        back[f] = lax.dot_general(
            slopes[...], w_flat[rows, :], NT, preferred_element_type=F32
        )
        return carry

    lax.fori_loop(0, FEATS, flat_back, 0)

    def grads(i, carry):
        for u in range(UNROLL):
            g = i * UNROLL + u
            rows = pl.ds(pl.multiple_of(g * lane_group, lane_group), lane_group)
            part = pl.ds(pl.multiple_of(g * GROUP, GROUP), GROUP)
            mine = mirror[part, :].astype(F32)
            tall = jnp.broadcast_to(mine[None], (FEATS, GROUP, lane_group)).reshape(sq)
            tall = jnp.where(i_hi == j_hi, tall, 0.0).astype(BF)
            wide = jnp.dot(tall, spread_t, preferred_element_type=F32)
            wide = jnp.where(i_lo == j_lo, wide, 0.0).astype(BF)
            total = jnp.dot(wide, x[rows, :], preferred_element_type=F32)
            total = total + back[:, part, :].reshape(lane_group, width)
            hi = total.astype(BF)
            lo = (total - hi.astype(F32)).astype(BF)
            for f in range(F_COLD):
                dst = pl.ds(pl.multiple_of(f * samples + g * GROUP, GROUP), GROUP)
                at = f * GROUP
                g_hi[dst, :] = hi[at : at + GROUP]
                g_lo[dst, :] = lo[at : at + GROUP]
                h_hi[dst, :] = hi[half + at : half + at + GROUP]
                h_lo[dst, :] = lo[half + at : half + at + GROUP]
        return carry

    lax.fori_loop(0, groups // UNROLL, grads, 0)
    outs = load_all([(h_hi, hot_hi), (h_lo, hot_lo)], sems.at[pl.ds(0, 2)])

    rows_blk = 512

    def scatter(b, carry):
        at = pl.multiple_of(b * rows_blk, rows_blk)
        subs = iota((rows_blk, samples), 0).astype(jnp.int16)
        for f in range(F_COLD):
            mine = jnp.broadcast_to(slots_t[f : f + 1, :] - at, (16, samples)).astype(jnp.int16)
            same = subs == jnp.concatenate([mine] * (rows_blk // 16), axis=0)
            match[:, f * samples : (f + 1) * samples] = as_one(same)
        total = jnp.dot(match[...], g_hi[...], preferred_element_type=F32)
        total = total + jnp.dot(match[...], g_lo[...], preferred_element_type=F32)
        fetched[pl.ds(at, rows_blk), :] = total.astype(BF)
        pltpu.make_async_copy(
            fetched.at[pl.ds(at, rows_blk), :], slot_grad.at[pl.ds(at, rows_blk), :], sems.at[3 + b]
        ).start()
        return carry

    n_out = slot_grad.shape[0] // rows_blk
    lax.fori_loop(0, n_out, scatter, 0)
    for b in range(n_out):
        pltpu.make_async_copy(
            fetched.at[pl.ds(b * rows_blk, rows_blk), :],
            slot_grad.at[pl.ds(b * rows_blk, rows_blk), :],
            sems.at[3 + b],
        ).wait()
    for c in outs:
        c.wait()


def backprop(m, fetched, xh, slots, slots_t, targets, w_flat, w_inter, bias, w_out):
    count, width = fetched.shape
    samples = slots.shape[0] // MB
    hidden = w_flat.shape[1]
    lookups = samples * F_COLD
    wide = FEATS * width
    rows = jax.ShapeDtypeStruct((lookups, width), BF)
    return pl.pallas_call(
        lambda *refs: step_kernel(m, *refs),
        in_specs=[HBM] * 9,
        out_specs=(HBM,) * 3,
        out_shape=(jax.ShapeDtypeStruct((count, width), BF), rows, rows),
        scratch_shapes=[
            pltpu.VMEM((count, width), BF),
            pltpu.VMEM((samples * FEATS, width), BF),
            pltpu.VMEM((samples, F_COLD), jnp.int32),
            pltpu.VMEM((F_COLD, samples), jnp.int32),
            pltpu.VMEM((1, samples), F32),
            pltpu.VMEM(w_flat.shape, BF),
            pltpu.VMEM(w_inter.shape, BF),
            pltpu.VMEM((1, hidden), F32),
            pltpu.VMEM((1, hidden), F32),
            pltpu.VMEM((samples, wide), BF),
            pltpu.VMEM((samples, FEATS * FEATS), BF),
            pltpu.VMEM((FEATS, samples, width), F32),
            pltpu.VMEM((samples, FEATS * FEATS), BF),
            pltpu.VMEM((lookups, width), BF),
            pltpu.VMEM((lookups, width), BF),
            pltpu.VMEM((lookups, width), BF),
            pltpu.VMEM((lookups, width), BF),
            pltpu.VMEM((512, 2048), BF),
            pltpu.VMEM((samples, hidden), BF),
            pltpu.SemaphoreType.DMA((9,)),
        ],
        compiler_params=params(),
        name="train_step",
    )(fetched, xh, slots, slots_t, targets, w_flat, w_inter, bias, w_out)


def hot_scatter_kernel(at_ref, ids_h, hi0, lo0, hi1, lo1, *refs):
    outs = refs[:N_X]
    other, ids, h0, l0, h1, l1, match, res, sems = refs[N_X:]
    copies = load_all([(ids_h, ids), (hi0, h0), (lo0, l0), (hi1, h1), (lo1, l1)], sems)
    samples = ids.shape[1] // MB
    block = match.shape[1]
    size = res.shape[0] // N_DP
    subs = iota((block, samples), 0).astype(jnp.int16)
    copies[0].wait()

    def body(b, carry):
        at = pl.multiple_of(b * block, block)
        total = None
        for m, parts in enumerate(((h0, l0), (h1, l1))):
            for f in range(F_COLD):
                row = ids[f : f + 1, m * samples : (m + 1) * samples] - at
                mine = jnp.broadcast_to(row, (16, samples)).astype(jnp.int16)
                same = subs == jnp.concatenate([mine] * (block // 16), axis=0)
                match[m, :, f * samples : (f + 1) * samples] = as_one(same)

            @pl.when(b == 0)
            def _():
                copies[1 + 2 * m].wait()
                copies[2 + 2 * m].wait()

            for part in parts:
                term = jnp.dot(match[m], part[...], preferred_element_type=F32)
                total = term if total is None else total + term
        res[pl.ds(at, block), :] = total
        for q in range(block // size):
            chunk = b * (block // size) + q
            src = res.at[pl.ds(pl.multiple_of(chunk * size, size), size), :]
            place = ((chunk >> 1) - (at_ref[0] >> 1)) & (N_X - 1)
            mine = (chunk & 1) == (at_ref[0] & 1)
            for k in range(N_X):

                @pl.when(mine & (place == k))
                def _():
                    pltpu.make_async_copy(src, outs[k], sems.at[5 + k]).start()

            @pl.when(jnp.logical_not(mine))
            def _():
                pltpu.make_async_copy(src, other.at[place], sems.at[5 + N_X + place]).start()

        return carry

    lax.fori_loop(0, res.shape[0] // block, body, 0)
    for k in range(N_X):
        src = res.at[pl.ds(0, size), :]
        pltpu.make_async_copy(src, outs[k], sems.at[5 + k]).wait()
        pltpu.make_async_copy(src, other.at[k], sems.at[5 + N_X + k]).wait()


def hot_scatter(dp_at, ids, hi0, lo0, hi1, lo1, count):
    rows, width = hi0.shape
    return pl.pallas_call(
        hot_scatter_kernel,
        in_specs=[SMEM] + [HBM] * 5,
        out_specs=(HBM,) * (N_X + 1),
        out_shape=(jax.ShapeDtypeStruct((count // N_DP, width), F32),) * N_X
        + (jax.ShapeDtypeStruct((N_X, count // N_DP, width), F32),),
        scratch_shapes=[pltpu.VMEM(ids.shape, jnp.int32)]
        + [pltpu.VMEM((rows, width), BF)] * 4
        + [
            pltpu.VMEM((MB, 256, rows), BF),
            pltpu.VMEM((count, width), F32),
            pltpu.SemaphoreType.DMA((5 + N_DP,)),
        ],
        compiler_params=params(),
        name="hot_scatter",
    )(dp_at, ids, hi0, lo0, hi1, lo1)


def serve_kernel(m, with_hits, wanted, table_h, rows, *refs):
    if with_hits:
        hits, table, match, res, count_acc, sems = refs
    else:
        table, match, res, sems = refs
    load = pltpu.make_async_copy(table_h, table, sems.at[0])
    load.start()
    shards, lanes = wanted.shape
    capacity = lanes // MB
    count = table.shape[0]
    per = 8
    block = per * capacity
    ids = jnp.concatenate([wanted[...], jnp.zeros((lanes - shards, lanes), jnp.int32)], axis=0)
    turned = ids.T
    names = iota((capacity, count), 1).astype(jnp.int16)
    if with_hits:
        count_acc[...] = jnp.zeros_like(count_acc)

    def ones_of(part, mb, j):
        col = part[mb * capacity : (mb + 1) * capacity, j : j + 1]
        mine = jnp.broadcast_to(col, (capacity, 128)).astype(jnp.int16)
        return as_one(names == jnp.concatenate([mine] * (count // 128), axis=1))

    def add_hits(one):
        tall = one[0:16] + one[16:32] + one[32:48] + one[48:64]
        count_acc[...] += tall

    def body(b, carry):
        part = pltpu.roll(turned, lanes - b * per, 1)
        for j in range(per):
            one = ones_of(part, m, j)
            match[j * capacity : (j + 1) * capacity, :] = one
            if with_hits:
                add_hits(one)
                for other in range(MB):
                    if other != m:
                        add_hits(ones_of(part, other, j))
        at = pl.ds(pl.multiple_of(b * block, block), block)

        @pl.when(b == 0)
        def _():
            load.wait()

        res[at, :] = jnp.dot(match[...], table[...], preferred_element_type=F32).astype(BF)
        pltpu.make_async_copy(res.at[at, :], rows.at[at, :], sems.at[1 + b]).start()
        return carry

    steps = shards // per
    lax.fori_loop(0, steps, body, 0)
    if with_hits:
        total = jnp.sum(count_acc[...].astype(F32), axis=0, keepdims=True)
        size = count // N_DP
        for p in range(N_DP):
            hits[p : p + 1, :] = total[:, p * size : (p + 1) * size]
    for b in range(steps):
        at = pl.ds(b * block, block)
        pltpu.make_async_copy(res.at[at, :], rows.at[at, :], sems.at[1 + b]).wait()


def serve(m, with_hits, wanted, table):
    shards, lanes = wanted.shape
    capacity = lanes // MB
    slots = shards * capacity
    count, width = table.shape
    rows = jax.ShapeDtypeStruct((slots, width), BF)
    extra = [pltpu.VMEM((16, count), BF)] if with_hits else []
    return pl.pallas_call(
        lambda *refs: serve_kernel(m, with_hits, *refs),
        in_specs=[VMEM, HBM],
        out_specs=(HBM, VMEM) if with_hits else HBM,
        out_shape=(rows, jax.ShapeDtypeStruct((N_DP, count // N_DP), F32))
        if with_hits
        else rows,
        scratch_shapes=[
            pltpu.VMEM(table.shape, BF),
            pltpu.VMEM((512, count), BF),
            pltpu.VMEM((slots, width), BF),
        ]
        + extra
        + [pltpu.SemaphoreType.DMA((1 + shards // 8,))],
        compiler_params=params(),
        name="serve_rows",
    )(wanted, table)


def id_tiles(wanted, m):
    ids = wanted[...]
    other = pltpu.roll(ids, 64, 1)
    left, right = (ids, other) if m == 0 else (other, ids)
    low = iota((1, 128), 1) < 64
    return [
        jnp.where(low, left[2 * i : 2 * i + 1], right[2 * i + 1 : 2 * i + 2])
        for i in range(ids.shape[0] // 2)
    ]


def owner_match(tiles, base, match, subs):
    size = match.shape[0]
    for i, tile in enumerate(tiles):
        mine = jnp.broadcast_to(tile - base, (16, 128)).astype(jnp.int16)
        same = subs == jnp.concatenate([mine] * (size // 16), axis=0)
        match[:, i * 128 : (i + 1) * 128] = as_one(same)


def owner_first_kernel(wanted, grads_h, out, grads, match, res, sems):
    load = pltpu.make_async_copy(grads_h, grads, sems.at[0])
    load.start()
    block = match.shape[0]
    tiles = id_tiles(wanted, 0)
    subs = iota((block, 128), 0).astype(jnp.int16)
    steps = res.shape[0] // block

    def body(b, carry):
        at = pl.multiple_of(b * block, block)
        owner_match(tiles, at, match, subs)

        @pl.when(b == 0)
        def _():
            load.wait()

        rows = pl.ds(at, block)
        res[rows, :] = jnp.dot(match[...], grads[...], preferred_element_type=F32)
        pltpu.make_async_copy(res.at[rows, :], out.at[rows, :], sems.at[1 + b]).start()
        return carry

    lax.fori_loop(0, steps, body, 0)
    for b in range(steps):
        rows = pl.ds(b * block, block)
        pltpu.make_async_copy(res.at[rows, :], out.at[rows, :], sems.at[1 + b]).wait()


def owner_first(wanted, grads, count):
    slots, width = grads.shape
    return pl.pallas_call(
        owner_first_kernel,
        in_specs=[VMEM, HBM],
        out_specs=HBM,
        out_shape=jax.ShapeDtypeStruct((count, width), F32),
        scratch_shapes=[
            pltpu.VMEM((slots, width), BF),
            pltpu.VMEM((256, slots), BF),
            pltpu.VMEM((count, width), F32),
            pltpu.SemaphoreType.DMA((1 + count // 256,)),
        ],
        compiler_params=params(),
        name="owner_first",
    )(wanted, grads)


def owner_second_kernel(at_ref, wanted, hits, grads_h, prev_h, *refs):
    outs = refs[:N_X]
    other, grads, prev, match, res, sems = refs[N_X:]
    size = match.shape[0]
    load = pltpu.make_async_copy(grads_h, grads, sems.at[0])
    load.start()
    load_prev = pltpu.make_async_copy(prev_h, prev, sems.at[1])
    load_prev.start()
    tiles = id_tiles(wanted, 1)
    subs = iota((size, 128), 0).astype(jnp.int16)

    def body(k, carry):
        x = ((at_ref[0] >> 1) + k) & (N_X - 1)
        chunk = x * 2 + ((at_ref[0] & 1) ^ (1 - (k >> 2)))
        at = pl.multiple_of(chunk * size, size)
        owner_match(tiles, at, match, subs)

        @pl.when(k == 0)
        def _():
            load.wait()

        total = jnp.dot(match[...], grads[...], preferred_element_type=F32)

        @pl.when(k == 0)
        def _():
            load_prev.wait()

        total = total + prev[pl.ds(at, size), :]
        res[k, :size, :] = total.astype(BF)
        mine = hits[pl.ds(chunk, 1), :]
        res[k, size:, :] = jnp.broadcast_to(mine, (16, size)).astype(BF)

        @pl.when(k < N_X)
        def _():
            place = k & (N_X - 1)
            pltpu.make_async_copy(res.at[k], other.at[place], sems.at[2 + k]).start()

        for j in range(N_X):

            @pl.when(k == N_X + j)
            def _():
                pltpu.make_async_copy(res.at[k], outs[j], sems.at[2 + k]).start()

        return carry

    lax.fori_loop(0, N_DP, body, 0)
    for j in range(N_X):
        pltpu.make_async_copy(res.at[j], other.at[j], sems.at[2 + j]).wait()
        pltpu.make_async_copy(res.at[N_X + j], outs[j], sems.at[2 + N_X + j]).wait()


def owner_second(dp_at, wanted, hits, grads, prev):
    slots, width = grads.shape
    count = prev.shape[0]
    size = count // N_DP
    return pl.pallas_call(
        owner_second_kernel,
        in_specs=[SMEM, VMEM, VMEM, HBM, HBM],
        out_specs=(HBM,) * (N_X + 1),
        out_shape=(jax.ShapeDtypeStruct((size + 16, width), BF),) * N_X
        + (jax.ShapeDtypeStruct((N_X, size + 16, width), BF),),
        scratch_shapes=[
            pltpu.VMEM((slots, width), BF),
            pltpu.VMEM((count, width), F32),
            pltpu.VMEM((size, slots), BF),
            pltpu.VMEM((N_DP, size + 16, width), BF),
            pltpu.SemaphoreType.DMA((2 + N_DP,)),
        ],
        compiler_params=params(),
        name="owner_second",
    )(dp_at, wanted, hits, grads, prev)


def to_col(row, eye):
    return jnp.sum(jnp.where(eye, row, 0.0), axis=1, keepdims=True)


def to_row(col, eye):
    return jnp.sum(jnp.where(eye, col, 0.0), axis=0, keepdims=True)


def adagrad(table, accum, grad):
    accum_new = accum + jnp.mean(grad * grad, axis=-1, keepdims=True)
    return table - learn_rate * grad / jnp.sqrt(accum_new), accum_new


def pick_kernel(at_ref, table_h, bits_h, table_out, bits_out, table, bits, sems):
    size = table.shape[0]
    rows = pl.ds(pl.multiple_of(at_ref[0] * size, size), size)
    for pairs in (
        [(table_h.at[rows, :], table), (bits_h.at[rows, :], bits)],
        [(table, table_out), (bits, bits_out)],
    ):
        for c in load_all(pairs, sems):
            c.wait()


def pick(dp_at, table, bits):
    shape = (table.shape[0] // N_DP, table.shape[1])
    return pl.pallas_call(
        pick_kernel,
        in_specs=[SMEM, HBM, HBM],
        out_specs=(HBM, HBM),
        out_shape=(
            jax.ShapeDtypeStruct(shape, table.dtype),
            jax.ShapeDtypeStruct(shape, bits.dtype),
        ),
        scratch_shapes=[
            pltpu.VMEM(shape, table.dtype),
            pltpu.VMEM(shape, bits.dtype),
            pltpu.SemaphoreType.DMA((2,)),
        ],
        compiler_params=params(),
        name="pick_rows",
    )(dp_at, table, bits)


def cold_update_kernel(at_ref, table, accum, bits, *refs):
    parts = refs[:N_X]
    out = refs[N_X]
    size = table.shape[0]
    eye = iota((size, size), 0) == iota((size, size), 1)
    total = parts[0][...].astype(F32)
    for k in range(1, N_X):
        total = total + parts[k][...].astype(F32)
    touched = to_col(total[size : size + 1], eye)
    averaged = total[:size] / jnp.maximum(touched, 1.0)
    at = at_ref[0] * 2
    old = jnp.concatenate([accum[pl.ds(at, 1), :], accum[pl.ds(at + 1, 1), :]], axis=1)
    old = to_col(old, eye)
    updated, accum_new = adagrad(table[...].astype(F32), old, averaged)
    grid_step = jnp.max(jnp.abs(updated), axis=-1, keepdims=True) / 8.0
    dither = bits[...].astype(F32) * (1.0 / 65280.0) - 0.5
    out[:size, :] = jnp.where(touched > 0.5, updated + grid_step * dither, updated).astype(BF)
    row = to_row(accum_new, eye)
    high = row.astype(BF).astype(F32)
    middle = (row - high).astype(BF).astype(F32)
    low = (row - high) - middle
    which = iota((16, size), 0)
    packed = jnp.where(which == 0, high, jnp.where(which == 1, middle, low))
    out[size:, :] = packed.astype(BF)


def cold_update(dp_at, table, accum, bits, parts):
    return pl.pallas_call(
        cold_update_kernel,
        in_specs=[SMEM] + [VMEM] * (3 + N_X),
        out_specs=VMEM,
        out_shape=jax.ShapeDtypeStruct(parts[0].shape, BF),
        compiler_params=small_params(),
        name="cold_update",
    )(dp_at, table, accum, bits, *parts)


def cold_join_kernel(at_ref, *refs):
    parts = refs[:N_DP]
    out, accum_out, sems = refs[N_DP:]
    size = out.shape[0] // N_DP
    done = []
    for i in range(N_DP):
        chunk = chunk_of(at_ref[0], i)
        dst = out.at[pl.ds(pl.multiple_of(chunk * size, size), size), :]
        done.append(pltpu.make_async_copy(parts[i].at[pl.ds(0, size), :], dst, sems.at[i]))
        done[i].start()
    for i in range(N_DP):
        chunk = chunk_of(at_ref[0], i)
        rows = parts[i][size:, :].astype(F32)
        row = (rows[2:3] + rows[1:2]) + rows[0:1]
        accum_out[pl.ds(chunk * 2, 1), :] = row[:, :128]
        accum_out[pl.ds(chunk * 2 + 1, 1), :] = row[:, 128:]
    for c in done:
        c.wait()


def cold_join(dp_at, parts):
    width = parts[0].shape[1]
    size = parts[0].shape[0] - 16
    return pl.pallas_call(
        cold_join_kernel,
        in_specs=[SMEM] + [VMEM] * N_DP,
        out_specs=(HBM, VMEM),
        out_shape=(
            jax.ShapeDtypeStruct((N_DP * size, width), BF),
            jax.ShapeDtypeStruct((N_DP * size // 128, 128), F32),
        ),
        scratch_shapes=[pltpu.SemaphoreType.DMA((N_DP,))],
        compiler_params=small_params(),
        name="cold_join",
    )(dp_at, *parts)


def pair_sum_kernel(*refs):
    mine_h = refs[:N_X]
    other_h = refs[N_X]
    outs = refs[N_X + 1 : 2 * N_X + 1]
    mine, other, sems = refs[2 * N_X + 1 :]
    copies = load_all([(mine_h[k], mine.at[k]) for k in range(N_X)] + [(other_h, other)], sems)
    for c in copies:
        c.wait()
    mine[...] = (mine[...].astype(F32) + other[...].astype(F32)).astype(mine.dtype)
    done = load_all([(mine.at[k], outs[k]) for k in range(N_X)], sems)
    for c in done:
        c.wait()


def pair_sum(mine, other):
    outs = tuple(jax.ShapeDtypeStruct(part.shape, part.dtype) for part in mine)
    return pl.pallas_call(
        pair_sum_kernel,
        in_specs=[HBM] * (N_X + 1),
        out_specs=(HBM,) * N_X,
        out_shape=outs,
        scratch_shapes=[
            pltpu.VMEM(other.shape, other.dtype),
            pltpu.VMEM(other.shape, other.dtype),
            pltpu.SemaphoreType.DMA((N_X + 1,)),
        ],
        compiler_params=params(),
        name="pair_sum",
    )(*mine, other)


def sum_parts_kernel(*refs):
    parts = refs[:N_X]
    out = refs[N_X]
    out[...] = (parts[0][...] + parts[1][...]) + (parts[2][...] + parts[3][...])


def sum_parts(parts):
    return pl.pallas_call(
        sum_parts_kernel,
        in_specs=[VMEM] * N_X,
        out_specs=VMEM,
        out_shape=jax.ShapeDtypeStruct(parts[0].shape, F32),
        compiler_params=small_params(),
        name="sum_parts",
    )(*parts)


def hot_update_kernel(at_ref, table_h, accum_h, *refs):
    grads = refs[:N_DP]
    out, accum_out, table, accum, res, sems = refs[N_DP:]
    size = grads[0].shape[0]
    copies = load_all([(table_h, table), (accum_h, accum)], sems)
    eye = iota((size, size), 0) == iota((size, size), 1)
    for c in copies:
        c.wait()
    done = []
    for k in range(N_DP):
        chunk = chunk_of(at_ref[0], k)
        rows = pl.ds(pl.multiple_of(chunk * size, size), size)
        old = to_col(accum[pl.ds(chunk, 1), :], eye)
        updated, accum_new = adagrad(table[rows, :], old, grads[k][...])
        res[rows, :] = updated
        accum_out[pl.ds(chunk, 1), :] = to_row(accum_new, eye)
        done.append(pltpu.make_async_copy(res.at[rows, :], out.at[rows, :], sems.at[2 + k]))
        done[k].start()
    for c in done:
        c.wait()


def hot_update(dp_at, table, accum, grads):
    count, width = table.shape
    size = count // N_DP
    return pl.pallas_call(
        hot_update_kernel,
        in_specs=[SMEM] + [HBM] * 2 + [VMEM] * N_DP,
        out_specs=(HBM, VMEM),
        out_shape=(
            jax.ShapeDtypeStruct((count, width), F32),
            jax.ShapeDtypeStruct((N_DP, size), F32),
        ),
        scratch_shapes=[
            pltpu.VMEM((count, width), F32),
            pltpu.VMEM((N_DP, size), F32),
            pltpu.VMEM((count, width), F32),
            pltpu.SemaphoreType.DMA((2 + N_DP,)),
        ],
        compiler_params=small_params(),
        name="hot_update",
    )(dp_at, table, accum, *grads)


def exchange(value, axis):
    return lax.all_to_all(value, axis, split_axis=0, concat_axis=0, tiled=True)


def along_x(value, k):
    perm = [(i, ((i // 2 + k) % N_X) * 2 + i % 2) for i in range(N_DP)]
    return lax.ppermute(value, "dp", perm)


def to_partner(value):
    return lax.ppermute(value, "dp", [(i, i ^ 1) for i in range(N_DP)])


def to_owners(parts):
    *mine, other = parts
    other = to_partner(other)
    mine = pair_sum(mine, other)
    return [mine[0]] + [along_x(mine[k], k) for k in range(1, N_X)]


def to_all(part):
    along = [part] + [along_x(part, k) for k in range(1, N_X)]
    return along + [to_partner(value) for value in along]


def step(
    cold_table,
    cold_accum,
    dither_bits,
    hot_table,
    hot_accum,
    w_flat,
    w_inter,
    hidden_bias,
    w_out,
    targets,
    hot_ids,
    cold_slots,
    requests,
    counts,
):
    shards = lax.axis_size("shard")
    capacity = requests.shape[1]
    row_count, row_width = cold_table.shape
    hot_count = hot_table.shape[0]
    slots = shards * capacity
    dp_at = lax.axis_index("dp").astype(jnp.int32).reshape(1)

    live = jnp.arange(capacity, dtype=jnp.int32) < counts[:, :, None]
    asked = jnp.where(live, requests.reshape(MB, shards, capacity), -1)
    asked = asked.transpose(1, 0, 2).reshape(shards, MB * capacity)
    wanted = exchange(asked, "shard")

    fetched = []
    for m in range(MB):
        rows = serve(m, m == 1, wanted, cold_table)
        if m == 1:
            rows, hits = rows
        rows = exchange(rows.reshape(shards, capacity, row_width), "shard")
        fetched.append(rows.reshape(slots, row_width))
    own_table, own_bits = pick(dp_at, cold_table, dither_bits)
    xh = hot_rows(hot_ids, hot_table, cold_slots)

    owned = []
    hot_parts = []
    for m in range(MB):
        slot_grad, *hot_part = backprop(
            m,
            fetched[m],
            xh,
            cold_slots,
            cold_slots.T,
            targets.reshape(1, -1),
            w_flat,
            w_inter,
            hidden_bias.reshape(1, -1),
            w_out.reshape(1, -1),
        )
        hot_parts += hot_part
        rows = exchange(slot_grad.reshape(shards, capacity, row_width), "shard")
        owned.append(rows.reshape(slots, row_width))

    hot_grads = hot_scatter(dp_at, hot_ids.T, *hot_parts, hot_count)
    hot_grads = to_owners(hot_grads)
    hot_all = sum_parts(hot_grads)
    step_bit = 1
    while step_bit < shards:
        perm = [(i, i ^ step_bit) for i in range(shards)]
        hot_all = hot_all + lax.ppermute(hot_all, "shard", perm)
        step_bit *= 2
    hot_all = to_all(hot_all)
    hot_out, hot_accum_out = hot_update(
        dp_at, hot_table, hot_accum.reshape(N_DP, -1), hot_all
    )

    first = owner_first(wanted, owned[0], row_count)
    parts = owner_second(dp_at, wanted, hits, owned[1], first)
    parts = to_owners(parts)
    packed = cold_update(dp_at, own_table, cold_accum.reshape(-1, 128), own_bits, parts)
    parts = to_all(packed)
    cold_out, cold_accum_out = cold_join(dp_at, parts)
    return (cold_out, cold_accum_out.reshape(-1), hot_out, hot_accum_out.reshape(-1))


def solution(mesh):
    return jax.shard_map(
        step,
        mesh=mesh,
        in_specs=(
            P("shard", None),
            P("shard"),
            P("shard", None),
            P(),
            P(),
            P(),
            P(),
            P(),
            P(),
            P(("shard", "dp")),
            P(("shard", "dp"), None),
            P(("shard", "dp"), None),
            P(("shard", "dp"), None),
            P(("shard", "dp"), None),
        ),
        out_specs=(P("shard", None), P("shard"), P(), P()),
        check_vma=False,
    )
```

```python
import jax
import jax.numpy as jnp
from jax import lax
from jax.experimental import pallas as pl
from jax.experimental.pallas import tpu as pltpu
from jax.sharding import PartitionSpec as P


MB = 2
GROUP = 16
FEATS = 16
F_COLD = 8
BF = jnp.bfloat16
F32 = jnp.float32
NT = (((1,), (1,)), ((), ()))
HBM = pl.BlockSpec(memory_space=pltpu.HBM)
VMEM = pl.BlockSpec(memory_space=pltpu.VMEM)
SMEM = pl.BlockSpec(memory_space=pltpu.SMEM)
N_DP = 8
N_X = 4
VMEM_LIMIT = 64 << 20
learn_rate = 0.3
UNROLL = 4


def iota(shape, axis):
    return lax.broadcasted_iota(jnp.int32, shape, axis)


def as_one(same):
    return jnp.where(same, jnp.ones(same.shape, BF), jnp.zeros(same.shape, BF))


def mine_of(at, k, flip):
    return (((at >> 1) + k) & (N_X - 1)) * 2 + ((at & 1) ^ flip)


def chunk_of(at, i):
    x = ((at >> 1) - (i & 3)) & 3
    return x * 2 + ((at & 1) ^ (i >> 2))


def params():
    return pltpu.CompilerParams(vmem_limit_bytes=VMEM_LIMIT)


def small_params():
    return pltpu.CompilerParams(vmem_limit_bytes=20 << 20)


def load_all(pairs, sems):
    copies = [pltpu.make_async_copy(s, d, sems.at[i]) for i, (s, d) in enumerate(pairs)]
    for c in copies:
        c.start()
    return copies


def match_rows(ids, match, at, count):
    lanes = iota((GROUP, count), 1).astype(jnp.int16)
    for f in range(F_COLD):
        mine = jnp.broadcast_to(ids[:, f : f + 1], (GROUP, 128)).astype(jnp.int16)
        same = lanes == jnp.concatenate([mine] * (count // 128), axis=1)
        match[pl.ds(at + f * GROUP, GROUP), :count] = as_one(same)


def hot_rows_kernel(hot_ids, table, later, out, ids, src, match, res, sems):
    copies = load_all([(hot_ids, ids), (table, src)], sems)
    for c in copies:
        c.wait()
    source = src[...].astype(BF)
    half = F_COLD * GROUP
    block = 4
    steps = ids.shape[0] // GROUP // block

    def body(b, carry):
        for q in range(block):
            part = pl.ds(pl.multiple_of((b * block + q) * GROUP, GROUP), GROUP)
            match_rows(ids[part, :], match, q * half, source.shape[0])
        rows = pl.ds(pl.multiple_of(b * block * half, block * half), block * half)
        res[rows, :] = jnp.dot(match[...], source, preferred_element_type=F32).astype(BF)
        return carry

    lax.fori_loop(0, steps, body, 0)
    done = pltpu.make_async_copy(res, out, sems.at[2])
    done.start()
    done.wait()


def hot_rows(hot_ids, table, later):
    count, width = table.shape
    rows = hot_ids.shape[0] * F_COLD
    return pl.pallas_call(
        hot_rows_kernel,
        in_specs=[HBM] * 3,
        out_specs=HBM,
        out_shape=jax.ShapeDtypeStruct((rows, width), BF),
        scratch_shapes=[
            pltpu.VMEM(hot_ids.shape, jnp.int32),
            pltpu.VMEM(table.shape, F32),
            pltpu.VMEM((512, count), BF),
            pltpu.VMEM((rows, width), BF),
            pltpu.SemaphoreType.DMA((3,)),
        ],
        compiler_params=params(),
        name="hot_rows",
    )(hot_ids, table, later)


def step_kernel(m, *refs):
    (
        fetched_h, xh_h, slots_h, slots_t_h, targets_h, flat_h, inter_h, bias_h, w_out_h,
        slot_grad, hot_hi, hot_lo,
        fetched, x, slots, slots_t, targets, w_flat, w_inter, bias, w_out,
        a, pairs, back, mirror, g_hi, g_lo, h_hi, h_lo, match, slopes, sems,
    ) = refs
    width = fetched.shape[1]
    samples = targets.shape[1]
    groups = samples // GROUP
    lane_group = FEATS * GROUP
    half = F_COLD * GROUP
    scale = width ** (-0.5)
    block = 4
    first = m * samples

    head = load_all(
        [
            (slots_h.at[pl.ds(first, samples), :], slots),
            (fetched_h, fetched),
        ],
        sems,
    )
    hot_copies = [
        pltpu.make_async_copy(
            xh_h.at[pl.ds((m * groups + g) * half, half), :],
            x.at[pl.ds(g * lane_group + half, half), :],
            sems.at[2],
        )
        for g in range(groups)
    ]
    for c in hot_copies:
        c.start()
    tail = load_all(
        [
            (flat_h, w_flat),
            (inter_h, w_inter),
            (bias_h, bias),
            (w_out_h, w_out),
            (targets_h.at[:, pl.ds(first, samples)], targets),
            (slots_t_h.at[:, pl.ds(first, samples)], slots_t),
        ],
        sems.at[pl.ds(3, 6)],
    )

    sq = (lane_group, lane_group)
    i_hi = iota(sq, 0) >> 4
    i_lo = iota(sq, 0) & 15
    j_hi = iota(sq, 1) >> 4
    j_lo = iota(sq, 1) & 15
    spread = jnp.where(i_hi == j_lo, 1.0, 0.0).astype(BF)
    spread_t = jnp.where(i_lo == j_hi, 1.0, 0.0).astype(BF)
    swap = jnp.where((i_hi == j_lo) & (i_lo == j_hi), 1.0, 0.0).astype(BF)

    for c in head:
        c.wait()

    def gather(b, carry):
        for q in range(block):
            part = pl.ds(pl.multiple_of((b * block + q) * GROUP, GROUP), GROUP)
            match_rows(slots[part, :], match, q * half, fetched.shape[0])
        picked = jnp.dot(match[...], fetched[...], preferred_element_type=F32).astype(BF)
        for q in range(block):
            dst = pl.multiple_of((b * block + q) * lane_group, lane_group)
            x[pl.ds(dst, half), :] = picked[q * half : (q + 1) * half]
        return carry

    lax.fori_loop(0, groups // block, gather, 0)
    for c in hot_copies:
        c.wait()

    def dots(i, carry):
        for u in range(UNROLL):
            g = i * UNROLL + u
            rows = pl.ds(pl.multiple_of(g * lane_group, lane_group), lane_group)
            part = pl.ds(pl.multiple_of(g * GROUP, GROUP), GROUP)
            xg = x[rows, :]
            for f in range(FEATS):
                a[part, f * width : (f + 1) * width] = xg[f * GROUP : (f + 1) * GROUP]
            gram = lax.dot_general(xg, xg, NT, preferred_element_type=F32) * scale
            own = jnp.where(i_lo == j_lo, gram, 0.0).astype(BF)
            wide = jnp.dot(own, spread, preferred_element_type=F32)
            wide = jnp.where(i_hi == j_hi, wide, 0.0)
            pairs[part, :] = jnp.sum(
                wide.reshape(FEATS, GROUP, lane_group), axis=0
            ).astype(BF)
        return carry

    lax.fori_loop(0, groups // UNROLL, dots, 0)
    for c in tail:
        c.wait()

    pre = jnp.dot(a[...], w_flat[...], preferred_element_type=F32)
    pre = pre + jnp.dot(pairs[...], w_inter[...], preferred_element_type=F32)
    pre = pre + bias[...]
    gated = jax.nn.sigmoid(pre)
    logits = jnp.sum(pre * gated * w_out[...], axis=-1, keepdims=True)
    eye = iota((samples, samples), 0) == iota((samples, samples), 1)
    target = jnp.sum(jnp.where(eye, targets[...], 0.0), axis=1, keepdims=True)
    residual = jax.nn.sigmoid(logits) - target
    slopes[...] = (residual * w_out[...] * gated * (1.0 + pre * (1.0 - gated))).astype(BF)

    inter_t = jnp.dot(swap, w_inter[...], preferred_element_type=F32).astype(BF)
    both = lax.dot_general(slopes[...], w_inter[...], NT, preferred_element_type=F32)
    both = both + lax.dot_general(slopes[...], inter_t, NT, preferred_element_type=F32)
    mirror[...] = (both * scale).astype(BF)

    def flat_back(f, carry):
        rows = pl.ds(pl.multiple_of(f * width, width), width)
        back[f] = lax.dot_general(
            slopes[...], w_flat[rows, :], NT, preferred_element_type=F32
        )
        return carry

    lax.fori_loop(0, FEATS, flat_back, 0)

    def grads(i, carry):
        for u in range(UNROLL):
            g = i * UNROLL + u
            rows = pl.ds(pl.multiple_of(g * lane_group, lane_group), lane_group)
            part = pl.ds(pl.multiple_of(g * GROUP, GROUP), GROUP)
            mine = mirror[part, :].astype(F32)
            tall = jnp.broadcast_to(mine[None], (FEATS, GROUP, lane_group)).reshape(sq)
            tall = jnp.where(i_hi == j_hi, tall, 0.0).astype(BF)
            wide = jnp.dot(tall, spread_t, preferred_element_type=F32)
            wide = jnp.where(i_lo == j_lo, wide, 0.0).astype(BF)
            total = jnp.dot(wide, x[rows, :], preferred_element_type=F32)
            total = total + back[:, part, :].reshape(lane_group, width)
            hi = total.astype(BF)
            lo = (total - hi.astype(F32)).astype(BF)
            for f in range(F_COLD):
                dst = pl.ds(pl.multiple_of(f * samples + g * GROUP, GROUP), GROUP)
                at = f * GROUP
                g_hi[dst, :] = hi[at : at + GROUP]
                g_lo[dst, :] = lo[at : at + GROUP]
                h_hi[dst, :] = hi[half + at : half + at + GROUP]
                h_lo[dst, :] = lo[half + at : half + at + GROUP]
        return carry

    lax.fori_loop(0, groups // UNROLL, grads, 0)
    outs = load_all([(h_hi, hot_hi), (h_lo, hot_lo)], sems.at[pl.ds(0, 2)])

    rows_blk = 512

    def scatter(b, carry):
        at = pl.multiple_of(b * rows_blk, rows_blk)
        subs = iota((rows_blk, samples), 0).astype(jnp.int16)
        for f in range(F_COLD):
            mine = jnp.broadcast_to(slots_t[f : f + 1, :] - at, (16, samples)).astype(jnp.int16)
            same = subs == jnp.concatenate([mine] * (rows_blk // 16), axis=0)
            match[:, f * samples : (f + 1) * samples] = as_one(same)
        total = jnp.dot(match[...], g_hi[...], preferred_element_type=F32)
        total = total + jnp.dot(match[...], g_lo[...], preferred_element_type=F32)
        fetched[pl.ds(at, rows_blk), :] = total.astype(BF)
        pltpu.make_async_copy(
            fetched.at[pl.ds(at, rows_blk), :], slot_grad.at[pl.ds(at, rows_blk), :], sems.at[3 + b]
        ).start()
        return carry

    n_out = slot_grad.shape[0] // rows_blk
    lax.fori_loop(0, n_out, scatter, 0)
    for b in range(n_out):
        pltpu.make_async_copy(
            fetched.at[pl.ds(b * rows_blk, rows_blk), :],
            slot_grad.at[pl.ds(b * rows_blk, rows_blk), :],
            sems.at[3 + b],
        ).wait()
    for c in outs:
        c.wait()


def backprop(m, fetched, xh, slots, slots_t, targets, w_flat, w_inter, bias, w_out):
    count, width = fetched.shape
    samples = slots.shape[0] // MB
    hidden = w_flat.shape[1]
    lookups = samples * F_COLD
    wide = FEATS * width
    rows = jax.ShapeDtypeStruct((lookups, width), BF)
    return pl.pallas_call(
        lambda *refs: step_kernel(m, *refs),
        in_specs=[HBM] * 9,
        out_specs=(HBM,) * 3,
        out_shape=(jax.ShapeDtypeStruct((count, width), BF), rows, rows),
        scratch_shapes=[
            pltpu.VMEM((count, width), BF),
            pltpu.VMEM((samples * FEATS, width), BF),
            pltpu.VMEM((samples, F_COLD), jnp.int32),
            pltpu.VMEM((F_COLD, samples), jnp.int32),
            pltpu.VMEM((1, samples), F32),
            pltpu.VMEM(w_flat.shape, BF),
            pltpu.VMEM(w_inter.shape, BF),
            pltpu.VMEM((1, hidden), F32),
            pltpu.VMEM((1, hidden), F32),
            pltpu.VMEM((samples, wide), BF),
            pltpu.VMEM((samples, FEATS * FEATS), BF),
            pltpu.VMEM((FEATS, samples, width), F32),
            pltpu.VMEM((samples, FEATS * FEATS), BF),
            pltpu.VMEM((lookups, width), BF),
            pltpu.VMEM((lookups, width), BF),
            pltpu.VMEM((lookups, width), BF),
            pltpu.VMEM((lookups, width), BF),
            pltpu.VMEM((512, 2048), BF),
            pltpu.VMEM((samples, hidden), BF),
            pltpu.SemaphoreType.DMA((9,)),
        ],
        compiler_params=params(),
        name="train_step",
    )(fetched, xh, slots, slots_t, targets, w_flat, w_inter, bias, w_out)


def hot_scatter_kernel(at_ref, ids_h, hi0, lo0, hi1, lo1, *refs):
    outs = refs[:N_X]
    other, ids, h0, l0, h1, l1, match, res, sems = refs[N_X:]
    copies = load_all([(ids_h, ids), (hi0, h0), (lo0, l0), (hi1, h1), (lo1, l1)], sems)
    samples = ids.shape[1] // MB
    block = match.shape[1]
    size = res.shape[0] // N_DP
    subs = iota((block, samples), 0).astype(jnp.int16)
    for c in copies:
        c.wait()

    def body(b, carry):
        at = pl.multiple_of(b * block, block)
        total = None
        for m, parts in enumerate(((h0, l0), (h1, l1))):
            for f in range(F_COLD):
                row = ids[f : f + 1, m * samples : (m + 1) * samples] - at
                mine = jnp.broadcast_to(row, (16, samples)).astype(jnp.int16)
                same = subs == jnp.concatenate([mine] * (block // 16), axis=0)
                match[m, :, f * samples : (f + 1) * samples] = as_one(same)
            for part in parts:
                term = jnp.dot(match[m], part[...], preferred_element_type=F32)
                total = term if total is None else total + term
        res[pl.ds(at, block), :] = total
        return carry

    lax.fori_loop(0, res.shape[0] // block, body, 0)
    done = []
    for k in range(N_X):
        for flip, dst in ((0, outs[k]), (1, other.at[k])):
            chunk = mine_of(at_ref[0], k, flip)
            src = res.at[pl.ds(pl.multiple_of(chunk * size, size), size), :]
            done.append(pltpu.make_async_copy(src, dst, sems.at[2 * k + flip]))
            done[-1].start()
    for c in done:
        c.wait()


def hot_scatter(dp_at, ids, hi0, lo0, hi1, lo1, count):
    rows, width = hi0.shape
    return pl.pallas_call(
        hot_scatter_kernel,
        in_specs=[SMEM] + [HBM] * 5,
        out_specs=(HBM,) * (N_X + 1),
        out_shape=(jax.ShapeDtypeStruct((count // N_DP, width), F32),) * N_X
        + (jax.ShapeDtypeStruct((N_X, count // N_DP, width), F32),),
        scratch_shapes=[pltpu.VMEM(ids.shape, jnp.int32)]
        + [pltpu.VMEM((rows, width), BF)] * 4
        + [
            pltpu.VMEM((MB, 256, rows), BF),
            pltpu.VMEM((count, width), F32),
            pltpu.SemaphoreType.DMA((5 + N_DP,)),
        ],
        compiler_params=params(),
        name="hot_scatter",
    )(dp_at, ids, hi0, lo0, hi1, lo1)


def serve_kernel(m, with_hits, wanted, table_h, rows, *refs):
    if with_hits:
        hits, table, match, res, count_acc, sems = refs
    else:
        table, match, res, sems = refs
    load = pltpu.make_async_copy(table_h, table, sems.at[0])
    load.start()
    shards, lanes = wanted.shape
    capacity = lanes // MB
    count = table.shape[0]
    per = 8
    block = per * capacity
    ids = jnp.concatenate([wanted[...], jnp.zeros((lanes - shards, lanes), jnp.int32)], axis=0)
    turned = ids.T
    names = iota((capacity, count), 1).astype(jnp.int16)
    if with_hits:
        count_acc[...] = jnp.zeros_like(count_acc)

    def ones_of(part, mb, j):
        col = part[mb * capacity : (mb + 1) * capacity, j : j + 1]
        mine = jnp.broadcast_to(col, (capacity, 128)).astype(jnp.int16)
        return as_one(names == jnp.concatenate([mine] * (count // 128), axis=1))

    def add_hits(one):
        tall = one[0:16] + one[16:32] + one[32:48] + one[48:64]
        count_acc[...] += tall

    def body(b, carry):
        part = pltpu.roll(turned, lanes - b * per, 1)
        for j in range(per):
            one = ones_of(part, m, j)
            match[j * capacity : (j + 1) * capacity, :] = one
            if with_hits:
                add_hits(one)
                for other in range(MB):
                    if other != m:
                        add_hits(ones_of(part, other, j))
        at = pl.ds(pl.multiple_of(b * block, block), block)
        res[at, :] = jnp.dot(match[...], table[...], preferred_element_type=F32).astype(BF)
        pltpu.make_async_copy(res.at[at, :], rows.at[at, :], sems.at[1 + b]).start()
        return carry

    steps = shards // per
    load.wait()
    lax.fori_loop(0, steps, body, 0)
    if with_hits:
        total = jnp.sum(count_acc[...].astype(F32), axis=0, keepdims=True)
        size = count // N_DP
        for p in range(N_DP):
            hits[p : p + 1, :] = total[:, p * size : (p + 1) * size]
    for b in range(steps):
        at = pl.ds(b * block, block)
        pltpu.make_async_copy(res.at[at, :], rows.at[at, :], sems.at[1 + b]).wait()


def serve(m, with_hits, wanted, table):
    shards, lanes = wanted.shape
    capacity = lanes // MB
    slots = shards * capacity
    count, width = table.shape
    rows = jax.ShapeDtypeStruct((slots, width), BF)
    extra = [pltpu.VMEM((16, count), BF)] if with_hits else []
    return pl.pallas_call(
        lambda *refs: serve_kernel(m, with_hits, *refs),
        in_specs=[VMEM, HBM],
        out_specs=(HBM, VMEM) if with_hits else HBM,
        out_shape=(rows, jax.ShapeDtypeStruct((N_DP, count // N_DP), F32))
        if with_hits
        else rows,
        scratch_shapes=[
            pltpu.VMEM(table.shape, BF),
            pltpu.VMEM((512, count), BF),
            pltpu.VMEM((slots, width), BF),
        ]
        + extra
        + [pltpu.SemaphoreType.DMA((1 + shards // 8,))],
        compiler_params=params(),
        name="serve_rows",
    )(wanted, table)


def id_tiles(wanted, m):
    ids = wanted[...]
    other = pltpu.roll(ids, 64, 1)
    left, right = (ids, other) if m == 0 else (other, ids)
    low = iota((1, 128), 1) < 64
    return [
        jnp.where(low, left[2 * i : 2 * i + 1], right[2 * i + 1 : 2 * i + 2])
        for i in range(ids.shape[0] // 2)
    ]


def owner_match(tiles, base, match, subs):
    size = match.shape[0]
    for i, tile in enumerate(tiles):
        mine = jnp.broadcast_to(tile - base, (16, 128)).astype(jnp.int16)
        same = subs == jnp.concatenate([mine] * (size // 16), axis=0)
        match[:, i * 128 : (i + 1) * 128] = as_one(same)


def owner_kernel(flip, at_ref, wanted, hits, *refs):
    grads_h = refs[:MB]
    outs = refs[MB : -4]
    grads, match, res, sems = refs[-4:]
    size = match.shape[1]
    copies = load_all([(grads_h[m], grads.at[m]) for m in range(MB)], sems)
    tiles = [id_tiles(wanted, m) for m in range(MB)]
    subs = iota((size, 128), 0).astype(jnp.int16)
    for c in copies:
        c.wait()

    def body(k, carry):
        chunk = mine_of(at_ref[0], k, flip)
        at = pl.multiple_of(chunk * size, size)
        total = None
        for m in range(MB):
            owner_match(tiles[m], at, match.at[m], subs)
            term = jnp.dot(match[m], grads[m], preferred_element_type=F32)
            total = term if total is None else total + term
        res[k, :size, :] = total.astype(BF)
        mine = hits[pl.ds(chunk, 1), :]
        res[k, size:, :] = jnp.broadcast_to(mine, (16, size)).astype(BF)
        return carry

    lax.fori_loop(0, N_X, body, 0)
    if flip:
        done = load_all([(res, outs[0])], sems)
    else:
        done = load_all([(res.at[k], outs[k]) for k in range(N_X)], sems)
    for c in done:
        c.wait()


def owner(flip, dp_at, wanted, hits, grads):
    slots, width = grads[0].shape
    size = hits.shape[1]
    part = (size + 16, width)
    whole = (jax.ShapeDtypeStruct((N_X,) + part, BF),)
    each = (jax.ShapeDtypeStruct(part, BF),) * N_X
    return pl.pallas_call(
        lambda *refs: owner_kernel(flip, *refs),
        in_specs=[SMEM, VMEM, VMEM] + [HBM] * MB,
        out_specs=(HBM,) * (1 if flip else N_X),
        out_shape=whole if flip else each,
        scratch_shapes=[
            pltpu.VMEM((MB, slots, width), BF),
            pltpu.VMEM((MB, size, slots), BF),
            pltpu.VMEM((N_X,) + part, BF),
            pltpu.SemaphoreType.DMA((MB + N_X,)),
        ],
        compiler_params=params(),
        name="owner_other" if flip else "owner_mine",
    )(dp_at, wanted, hits, *grads)


def to_col(row, eye):
    return jnp.sum(jnp.where(eye, row, 0.0), axis=1, keepdims=True)


def to_row(col, eye):
    return jnp.sum(jnp.where(eye, col, 0.0), axis=0, keepdims=True)


def adagrad(table, accum, grad):
    accum_new = accum + jnp.mean(grad * grad, axis=-1, keepdims=True)
    return table - learn_rate * grad / jnp.sqrt(accum_new), accum_new


def pick_kernel(at_ref, table_h, bits_h, table_out, bits_out, table, bits, sems):
    size = table.shape[0]
    rows = pl.ds(pl.multiple_of(at_ref[0] * size, size), size)
    for pairs in (
        [(table_h.at[rows, :], table), (bits_h.at[rows, :], bits)],
        [(table, table_out), (bits, bits_out)],
    ):
        for c in load_all(pairs, sems):
            c.wait()


def pick(dp_at, table, bits):
    shape = (table.shape[0] // N_DP, table.shape[1])
    return pl.pallas_call(
        pick_kernel,
        in_specs=[SMEM, HBM, HBM],
        out_specs=(HBM, HBM),
        out_shape=(
            jax.ShapeDtypeStruct(shape, table.dtype),
            jax.ShapeDtypeStruct(shape, bits.dtype),
        ),
        scratch_shapes=[
            pltpu.VMEM(shape, table.dtype),
            pltpu.VMEM(shape, bits.dtype),
            pltpu.SemaphoreType.DMA((2,)),
        ],
        compiler_params=params(),
        name="pick_rows",
    )(dp_at, table, bits)


def cold_update_kernel(at_ref, *refs):
    ins = refs[: 3 + N_X]
    out = refs[3 + N_X]
    table, accum, bits, parts, res, sems = refs[4 + N_X :]
    size = table.shape[0]
    spots = [table, accum, bits] + [parts.at[k] for k in range(N_X)]
    copies = load_all(list(zip(ins, spots)), sems)
    eye = iota((size, size), 0) == iota((size, size), 1)
    for c in copies:
        c.wait()
    total = parts[0].astype(F32)
    for k in range(1, N_X):
        total = total + parts[k].astype(F32)
    touched = to_col(total[size : size + 1], eye)
    averaged = total[:size] / jnp.maximum(touched, 1.0)
    at = at_ref[0] * 2
    old = jnp.concatenate([accum[pl.ds(at, 1), :], accum[pl.ds(at + 1, 1), :]], axis=1)
    old = to_col(old, eye)
    updated, accum_new = adagrad(table[...].astype(F32), old, averaged)
    grid_step = jnp.max(jnp.abs(updated), axis=-1, keepdims=True) / 8.0
    dither = bits[...].astype(F32) * (1.0 / 65280.0) - 0.5
    res[:size, :] = jnp.where(touched > 0.5, updated + grid_step * dither, updated).astype(BF)
    row = to_row(accum_new, eye)
    high = row.astype(BF).astype(F32)
    middle = (row - high).astype(BF).astype(F32)
    low = (row - high) - middle
    which = iota((16, size), 0)
    packed = jnp.where(which == 0, high, jnp.where(which == 1, middle, low))
    res[size:, :] = packed.astype(BF)
    done = pltpu.make_async_copy(res, out, sems.at[0])
    done.start()
    done.wait()


def cold_update(dp_at, table, accum, bits, parts):
    shape = parts[0].shape
    return pl.pallas_call(
        cold_update_kernel,
        in_specs=[SMEM] + [HBM] * (3 + N_X),
        out_specs=HBM,
        out_shape=jax.ShapeDtypeStruct(shape, BF),
        scratch_shapes=[
            pltpu.VMEM(table.shape, BF),
            pltpu.VMEM(accum.shape, F32),
            pltpu.VMEM(bits.shape, jnp.int32),
            pltpu.VMEM((N_X,) + shape, BF),
            pltpu.VMEM(shape, BF),
            pltpu.SemaphoreType.DMA((3 + N_X,)),
        ],
        compiler_params=params(),
        name="cold_update",
    )(dp_at, table, accum, bits, *parts)


def cold_join_kernel(at_ref, *refs):
    parts = refs[:N_DP]
    out, accum_out, sems = refs[N_DP:]
    size = out.shape[0] // N_DP
    done = []
    for i in range(N_DP):
        chunk = chunk_of(at_ref[0], i)
        dst = out.at[pl.ds(pl.multiple_of(chunk * size, size), size), :]
        done.append(pltpu.make_async_copy(parts[i].at[pl.ds(0, size), :], dst, sems.at[i]))
        done[i].start()
    for i in range(N_DP):
        chunk = chunk_of(at_ref[0], i)
        rows = parts[i][size:, :].astype(F32)
        row = (rows[2:3] + rows[1:2]) + rows[0:1]
        accum_out[pl.ds(chunk * 2, 1), :] = row[:, :128]
        accum_out[pl.ds(chunk * 2 + 1, 1), :] = row[:, 128:]
    for c in done:
        c.wait()


def cold_join(dp_at, parts):
    width = parts[0].shape[1]
    size = parts[0].shape[0] - 16
    return pl.pallas_call(
        cold_join_kernel,
        in_specs=[SMEM] + [VMEM] * N_DP,
        out_specs=(HBM, VMEM),
        out_shape=(
            jax.ShapeDtypeStruct((N_DP * size, width), BF),
            jax.ShapeDtypeStruct((N_DP * size // 128, 128), F32),
        ),
        scratch_shapes=[pltpu.SemaphoreType.DMA((N_DP,))],
        compiler_params=small_params(),
        name="cold_join",
    )(dp_at, *parts)


def pair_sum_kernel(*refs):
    mine_h = refs[:N_X]
    other_h = refs[N_X]
    outs = refs[N_X + 1 : 2 * N_X + 1]
    mine, other, sems = refs[2 * N_X + 1 :]
    copies = load_all([(mine_h[k], mine.at[k]) for k in range(N_X)] + [(other_h, other)], sems)
    for c in copies:
        c.wait()
    mine[...] = (mine[...].astype(F32) + other[...].astype(F32)).astype(mine.dtype)
    done = load_all([(mine.at[k], outs[k]) for k in range(N_X)], sems)
    for c in done:
        c.wait()


def pair_sum(mine, other):
    outs = tuple(jax.ShapeDtypeStruct(part.shape, part.dtype) for part in mine)
    return pl.pallas_call(
        pair_sum_kernel,
        in_specs=[HBM] * (N_X + 1),
        out_specs=(HBM,) * N_X,
        out_shape=outs,
        scratch_shapes=[
            pltpu.VMEM(other.shape, other.dtype),
            pltpu.VMEM(other.shape, other.dtype),
            pltpu.SemaphoreType.DMA((N_X + 1,)),
        ],
        compiler_params=params(),
        name="pair_sum",
    )(*mine, other)


def sum_parts_kernel(*refs):
    parts_h = refs[:N_X]
    out, parts, res, sems = refs[N_X:]
    copies = load_all([(parts_h[k], parts.at[k]) for k in range(N_X)], sems)
    for c in copies:
        c.wait()
    res[...] = (parts[0] + parts[1]) + (parts[2] + parts[3])
    done = pltpu.make_async_copy(res, out, sems.at[0])
    done.start()
    done.wait()


def sum_parts(parts):
    shape = parts[0].shape
    return pl.pallas_call(
        sum_parts_kernel,
        in_specs=[HBM] * N_X,
        out_specs=HBM,
        out_shape=jax.ShapeDtypeStruct(shape, F32),
        scratch_shapes=[
            pltpu.VMEM((N_X,) + shape, F32),
            pltpu.VMEM(shape, F32),
            pltpu.SemaphoreType.DMA((N_X,)),
        ],
        compiler_params=params(),
        name="sum_parts",
    )(*parts)


def hot_update_kernel(at_ref, table_h, accum_h, *refs):
    grads = refs[:N_DP]
    out, accum_out, table, accum, res, sems = refs[N_DP:]
    size = grads[0].shape[0]
    copies = load_all([(table_h, table), (accum_h, accum)], sems)
    eye = iota((size, size), 0) == iota((size, size), 1)
    for c in copies:
        c.wait()
    done = []
    for k in range(N_DP):
        chunk = chunk_of(at_ref[0], k)
        rows = pl.ds(pl.multiple_of(chunk * size, size), size)
        old = to_col(accum[pl.ds(chunk, 1), :], eye)
        updated, accum_new = adagrad(table[rows, :], old, grads[k][...])
        res[rows, :] = updated
        accum_out[pl.ds(chunk, 1), :] = to_row(accum_new, eye)
        done.append(pltpu.make_async_copy(res.at[rows, :], out.at[rows, :], sems.at[2 + k]))
        done[k].start()
    for c in done:
        c.wait()


def hot_update(dp_at, table, accum, grads):
    count, width = table.shape
    size = count // N_DP
    return pl.pallas_call(
        hot_update_kernel,
        in_specs=[SMEM] + [HBM] * 2 + [VMEM] * N_DP,
        out_specs=(HBM, VMEM),
        out_shape=(
            jax.ShapeDtypeStruct((count, width), F32),
            jax.ShapeDtypeStruct((N_DP, size), F32),
        ),
        scratch_shapes=[
            pltpu.VMEM((count, width), F32),
            pltpu.VMEM((N_DP, size), F32),
            pltpu.VMEM((count, width), F32),
            pltpu.SemaphoreType.DMA((2 + N_DP,)),
        ],
        compiler_params=small_params(),
        name="hot_update",
    )(dp_at, table, accum, *grads)


def exchange(value, axis):
    return lax.all_to_all(value, axis, split_axis=0, concat_axis=0, tiled=True)


def along_x(value, k):
    perm = [(i, ((i // 2 + k) % N_X) * 2 + i % 2) for i in range(N_DP)]
    return lax.ppermute(value, "dp", perm)


def to_partner(value):
    return lax.ppermute(value, "dp", [(i, i ^ 1) for i in range(N_DP)])


def to_owners(parts):
    *mine, other = parts
    other = to_partner(other)
    mine = pair_sum(mine, other)
    return [mine[0]] + [along_x(mine[k], k) for k in range(1, N_X)]


def to_all(part):
    along = [part] + [along_x(part, k) for k in range(1, N_X)]
    return along + [to_partner(value) for value in along]


def step(
    cold_table,
    cold_accum,
    dither_bits,
    hot_table,
    hot_accum,
    w_flat,
    w_inter,
    hidden_bias,
    w_out,
    targets,
    hot_ids,
    cold_slots,
    requests,
    counts,
):
    shards = lax.axis_size("shard")
    capacity = requests.shape[1]
    _, row_width = cold_table.shape
    hot_count = hot_table.shape[0]
    slots = shards * capacity
    dp_at = lax.axis_index("dp").astype(jnp.int32).reshape(1)

    live = jnp.arange(capacity, dtype=jnp.int32) < counts[:, :, None]
    asked = jnp.where(live, requests.reshape(MB, shards, capacity), -1)
    asked = asked.transpose(1, 0, 2).reshape(shards, MB * capacity)
    wanted = exchange(asked, "shard")

    fetched = []
    for m in range(MB):
        rows = serve(m, m == 1, wanted, cold_table)
        if m == 1:
            rows, hits = rows
        rows = exchange(rows.reshape(shards, capacity, row_width), "shard")
        fetched.append(rows.reshape(slots, row_width))
    own_table, own_bits = pick(dp_at, cold_table, dither_bits)
    xh = hot_rows(hot_ids, hot_table, cold_slots)

    owned = []
    hot_parts = []
    for m in range(MB):
        slot_grad, *hot_part = backprop(
            m,
            fetched[m],
            xh,
            cold_slots,
            cold_slots.T,
            targets.reshape(1, -1),
            w_flat,
            w_inter,
            hidden_bias.reshape(1, -1),
            w_out.reshape(1, -1),
        )
        hot_parts += hot_part
        rows = exchange(slot_grad.reshape(shards, capacity, row_width), "shard")
        owned.append(rows.reshape(slots, row_width))

    hot_grads = hot_scatter(dp_at, hot_ids.T, *hot_parts, hot_count)
    hot_grads = to_owners(hot_grads)
    hot_all = sum_parts(hot_grads)
    step_bit = 1
    while step_bit < shards:
        perm = [(i, i ^ step_bit) for i in range(shards)]
        hot_all = hot_all + lax.ppermute(hot_all, "shard", perm)
        step_bit *= 2
    hot_all = to_all(hot_all)
    hot_out, hot_accum_out = hot_update(
        dp_at, hot_table, hot_accum.reshape(N_DP, -1), hot_all
    )

    other = owner(1, dp_at, wanted, hits, owned)
    mine = owner(0, dp_at, wanted, hits, owned)
    parts = to_owners([*mine, *other])
    packed = cold_update(dp_at, own_table, cold_accum.reshape(-1, 128), own_bits, parts)
    parts = to_all(packed)
    cold_out, cold_accum_out = cold_join(dp_at, parts)
    return (cold_out, cold_accum_out.reshape(-1), hot_out, hot_accum_out.reshape(-1))


def solution(mesh):
    return jax.shard_map(
        step,
        mesh=mesh,
        in_specs=(
            P("shard", None),
            P("shard"),
            P("shard", None),
            P(),
            P(),
            P(),
            P(),
            P(),
            P(),
            P(("shard", "dp")),
            P(("shard", "dp"), None),
            P(("shard", "dp"), None),
            P(("shard", "dp"), None),
            P(("shard", "dp"), None),
        ),
        out_specs=(P("shard", None), P("shard"), P(), P()),
        check_vma=False,
    )
```

```python
import jax
import jax.numpy as jnp
from jax import lax
from jax.experimental import pallas as pl
from jax.experimental.pallas import tpu as pltpu
from jax.sharding import PartitionSpec as P


MB = 2
GROUP = 16
FEATS = 16
F_COLD = 8
BF = jnp.bfloat16
F32 = jnp.float32
NT = (((1,), (1,)), ((), ()))
HBM = pl.BlockSpec(memory_space=pltpu.HBM)
VMEM = pl.BlockSpec(memory_space=pltpu.VMEM)
SMEM = pl.BlockSpec(memory_space=pltpu.SMEM)
N_DP = 8
N_X = 4
VMEM_LIMIT = 64 << 20
learn_rate = 0.3
UNROLL = 8


def iota(shape, axis):
    return lax.broadcasted_iota(jnp.int32, shape, axis)


def as_one(same):
    return jnp.where(same, jnp.ones(same.shape, BF), jnp.zeros(same.shape, BF))


def mine_of(at, k, flip):
    return (((at >> 1) + k) & (N_X - 1)) * 2 + ((at & 1) ^ flip)


def chunk_of(at, i):
    x = ((at >> 1) - (i & 3)) & 3
    return x * 2 + ((at & 1) ^ (i >> 2))


def params():
    return pltpu.CompilerParams(vmem_limit_bytes=VMEM_LIMIT)


def small_params():
    return pltpu.CompilerParams(vmem_limit_bytes=20 << 20)


def load_all(pairs, sems):
    copies = [pltpu.make_async_copy(s, d, sems.at[i]) for i, (s, d) in enumerate(pairs)]
    for c in copies:
        c.start()
    return copies


def match_rows(ids, match, at, count):
    lanes = iota((GROUP, count), 1).astype(jnp.int16)
    for f in range(F_COLD):
        mine = jnp.broadcast_to(ids[:, f : f + 1], (GROUP, 128)).astype(jnp.int16)
        same = lanes == jnp.concatenate([mine] * (count // 128), axis=1)
        match[pl.ds(at + f * GROUP, GROUP), :count] = as_one(same)


def hot_rows_kernel(hot_ids, table, later, out, ids, src, match, res, sems):
    copies = load_all([(hot_ids, ids), (table, src)], sems)
    for c in copies:
        c.wait()
    source = src[...].astype(BF)
    half = F_COLD * GROUP
    block = 4
    steps = ids.shape[0] // GROUP // block

    def body(b, carry):
        for q in range(block):
            part = pl.ds(pl.multiple_of((b * block + q) * GROUP, GROUP), GROUP)
            match_rows(ids[part, :], match, q * half, source.shape[0])
        rows = pl.ds(pl.multiple_of(b * block * half, block * half), block * half)
        res[rows, :] = jnp.dot(match[...], source, preferred_element_type=F32).astype(BF)
        return carry

    lax.fori_loop(0, steps, body, 0)
    done = pltpu.make_async_copy(res, out, sems.at[2])
    done.start()
    done.wait()


def hot_rows(hot_ids, table, later):
    count, width = table.shape
    rows = hot_ids.shape[0] * F_COLD
    return pl.pallas_call(
        hot_rows_kernel,
        in_specs=[HBM] * 3,
        out_specs=HBM,
        out_shape=jax.ShapeDtypeStruct((rows, width), BF),
        scratch_shapes=[
            pltpu.VMEM(hot_ids.shape, jnp.int32),
            pltpu.VMEM(table.shape, F32),
            pltpu.VMEM((512, count), BF),
            pltpu.VMEM((rows, width), BF),
            pltpu.SemaphoreType.DMA((3,)),
        ],
        compiler_params=params(),
        name="hot_rows",
    )(hot_ids, table, later)


def step_kernel(m, *refs):
    (
        fetched_h, xh_h, slots_h, slots_t_h, targets_h, flat_h, inter_h, bias_h, w_out_h,
        slot_grad, hot_hi, hot_lo,
        fetched, x, slots, slots_t, targets, w_flat, w_inter, bias, w_out,
        a, pairs, back, mirror, g_hi, g_lo, h_hi, h_lo, match, slopes, sems,
    ) = refs
    width = fetched.shape[1]
    samples = targets.shape[1]
    groups = samples // GROUP
    lane_group = FEATS * GROUP
    half = F_COLD * GROUP
    scale = width ** (-0.5)
    block = 4
    first = m * samples

    head = load_all(
        [
            (slots_h.at[pl.ds(first, samples), :], slots),
            (fetched_h, fetched),
        ],
        sems,
    )
    hot_copies = [
        pltpu.make_async_copy(
            xh_h.at[pl.ds((m * groups + g) * half, half), :],
            x.at[pl.ds(g * lane_group + half, half), :],
            sems.at[2],
        )
        for g in range(groups)
    ]
    for c in hot_copies:
        c.start()
    tail = load_all(
        [
            (flat_h, w_flat),
            (inter_h, w_inter),
            (bias_h, bias),
            (w_out_h, w_out),
            (targets_h.at[:, pl.ds(first, samples)], targets),
            (slots_t_h.at[:, pl.ds(first, samples)], slots_t),
        ],
        sems.at[pl.ds(3, 6)],
    )

    sq = (lane_group, lane_group)
    i_hi = iota(sq, 0) >> 4
    i_lo = iota(sq, 0) & 15
    j_hi = iota(sq, 1) >> 4
    j_lo = iota(sq, 1) & 15
    spread = jnp.where(i_hi == j_lo, 1.0, 0.0).astype(BF)
    spread_t = jnp.where(i_lo == j_hi, 1.0, 0.0).astype(BF)
    swap = jnp.where((i_hi == j_lo) & (i_lo == j_hi), 1.0, 0.0).astype(BF)

    for c in head:
        c.wait()

    def gather(b, carry):
        for q in range(block):
            part = pl.ds(pl.multiple_of((b * block + q) * GROUP, GROUP), GROUP)
            match_rows(slots[part, :], match, q * half, fetched.shape[0])
        picked = jnp.dot(match[...], fetched[...], preferred_element_type=F32).astype(BF)
        for q in range(block):
            dst = pl.multiple_of((b * block + q) * lane_group, lane_group)
            x[pl.ds(dst, half), :] = picked[q * half : (q + 1) * half]
        return carry

    lax.fori_loop(0, groups // block, gather, 0)
    for c in hot_copies:
        c.wait()

    def dots(i, carry):
        for u in range(UNROLL):
            g = i * UNROLL + u
            rows = pl.ds(pl.multiple_of(g * lane_group, lane_group), lane_group)
            part = pl.ds(pl.multiple_of(g * GROUP, GROUP), GROUP)
            xg = x[rows, :]
            for f in range(FEATS):
                a[part, f * width : (f + 1) * width] = xg[f * GROUP : (f + 1) * GROUP]
            gram = lax.dot_general(xg, xg, NT, preferred_element_type=F32) * scale
            own = jnp.where(i_lo == j_lo, gram, 0.0).astype(BF)
            wide = jnp.dot(own, spread, preferred_element_type=F32)
            wide = jnp.where(i_hi == j_hi, wide, 0.0)
            pairs[part, :] = jnp.sum(
                wide.reshape(FEATS, GROUP, lane_group), axis=0
            ).astype(BF)
        return carry

    lax.fori_loop(0, groups // UNROLL, dots, 0)
    for c in tail:
        c.wait()

    pre = jnp.dot(a[...], w_flat[...], preferred_element_type=F32)
    pre = pre + jnp.dot(pairs[...], w_inter[...], preferred_element_type=F32)
    pre = pre + bias[...]
    gated = jax.nn.sigmoid(pre)
    logits = jnp.sum(pre * gated * w_out[...], axis=-1, keepdims=True)
    eye = iota((samples, samples), 0) == iota((samples, samples), 1)
    target = jnp.sum(jnp.where(eye, targets[...], 0.0), axis=1, keepdims=True)
    residual = jax.nn.sigmoid(logits) - target
    slopes[...] = (residual * w_out[...] * gated * (1.0 + pre * (1.0 - gated))).astype(BF)

    inter_t = jnp.dot(swap, w_inter[...], preferred_element_type=F32).astype(BF)
    both = lax.dot_general(slopes[...], w_inter[...], NT, preferred_element_type=F32)
    both = both + lax.dot_general(slopes[...], inter_t, NT, preferred_element_type=F32)
    mirror[...] = (both * scale).astype(BF)

    def flat_back(f, carry):
        rows = pl.ds(pl.multiple_of(f * width, width), width)
        back[f] = lax.dot_general(
            slopes[...], w_flat[rows, :], NT, preferred_element_type=F32
        )
        return carry

    lax.fori_loop(0, FEATS, flat_back, 0)

    def grads(i, carry):
        for u in range(UNROLL):
            g = i * UNROLL + u
            rows = pl.ds(pl.multiple_of(g * lane_group, lane_group), lane_group)
            part = pl.ds(pl.multiple_of(g * GROUP, GROUP), GROUP)
            mine = mirror[part, :].astype(F32)
            tall = jnp.broadcast_to(mine[None], (FEATS, GROUP, lane_group)).reshape(sq)
            tall = jnp.where(i_hi == j_hi, tall, 0.0).astype(BF)
            wide = jnp.dot(tall, spread_t, preferred_element_type=F32)
            wide = jnp.where(i_lo == j_lo, wide, 0.0).astype(BF)
            total = jnp.dot(wide, x[rows, :], preferred_element_type=F32)
            total = total + back[:, part, :].reshape(lane_group, width)
            hi = total.astype(BF)
            lo = (total - hi.astype(F32)).astype(BF)
            for f in range(F_COLD):
                dst = pl.ds(pl.multiple_of(f * samples + g * GROUP, GROUP), GROUP)
                at = f * GROUP
                g_hi[dst, :] = hi[at : at + GROUP]
                g_lo[dst, :] = lo[at : at + GROUP]
                h_hi[dst, :] = hi[half + at : half + at + GROUP]
                h_lo[dst, :] = lo[half + at : half + at + GROUP]
        return carry

    lax.fori_loop(0, groups // UNROLL, grads, 0)
    outs = load_all([(h_hi, hot_hi), (h_lo, hot_lo)], sems.at[pl.ds(0, 2)])

    rows_blk = 512

    def scatter(b, carry):
        at = pl.multiple_of(b * rows_blk, rows_blk)
        subs = iota((rows_blk, samples), 0).astype(jnp.int16)
        for f in range(F_COLD):
            mine = jnp.broadcast_to(slots_t[f : f + 1, :] - at, (16, samples)).astype(jnp.int16)
            same = subs == jnp.concatenate([mine] * (rows_blk // 16), axis=0)
            match[:, f * samples : (f + 1) * samples] = as_one(same)
        total = jnp.dot(match[...], g_hi[...], preferred_element_type=F32)
        total = total + jnp.dot(match[...], g_lo[...], preferred_element_type=F32)
        fetched[pl.ds(at, rows_blk), :] = total.astype(BF)
        pltpu.make_async_copy(
            fetched.at[pl.ds(at, rows_blk), :], slot_grad.at[pl.ds(at, rows_blk), :], sems.at[3 + b]
        ).start()
        return carry

    n_out = slot_grad.shape[0] // rows_blk
    lax.fori_loop(0, n_out, scatter, 0)
    for b in range(n_out):
        pltpu.make_async_copy(
            fetched.at[pl.ds(b * rows_blk, rows_blk), :],
            slot_grad.at[pl.ds(b * rows_blk, rows_blk), :],
            sems.at[3 + b],
        ).wait()
    for c in outs:
        c.wait()


def backprop(m, fetched, xh, slots, slots_t, targets, w_flat, w_inter, bias, w_out):
    count, width = fetched.shape
    samples = slots.shape[0] // MB
    hidden = w_flat.shape[1]
    lookups = samples * F_COLD
    wide = FEATS * width
    rows = jax.ShapeDtypeStruct((lookups, width), BF)
    return pl.pallas_call(
        lambda *refs: step_kernel(m, *refs),
        in_specs=[HBM] * 9,
        out_specs=(HBM,) * 3,
        out_shape=(jax.ShapeDtypeStruct((count, width), BF), rows, rows),
        scratch_shapes=[
            pltpu.VMEM((count, width), BF),
            pltpu.VMEM((samples * FEATS, width), BF),
            pltpu.VMEM((samples, F_COLD), jnp.int32),
            pltpu.VMEM((F_COLD, samples), jnp.int32),
            pltpu.VMEM((1, samples), F32),
            pltpu.VMEM(w_flat.shape, BF),
            pltpu.VMEM(w_inter.shape, BF),
            pltpu.VMEM((1, hidden), F32),
            pltpu.VMEM((1, hidden), F32),
            pltpu.VMEM((samples, wide), BF),
            pltpu.VMEM((samples, FEATS * FEATS), BF),
            pltpu.VMEM((FEATS, samples, width), F32),
            pltpu.VMEM((samples, FEATS * FEATS), BF),
            pltpu.VMEM((lookups, width), BF),
            pltpu.VMEM((lookups, width), BF),
            pltpu.VMEM((lookups, width), BF),
            pltpu.VMEM((lookups, width), BF),
            pltpu.VMEM((512, 2048), BF),
            pltpu.VMEM((samples, hidden), BF),
            pltpu.SemaphoreType.DMA((9,)),
        ],
        compiler_params=params(),
        name="train_step",
    )(fetched, xh, slots, slots_t, targets, w_flat, w_inter, bias, w_out)


def hot_scatter_kernel(at_ref, ids_h, hi0, lo0, hi1, lo1, *refs):
    outs = refs[:N_X]
    other, ids, h0, l0, h1, l1, match, res, sems = refs[N_X:]
    copies = load_all([(ids_h, ids), (hi0, h0), (lo0, l0), (hi1, h1), (lo1, l1)], sems)
    samples = ids.shape[1] // MB
    block = match.shape[1]
    size = res.shape[0] // N_DP
    subs = iota((block, samples), 0).astype(jnp.int16)
    for c in copies:
        c.wait()

    def body(b, carry):
        at = pl.multiple_of(b * block, block)
        total = None
        for m, parts in enumerate(((h0, l0), (h1, l1))):
            for f in range(F_COLD):
                row = ids[f : f + 1, m * samples : (m + 1) * samples] - at
                mine = jnp.broadcast_to(row, (16, samples)).astype(jnp.int16)
                same = subs == jnp.concatenate([mine] * (block // 16), axis=0)
                match[m, :, f * samples : (f + 1) * samples] = as_one(same)
            for part in parts:
                term = jnp.dot(match[m], part[...], preferred_element_type=F32)
                total = term if total is None else total + term
        res[pl.ds(at, block), :] = total
        return carry

    lax.fori_loop(0, res.shape[0] // block, body, 0)
    done = []
    for k in range(N_X):
        for flip, dst in ((0, outs[k]), (1, other.at[k])):
            chunk = mine_of(at_ref[0], k, flip)
            src = res.at[pl.ds(pl.multiple_of(chunk * size, size), size), :]
            done.append(pltpu.make_async_copy(src, dst, sems.at[2 * k + flip]))
            done[-1].start()
    for c in done:
        c.wait()


def hot_scatter(dp_at, ids, hi0, lo0, hi1, lo1, count):
    rows, width = hi0.shape
    return pl.pallas_call(
        hot_scatter_kernel,
        in_specs=[SMEM] + [HBM] * 5,
        out_specs=(HBM,) * (N_X + 1),
        out_shape=(jax.ShapeDtypeStruct((count // N_DP, width), F32),) * N_X
        + (jax.ShapeDtypeStruct((N_X, count // N_DP, width), F32),),
        scratch_shapes=[pltpu.VMEM(ids.shape, jnp.int32)]
        + [pltpu.VMEM((rows, width), BF)] * 4
        + [
            pltpu.VMEM((MB, 256, rows), BF),
            pltpu.VMEM((count, width), F32),
            pltpu.SemaphoreType.DMA((5 + N_DP,)),
        ],
        compiler_params=params(),
        name="hot_scatter",
    )(dp_at, ids, hi0, lo0, hi1, lo1)


def serve_kernel(m, with_hits, wanted, table_h, rows, *refs):
    if with_hits:
        hits, table, match, res, count_acc, sems = refs
    else:
        table, match, res, sems = refs
    load = pltpu.make_async_copy(table_h, table, sems.at[0])
    load.start()
    shards, lanes = wanted.shape
    capacity = lanes // MB
    count = table.shape[0]
    per = 8
    block = per * capacity
    ids = jnp.concatenate([wanted[...], jnp.zeros((lanes - shards, lanes), jnp.int32)], axis=0)
    turned = ids.T
    names = iota((capacity, count), 1).astype(jnp.int16)
    if with_hits:
        count_acc[...] = jnp.zeros_like(count_acc)

    def ones_of(part, mb, j):
        col = part[mb * capacity : (mb + 1) * capacity, j : j + 1]
        mine = jnp.broadcast_to(col, (capacity, 128)).astype(jnp.int16)
        return as_one(names == jnp.concatenate([mine] * (count // 128), axis=1))

    def add_hits(one):
        tall = one[0:16] + one[16:32] + one[32:48] + one[48:64]
        count_acc[...] += tall

    def body(b, carry):
        part = pltpu.roll(turned, lanes - b * per, 1)
        for j in range(per):
            one = ones_of(part, m, j)
            match[j * capacity : (j + 1) * capacity, :] = one
            if with_hits:
                add_hits(one)
                for other in range(MB):
                    if other != m:
                        add_hits(ones_of(part, other, j))
        at = pl.ds(pl.multiple_of(b * block, block), block)
        res[at, :] = jnp.dot(match[...], table[...], preferred_element_type=F32).astype(BF)
        pltpu.make_async_copy(res.at[at, :], rows.at[at, :], sems.at[1 + b]).start()
        return carry

    steps = shards // per
    load.wait()
    lax.fori_loop(0, steps, body, 0)
    if with_hits:
        total = jnp.sum(count_acc[...].astype(F32), axis=0, keepdims=True)
        size = count // N_DP
        for p in range(N_DP):
            hits[p : p + 1, :] = total[:, p * size : (p + 1) * size]
    for b in range(steps):
        at = pl.ds(b * block, block)
        pltpu.make_async_copy(res.at[at, :], rows.at[at, :], sems.at[1 + b]).wait()


def serve(m, with_hits, wanted, table):
    shards, lanes = wanted.shape
    capacity = lanes // MB
    slots = shards * capacity
    count, width = table.shape
    rows = jax.ShapeDtypeStruct((slots, width), BF)
    extra = [pltpu.VMEM((16, count), BF)] if with_hits else []
    return pl.pallas_call(
        lambda *refs: serve_kernel(m, with_hits, *refs),
        in_specs=[VMEM, HBM],
        out_specs=(HBM, VMEM) if with_hits else HBM,
        out_shape=(rows, jax.ShapeDtypeStruct((N_DP, count // N_DP), F32))
        if with_hits
        else rows,
        scratch_shapes=[
            pltpu.VMEM(table.shape, BF),
            pltpu.VMEM((512, count), BF),
            pltpu.VMEM((slots, width), BF),
        ]
        + extra
        + [pltpu.SemaphoreType.DMA((1 + shards // 8,))],
        compiler_params=params(),
        name="serve_rows",
    )(wanted, table)


def id_tiles(wanted, m):
    ids = wanted[...]
    other = pltpu.roll(ids, 64, 1)
    left, right = (ids, other) if m == 0 else (other, ids)
    low = iota((1, 128), 1) < 64
    return [
        jnp.where(low, left[2 * i : 2 * i + 1], right[2 * i + 1 : 2 * i + 2])
        for i in range(ids.shape[0] // 2)
    ]


def owner_match(tiles, base, match, subs):
    size = match.shape[0]
    for i, tile in enumerate(tiles):
        mine = jnp.broadcast_to(tile - base, (16, 128)).astype(jnp.int16)
        same = subs == jnp.concatenate([mine] * (size // 16), axis=0)
        match[:, i * 128 : (i + 1) * 128] = as_one(same)


def owner_kernel(flip, at_ref, wanted, hits, *refs):
    grads_h = refs[:MB]
    outs = refs[MB : -4]
    grads, match, res, sems = refs[-4:]
    size = match.shape[1]
    copies = load_all([(grads_h[m], grads.at[m]) for m in range(MB)], sems)
    tiles = [id_tiles(wanted, m) for m in range(MB)]
    subs = iota((size, 128), 0).astype(jnp.int16)
    for c in copies:
        c.wait()

    def body(k, carry):
        chunk = mine_of(at_ref[0], k, flip)
        at = pl.multiple_of(chunk * size, size)
        total = None
        for m in range(MB):
            owner_match(tiles[m], at, match.at[m], subs)
            term = jnp.dot(match[m], grads[m], preferred_element_type=F32)
            total = term if total is None else total + term
        res[k, :size, :] = total.astype(BF)
        mine = hits[pl.ds(chunk, 1), :]
        res[k, size:, :] = jnp.broadcast_to(mine, (16, size)).astype(BF)
        return carry

    lax.fori_loop(0, N_X, body, 0)
    if flip:
        done = load_all([(res, outs[0])], sems)
    else:
        done = load_all([(res.at[k], outs[k]) for k in range(N_X)], sems)
    for c in done:
        c.wait()


def owner(flip, dp_at, wanted, hits, grads):
    slots, width = grads[0].shape
    size = hits.shape[1]
    part = (size + 16, width)
    whole = (jax.ShapeDtypeStruct((N_X,) + part, BF),)
    each = (jax.ShapeDtypeStruct(part, BF),) * N_X
    return pl.pallas_call(
        lambda *refs: owner_kernel(flip, *refs),
        in_specs=[SMEM, VMEM, VMEM] + [HBM] * MB,
        out_specs=(HBM,) * (1 if flip else N_X),
        out_shape=whole if flip else each,
        scratch_shapes=[
            pltpu.VMEM((MB, slots, width), BF),
            pltpu.VMEM((MB, size, slots), BF),
            pltpu.VMEM((N_X,) + part, BF),
            pltpu.SemaphoreType.DMA((MB + N_X,)),
        ],
        compiler_params=params(),
        name="owner_other" if flip else "owner_mine",
    )(dp_at, wanted, hits, *grads)


def to_col(row, eye):
    return jnp.sum(jnp.where(eye, row, 0.0), axis=1, keepdims=True)


def to_row(col, eye):
    return jnp.sum(jnp.where(eye, col, 0.0), axis=0, keepdims=True)


def adagrad(table, accum, grad):
    accum_new = accum + jnp.mean(grad * grad, axis=-1, keepdims=True)
    return table - learn_rate * grad / jnp.sqrt(accum_new), accum_new


def pick_kernel(at_ref, table_h, bits_h, table_out, bits_out, table, bits, sems):
    size = table.shape[0]
    rows = pl.ds(pl.multiple_of(at_ref[0] * size, size), size)
    for pairs in (
        [(table_h.at[rows, :], table), (bits_h.at[rows, :], bits)],
        [(table, table_out), (bits, bits_out)],
    ):
        for c in load_all(pairs, sems):
            c.wait()


def pick(dp_at, table, bits):
    shape = (table.shape[0] // N_DP, table.shape[1])
    return pl.pallas_call(
        pick_kernel,
        in_specs=[SMEM, HBM, HBM],
        out_specs=(HBM, HBM),
        out_shape=(
            jax.ShapeDtypeStruct(shape, table.dtype),
            jax.ShapeDtypeStruct(shape, bits.dtype),
        ),
        scratch_shapes=[
            pltpu.VMEM(shape, table.dtype),
            pltpu.VMEM(shape, bits.dtype),
            pltpu.SemaphoreType.DMA((2,)),
        ],
        compiler_params=params(),
        name="pick_rows",
    )(dp_at, table, bits)


def cold_update_kernel(at_ref, *refs):
    ins = refs[: 3 + N_X]
    out = refs[3 + N_X]
    table, accum, bits, parts, res, sems = refs[4 + N_X :]
    size = table.shape[0]
    spots = [table, accum, bits] + [parts.at[k] for k in range(N_X)]
    copies = load_all(list(zip(ins, spots)), sems)
    eye = iota((size, size), 0) == iota((size, size), 1)
    for c in copies:
        c.wait()
    total = parts[0].astype(F32)
    for k in range(1, N_X):
        total = total + parts[k].astype(F32)
    touched = to_col(total[size : size + 1], eye)
    averaged = total[:size] / jnp.maximum(touched, 1.0)
    at = at_ref[0] * 2
    old = jnp.concatenate([accum[pl.ds(at, 1), :], accum[pl.ds(at + 1, 1), :]], axis=1)
    old = to_col(old, eye)
    updated, accum_new = adagrad(table[...].astype(F32), old, averaged)
    grid_step = jnp.max(jnp.abs(updated), axis=-1, keepdims=True) / 8.0
    dither = bits[...].astype(F32) * (1.0 / 65280.0) - 0.5
    res[:size, :] = jnp.where(touched > 0.5, updated + grid_step * dither, updated).astype(BF)
    row = to_row(accum_new, eye)
    high = row.astype(BF).astype(F32)
    middle = (row - high).astype(BF).astype(F32)
    low = (row - high) - middle
    which = iota((16, size), 0)
    packed = jnp.where(which == 0, high, jnp.where(which == 1, middle, low))
    res[size:, :] = packed.astype(BF)
    done = pltpu.make_async_copy(res, out, sems.at[0])
    done.start()
    done.wait()


def cold_update(dp_at, table, accum, bits, parts):
    shape = parts[0].shape
    return pl.pallas_call(
        cold_update_kernel,
        in_specs=[SMEM] + [HBM] * (3 + N_X),
        out_specs=HBM,
        out_shape=jax.ShapeDtypeStruct(shape, BF),
        scratch_shapes=[
            pltpu.VMEM(table.shape, BF),
            pltpu.VMEM(accum.shape, F32),
            pltpu.VMEM(bits.shape, jnp.int32),
            pltpu.VMEM((N_X,) + shape, BF),
            pltpu.VMEM(shape, BF),
            pltpu.SemaphoreType.DMA((3 + N_X,)),
        ],
        compiler_params=params(),
        name="cold_update",
    )(dp_at, table, accum, bits, *parts)


def cold_join_kernel(at_ref, *refs):
    parts = refs[:N_DP]
    out, accum_out, sems = refs[N_DP:]
    size = out.shape[0] // N_DP
    done = []
    for i in range(N_DP):
        chunk = chunk_of(at_ref[0], i)
        dst = out.at[pl.ds(pl.multiple_of(chunk * size, size), size), :]
        done.append(pltpu.make_async_copy(parts[i].at[pl.ds(0, size), :], dst, sems.at[i]))
        done[i].start()
    for i in range(N_DP):
        chunk = chunk_of(at_ref[0], i)
        rows = parts[i][size:, :].astype(F32)
        row = (rows[2:3] + rows[1:2]) + rows[0:1]
        accum_out[pl.ds(chunk * 2, 1), :] = row[:, :128]
        accum_out[pl.ds(chunk * 2 + 1, 1), :] = row[:, 128:]
    for c in done:
        c.wait()


def cold_join(dp_at, parts):
    width = parts[0].shape[1]
    size = parts[0].shape[0] - 16
    return pl.pallas_call(
        cold_join_kernel,
        in_specs=[SMEM] + [VMEM] * N_DP,
        out_specs=(HBM, VMEM),
        out_shape=(
            jax.ShapeDtypeStruct((N_DP * size, width), BF),
            jax.ShapeDtypeStruct((N_DP * size // 128, 128), F32),
        ),
        scratch_shapes=[pltpu.SemaphoreType.DMA((N_DP,))],
        compiler_params=small_params(),
        name="cold_join",
    )(dp_at, *parts)


def pair_sum_kernel(*refs):
    mine_h = refs[:N_X]
    other_h = refs[N_X]
    outs = refs[N_X + 1 : 2 * N_X + 1]
    mine, other, sems = refs[2 * N_X + 1 :]
    copies = load_all([(mine_h[k], mine.at[k]) for k in range(N_X)] + [(other_h, other)], sems)
    for c in copies:
        c.wait()
    mine[...] = (mine[...].astype(F32) + other[...].astype(F32)).astype(mine.dtype)
    done = load_all([(mine.at[k], outs[k]) for k in range(N_X)], sems)
    for c in done:
        c.wait()


def pair_sum(mine, other):
    outs = tuple(jax.ShapeDtypeStruct(part.shape, part.dtype) for part in mine)
    return pl.pallas_call(
        pair_sum_kernel,
        in_specs=[HBM] * (N_X + 1),
        out_specs=(HBM,) * N_X,
        out_shape=outs,
        scratch_shapes=[
            pltpu.VMEM(other.shape, other.dtype),
            pltpu.VMEM(other.shape, other.dtype),
            pltpu.SemaphoreType.DMA((N_X + 1,)),
        ],
        compiler_params=params(),
        name="pair_sum",
    )(*mine, other)


def sum_parts_kernel(*refs):
    parts_h = refs[:N_X]
    out, parts, res, sems = refs[N_X:]
    copies = load_all([(parts_h[k], parts.at[k]) for k in range(N_X)], sems)
    for c in copies:
        c.wait()
    res[...] = (parts[0] + parts[1]) + (parts[2] + parts[3])
    done = pltpu.make_async_copy(res, out, sems.at[0])
    done.start()
    done.wait()


def sum_parts(parts):
    shape = parts[0].shape
    return pl.pallas_call(
        sum_parts_kernel,
        in_specs=[HBM] * N_X,
        out_specs=HBM,
        out_shape=jax.ShapeDtypeStruct(shape, F32),
        scratch_shapes=[
            pltpu.VMEM((N_X,) + shape, F32),
            pltpu.VMEM(shape, F32),
            pltpu.SemaphoreType.DMA((N_X,)),
        ],
        compiler_params=params(),
        name="sum_parts",
    )(*parts)


def hot_update_kernel(at_ref, table_h, accum_h, *refs):
    grads = refs[:N_DP]
    out, accum_out, table, accum, res, sems = refs[N_DP:]
    size = grads[0].shape[0]
    copies = load_all([(table_h, table), (accum_h, accum)], sems)
    eye = iota((size, size), 0) == iota((size, size), 1)
    for c in copies:
        c.wait()
    done = []
    for k in range(N_DP):
        chunk = chunk_of(at_ref[0], k)
        rows = pl.ds(pl.multiple_of(chunk * size, size), size)
        old = to_col(accum[pl.ds(chunk, 1), :], eye)
        updated, accum_new = adagrad(table[rows, :], old, grads[k][...])
        res[rows, :] = updated
        accum_out[pl.ds(chunk, 1), :] = to_row(accum_new, eye)
        done.append(pltpu.make_async_copy(res.at[rows, :], out.at[rows, :], sems.at[2 + k]))
        done[k].start()
    for c in done:
        c.wait()


def hot_update(dp_at, table, accum, grads):
    count, width = table.shape
    size = count // N_DP
    return pl.pallas_call(
        hot_update_kernel,
        in_specs=[SMEM] + [HBM] * 2 + [VMEM] * N_DP,
        out_specs=(HBM, VMEM),
        out_shape=(
            jax.ShapeDtypeStruct((count, width), F32),
            jax.ShapeDtypeStruct((N_DP, size), F32),
        ),
        scratch_shapes=[
            pltpu.VMEM((count, width), F32),
            pltpu.VMEM((N_DP, size), F32),
            pltpu.VMEM((count, width), F32),
            pltpu.SemaphoreType.DMA((2 + N_DP,)),
        ],
        compiler_params=small_params(),
        name="hot_update",
    )(dp_at, table, accum, *grads)


def exchange(value, axis):
    return lax.all_to_all(value, axis, split_axis=0, concat_axis=0, tiled=True)


def along_x(value, k):
    perm = [(i, ((i // 2 + k) % N_X) * 2 + i % 2) for i in range(N_DP)]
    return lax.ppermute(value, "dp", perm)


def to_partner(value):
    return lax.ppermute(value, "dp", [(i, i ^ 1) for i in range(N_DP)])


def to_owners(parts):
    *mine, other = parts
    other = to_partner(other)
    mine = pair_sum(mine, other)
    return [mine[0]] + [along_x(mine[k], k) for k in range(1, N_X)]


def to_all(part):
    along = [part] + [along_x(part, k) for k in range(1, N_X)]
    return along + [to_partner(value) for value in along]


def step(
    cold_table,
    cold_accum,
    dither_bits,
    hot_table,
    hot_accum,
    w_flat,
    w_inter,
    hidden_bias,
    w_out,
    targets,
    hot_ids,
    cold_slots,
    requests,
    counts,
):
    shards = lax.axis_size("shard")
    capacity = requests.shape[1]
    _, row_width = cold_table.shape
    hot_count = hot_table.shape[0]
    slots = shards * capacity
    dp_at = lax.axis_index("dp").astype(jnp.int32).reshape(1)

    live = jnp.arange(capacity, dtype=jnp.int32) < counts[:, :, None]
    asked = jnp.where(live, requests.reshape(MB, shards, capacity), -1)
    asked = asked.transpose(1, 0, 2).reshape(shards, MB * capacity)
    wanted = exchange(asked, "shard")

    fetched = []
    for m in range(MB):
        rows = serve(m, m == 1, wanted, cold_table)
        if m == 1:
            rows, hits = rows
        rows = exchange(rows.reshape(shards, capacity, row_width), "shard")
        fetched.append(rows.reshape(slots, row_width))
    own_table, own_bits = pick(dp_at, cold_table, dither_bits)
    xh = hot_rows(hot_ids, hot_table, cold_slots)

    owned = []
    hot_parts = []
    for m in range(MB):
        slot_grad, *hot_part = backprop(
            m,
            fetched[m],
            xh,
            cold_slots,
            cold_slots.T,
            targets.reshape(1, -1),
            w_flat,
            w_inter,
            hidden_bias.reshape(1, -1),
            w_out.reshape(1, -1),
        )
        hot_parts += hot_part
        rows = exchange(slot_grad.reshape(shards, capacity, row_width), "shard")
        owned.append(rows.reshape(slots, row_width))

    hot_grads = hot_scatter(dp_at, hot_ids.T, *hot_parts, hot_count)
    hot_grads = to_owners(hot_grads)
    hot_all = sum_parts(hot_grads)
    step_bit = shards // 2
    while step_bit:
        perm = [(i, i ^ step_bit) for i in range(shards)]
        hot_all = hot_all + lax.ppermute(hot_all, "shard", perm)
        step_bit //= 2
    hot_all = to_all(hot_all)
    hot_out, hot_accum_out = hot_update(
        dp_at, hot_table, hot_accum.reshape(N_DP, -1), hot_all
    )

    other = owner(1, dp_at, wanted, hits, owned)
    mine = owner(0, dp_at, wanted, hits, owned)
    parts = to_owners([*mine, *other])
    packed = cold_update(dp_at, own_table, cold_accum.reshape(-1, 128), own_bits, parts)
    parts = to_all(packed)
    cold_out, cold_accum_out = cold_join(dp_at, parts)
    return (cold_out, cold_accum_out.reshape(-1), hot_out, hot_accum_out.reshape(-1))


def solution(mesh):
    return jax.shard_map(
        step,
        mesh=mesh,
        in_specs=(
            P("shard", None),
            P("shard"),
            P("shard", None),
            P(),
            P(),
            P(),
            P(),
            P(),
            P(),
            P(("shard", "dp")),
            P(("shard", "dp"), None),
            P(("shard", "dp"), None),
            P(("shard", "dp"), None),
            P(("shard", "dp"), None),
        ),
        out_specs=(P("shard", None), P("shard"), P(), P()),
        check_vma=False,
    )
```

```python
import jax
import jax.numpy as jnp
from jax import lax
from jax.experimental import pallas as pl
from jax.experimental.pallas import tpu as pltpu
from jax.sharding import PartitionSpec as P


MB = 2
GROUP = 16
FEATS = 16
F_COLD = 8
BF = jnp.bfloat16
F32 = jnp.float32
NT = (((1,), (1,)), ((), ()))
HBM = pl.BlockSpec(memory_space=pltpu.HBM)
VMEM = pl.BlockSpec(memory_space=pltpu.VMEM)
SMEM = pl.BlockSpec(memory_space=pltpu.SMEM)
N_DP = 8
N_X = 4
VMEM_LIMIT = 64 << 20
learn_rate = 0.3
UNROLL = 8


def iota(shape, axis):
    return lax.broadcasted_iota(jnp.int32, shape, axis)


def as_one(same):
    return jnp.where(same, jnp.ones(same.shape, BF), jnp.zeros(same.shape, BF))


def mine_of(at, k, flip):
    return (((at >> 1) + k) & (N_X - 1)) * 2 + ((at & 1) ^ flip)


def chunk_of(at, i):
    x = ((at >> 1) - (i & 3)) & 3
    return x * 2 + ((at & 1) ^ (i >> 2))


def params():
    return pltpu.CompilerParams(vmem_limit_bytes=VMEM_LIMIT)


def small_params():
    return pltpu.CompilerParams(vmem_limit_bytes=24 << 20)


def load_all(pairs, sems):
    copies = [pltpu.make_async_copy(s, d, sems.at[i]) for i, (s, d) in enumerate(pairs)]
    for c in copies:
        c.start()
    return copies


def match_rows(ids, match, at, count):
    lanes = iota((GROUP, count), 1).astype(jnp.int16)
    for f in range(F_COLD):
        mine = jnp.broadcast_to(ids[:, f : f + 1], (GROUP, 128)).astype(jnp.int16)
        same = lanes == jnp.concatenate([mine] * (count // 128), axis=1)
        match[pl.ds(at + f * GROUP, GROUP), :count] = as_one(same)


def hot_rows_kernel(hot_ids, table, later, out, ids, src, match, res, sems):
    copies = load_all([(hot_ids, ids), (table, src)], sems)
    for c in copies:
        c.wait()
    source = src[...].astype(BF)
    half = F_COLD * GROUP
    block = 4
    steps = ids.shape[0] // GROUP // block

    def body(b, carry):
        for q in range(block):
            part = pl.ds(pl.multiple_of((b * block + q) * GROUP, GROUP), GROUP)
            match_rows(ids[part, :], match, q * half, source.shape[0])
        rows = pl.ds(pl.multiple_of(b * block * half, block * half), block * half)
        res[rows, :] = jnp.dot(match[...], source, preferred_element_type=F32).astype(BF)
        return carry

    lax.fori_loop(0, steps, body, 0)
    done = pltpu.make_async_copy(res, out, sems.at[2])
    done.start()
    done.wait()


def hot_rows(hot_ids, table, later):
    count, width = table.shape
    rows = hot_ids.shape[0] * F_COLD
    return pl.pallas_call(
        hot_rows_kernel,
        in_specs=[HBM] * 3,
        out_specs=HBM,
        out_shape=jax.ShapeDtypeStruct((rows, width), BF),
        scratch_shapes=[
            pltpu.VMEM(hot_ids.shape, jnp.int32),
            pltpu.VMEM(table.shape, F32),
            pltpu.VMEM((512, count), BF),
            pltpu.VMEM((rows, width), BF),
            pltpu.SemaphoreType.DMA((3,)),
        ],
        compiler_params=params(),
        name="hot_rows",
    )(hot_ids, table, later)


def step_kernel(m, *refs):
    (
        fetched_h, xh_h, slots_h, slots_t_h, targets_h, flat_h, inter_h, bias_h, w_out_h,
        slot_grad, hot_hi, hot_lo,
        fetched, x, slots, slots_t, targets, w_flat, w_inter, bias, w_out,
        a, pairs, back, mirror, g_hi, g_lo, h_hi, h_lo, match, slopes, sems,
    ) = refs
    width = fetched.shape[1]
    samples = targets.shape[1]
    groups = samples // GROUP
    lane_group = FEATS * GROUP
    half = F_COLD * GROUP
    scale = width ** (-0.5)
    block = 4
    first = m * samples

    head = load_all(
        [
            (slots_h.at[pl.ds(first, samples), :], slots),
            (fetched_h, fetched),
        ],
        sems,
    )
    hot_copies = [
        pltpu.make_async_copy(
            xh_h.at[pl.ds((m * groups + g) * half, half), :],
            x.at[pl.ds(g * lane_group + half, half), :],
            sems.at[2],
        )
        for g in range(groups)
    ]
    for c in hot_copies:
        c.start()
    tail = load_all(
        [
            (flat_h, w_flat),
            (inter_h, w_inter),
            (bias_h, bias),
            (w_out_h, w_out),
            (targets_h.at[:, pl.ds(first, samples)], targets),
            (slots_t_h.at[:, pl.ds(first, samples)], slots_t),
        ],
        sems.at[pl.ds(3, 6)],
    )

    sq = (lane_group, lane_group)
    i_hi = iota(sq, 0) >> 4
    i_lo = iota(sq, 0) & 15
    j_hi = iota(sq, 1) >> 4
    j_lo = iota(sq, 1) & 15
    spread = jnp.where(i_hi == j_lo, 1.0, 0.0).astype(BF)
    spread_t = jnp.where(i_lo == j_hi, 1.0, 0.0).astype(BF)
    swap = jnp.where((i_hi == j_lo) & (i_lo == j_hi), 1.0, 0.0).astype(BF)

    for c in head:
        c.wait()

    def gather(b, carry):
        for q in range(block):
            part = pl.ds(pl.multiple_of((b * block + q) * GROUP, GROUP), GROUP)
            match_rows(slots[part, :], match, q * half, fetched.shape[0])
        picked = jnp.dot(match[...], fetched[...], preferred_element_type=F32).astype(BF)
        for q in range(block):
            dst = pl.multiple_of((b * block + q) * lane_group, lane_group)
            x[pl.ds(dst, half), :] = picked[q * half : (q + 1) * half]
        return carry

    lax.fori_loop(0, groups // block, gather, 0)
    for c in hot_copies:
        c.wait()

    def dots(i, carry):
        for u in range(UNROLL):
            g = i * UNROLL + u
            rows = pl.ds(pl.multiple_of(g * lane_group, lane_group), lane_group)
            part = pl.ds(pl.multiple_of(g * GROUP, GROUP), GROUP)
            xg = x[rows, :]
            for f in range(FEATS):
                a[part, f * width : (f + 1) * width] = xg[f * GROUP : (f + 1) * GROUP]
            gram = lax.dot_general(xg, xg, NT, preferred_element_type=F32) * scale
            own = jnp.where(i_lo == j_lo, gram, 0.0).astype(BF)
            wide = jnp.dot(own, spread, preferred_element_type=F32)
            wide = jnp.where(i_hi == j_hi, wide, 0.0)
            pairs[part, :] = jnp.sum(
                wide.reshape(FEATS, GROUP, lane_group), axis=0
            ).astype(BF)
        return carry

    lax.fori_loop(0, groups // UNROLL, dots, 0)
    for c in tail:
        c.wait()

    pre = jnp.dot(a[...], w_flat[...], preferred_element_type=F32)
    pre = pre + jnp.dot(pairs[...], w_inter[...], preferred_element_type=F32)
    pre = pre + bias[...]
    gated = jax.nn.sigmoid(pre)
    logits = jnp.sum(pre * gated * w_out[...], axis=-1, keepdims=True)
    eye = iota((samples, samples), 0) == iota((samples, samples), 1)
    target = jnp.sum(jnp.where(eye, targets[...], 0.0), axis=1, keepdims=True)
    residual = jax.nn.sigmoid(logits) - target
    slopes[...] = (residual * w_out[...] * gated * (1.0 + pre * (1.0 - gated))).astype(BF)

    inter_t = jnp.dot(swap, w_inter[...], preferred_element_type=F32).astype(BF)
    both = lax.dot_general(slopes[...], w_inter[...], NT, preferred_element_type=F32)
    both = both + lax.dot_general(slopes[...], inter_t, NT, preferred_element_type=F32)
    mirror[...] = (both * scale).astype(BF)

    def flat_back(f, carry):
        rows = pl.ds(pl.multiple_of(f * width, width), width)
        back[f] = lax.dot_general(
            slopes[...], w_flat[rows, :], NT, preferred_element_type=F32
        )
        return carry

    lax.fori_loop(0, FEATS, flat_back, 0)

    def grads(i, carry):
        for u in range(UNROLL):
            g = i * UNROLL + u
            rows = pl.ds(pl.multiple_of(g * lane_group, lane_group), lane_group)
            part = pl.ds(pl.multiple_of(g * GROUP, GROUP), GROUP)
            mine = mirror[part, :].astype(F32)
            tall = jnp.broadcast_to(mine[None], (FEATS, GROUP, lane_group)).reshape(sq)
            tall = jnp.where(i_hi == j_hi, tall, 0.0).astype(BF)
            wide = jnp.dot(tall, spread_t, preferred_element_type=F32)
            wide = jnp.where(i_lo == j_lo, wide, 0.0).astype(BF)
            total = jnp.dot(wide, x[rows, :], preferred_element_type=F32)
            total = total + back[:, part, :].reshape(lane_group, width)
            hi = total.astype(BF)
            lo = (total - hi.astype(F32)).astype(BF)
            for f in range(F_COLD):
                dst = pl.ds(pl.multiple_of(f * samples + g * GROUP, GROUP), GROUP)
                at = f * GROUP
                g_hi[dst, :] = hi[at : at + GROUP]
                g_lo[dst, :] = lo[at : at + GROUP]
                h_hi[dst, :] = hi[half + at : half + at + GROUP]
                h_lo[dst, :] = lo[half + at : half + at + GROUP]
        return carry

    lax.fori_loop(0, groups // UNROLL, grads, 0)
    outs = load_all([(h_hi, hot_hi), (h_lo, hot_lo)], sems.at[pl.ds(0, 2)])

    rows_blk = 512

    def scatter(b, carry):
        at = pl.multiple_of(b * rows_blk, rows_blk)
        subs = iota((rows_blk, samples), 0).astype(jnp.int16)
        for f in range(F_COLD):
            mine = jnp.broadcast_to(slots_t[f : f + 1, :] - at, (16, samples)).astype(jnp.int16)
            same = subs == jnp.concatenate([mine] * (rows_blk // 16), axis=0)
            match[:, f * samples : (f + 1) * samples] = as_one(same)
        total = jnp.dot(match[...], g_hi[...], preferred_element_type=F32)
        total = total + jnp.dot(match[...], g_lo[...], preferred_element_type=F32)
        fetched[pl.ds(at, rows_blk), :] = total.astype(BF)
        pltpu.make_async_copy(
            fetched.at[pl.ds(at, rows_blk), :], slot_grad.at[pl.ds(at, rows_blk), :], sems.at[3 + b]
        ).start()
        return carry

    n_out = slot_grad.shape[0] // rows_blk
    lax.fori_loop(0, n_out, scatter, 0)
    for b in range(n_out):
        pltpu.make_async_copy(
            fetched.at[pl.ds(b * rows_blk, rows_blk), :],
            slot_grad.at[pl.ds(b * rows_blk, rows_blk), :],
            sems.at[3 + b],
        ).wait()
    for c in outs:
        c.wait()


def backprop(m, fetched, xh, slots, slots_t, targets, w_flat, w_inter, bias, w_out):
    count, width = fetched.shape
    samples = slots.shape[0] // MB
    hidden = w_flat.shape[1]
    lookups = samples * F_COLD
    wide = FEATS * width
    rows = jax.ShapeDtypeStruct((lookups, width), BF)
    return pl.pallas_call(
        lambda *refs: step_kernel(m, *refs),
        in_specs=[HBM] * 9,
        out_specs=(HBM,) * 3,
        out_shape=(jax.ShapeDtypeStruct((count, width), BF), rows, rows),
        scratch_shapes=[
            pltpu.VMEM((count, width), BF),
            pltpu.VMEM((samples * FEATS, width), BF),
            pltpu.VMEM((samples, F_COLD), jnp.int32),
            pltpu.VMEM((F_COLD, samples), jnp.int32),
            pltpu.VMEM((1, samples), F32),
            pltpu.VMEM(w_flat.shape, BF),
            pltpu.VMEM(w_inter.shape, BF),
            pltpu.VMEM((1, hidden), F32),
            pltpu.VMEM((1, hidden), F32),
            pltpu.VMEM((samples, wide), BF),
            pltpu.VMEM((samples, FEATS * FEATS), BF),
            pltpu.VMEM((FEATS, samples, width), F32),
            pltpu.VMEM((samples, FEATS * FEATS), BF),
            pltpu.VMEM((lookups, width), BF),
            pltpu.VMEM((lookups, width), BF),
            pltpu.VMEM((lookups, width), BF),
            pltpu.VMEM((lookups, width), BF),
            pltpu.VMEM((512, 2048), BF),
            pltpu.VMEM((samples, hidden), BF),
            pltpu.SemaphoreType.DMA((9,)),
        ],
        compiler_params=params(),
        name="train_step",
    )(fetched, xh, slots, slots_t, targets, w_flat, w_inter, bias, w_out)


def hot_scatter_kernel(at_ref, ids_h, hi0, lo0, hi1, lo1, *refs):
    outs = refs[:N_X]
    other, ids, h0, l0, h1, l1, match, res, sems = refs[N_X:]
    copies = load_all([(ids_h, ids), (hi0, h0), (lo0, l0), (hi1, h1), (lo1, l1)], sems)
    samples = ids.shape[1] // MB
    block = match.shape[1]
    size = res.shape[0] // N_DP
    subs = iota((block, samples), 0).astype(jnp.int16)
    for c in copies:
        c.wait()

    def body(b, carry):
        at = pl.multiple_of(b * block, block)
        total = None
        for m, parts in enumerate(((h0, l0), (h1, l1))):
            for f in range(F_COLD):
                row = ids[f : f + 1, m * samples : (m + 1) * samples] - at
                mine = jnp.broadcast_to(row, (16, samples)).astype(jnp.int16)
                same = subs == jnp.concatenate([mine] * (block // 16), axis=0)
                match[m, :, f * samples : (f + 1) * samples] = as_one(same)
            for part in parts:
                term = jnp.dot(match[m], part[...], preferred_element_type=F32)
                total = term if total is None else total + term
        res[pl.ds(at, block), :] = total
        return carry

    lax.fori_loop(0, res.shape[0] // block, body, 0)
    done = []
    for k in range(N_X):
        for flip, dst in ((0, outs[k]), (1, other.at[k])):
            chunk = mine_of(at_ref[0], k, flip)
            src = res.at[pl.ds(pl.multiple_of(chunk * size, size), size), :]
            done.append(pltpu.make_async_copy(src, dst, sems.at[2 * k + flip]))
            done[-1].start()
    for c in done:
        c.wait()


def hot_scatter(dp_at, ids, hi0, lo0, hi1, lo1, count):
    rows, width = hi0.shape
    return pl.pallas_call(
        hot_scatter_kernel,
        in_specs=[SMEM] + [HBM] * 5,
        out_specs=(HBM,) * (N_X + 1),
        out_shape=(jax.ShapeDtypeStruct((count // N_DP, width), F32),) * N_X
        + (jax.ShapeDtypeStruct((N_X, count // N_DP, width), F32),),
        scratch_shapes=[pltpu.VMEM(ids.shape, jnp.int32)]
        + [pltpu.VMEM((rows, width), BF)] * 4
        + [
            pltpu.VMEM((MB, 256, rows), BF),
            pltpu.VMEM((count, width), F32),
            pltpu.SemaphoreType.DMA((5 + N_DP,)),
        ],
        compiler_params=params(),
        name="hot_scatter",
    )(dp_at, ids, hi0, lo0, hi1, lo1)


def serve_kernel(m, with_hits, wanted, table_h, rows, *refs):
    if with_hits:
        hits, table, match, res, count_acc, sems = refs
    else:
        table, match, res, sems = refs
    load = pltpu.make_async_copy(table_h, table, sems.at[0])
    load.start()
    shards, lanes = wanted.shape
    capacity = lanes // MB
    count = table.shape[0]
    per = 8
    block = per * capacity
    ids = jnp.concatenate([wanted[...], jnp.zeros((lanes - shards, lanes), jnp.int32)], axis=0)
    turned = ids.T
    names = iota((capacity, count), 1).astype(jnp.int16)
    if with_hits:
        count_acc[...] = jnp.zeros_like(count_acc)

    def ones_of(part, mb, j):
        col = part[mb * capacity : (mb + 1) * capacity, j : j + 1]
        mine = jnp.broadcast_to(col, (capacity, 128)).astype(jnp.int16)
        return as_one(names == jnp.concatenate([mine] * (count // 128), axis=1))

    def add_hits(one):
        tall = one[0:16] + one[16:32] + one[32:48] + one[48:64]
        count_acc[...] += tall

    def body(b, carry):
        part = pltpu.roll(turned, lanes - b * per, 1)
        for j in range(per):
            one = ones_of(part, m, j)
            match[j * capacity : (j + 1) * capacity, :] = one
            if with_hits:
                add_hits(one)
                for other in range(MB):
                    if other != m:
                        add_hits(ones_of(part, other, j))
        at = pl.ds(pl.multiple_of(b * block, block), block)
        res[at, :] = jnp.dot(match[...], table[...], preferred_element_type=F32).astype(BF)
        pltpu.make_async_copy(res.at[at, :], rows.at[at, :], sems.at[1 + b]).start()
        return carry

    steps = shards // per
    load.wait()
    lax.fori_loop(0, steps, body, 0)
    if with_hits:
        total = jnp.sum(count_acc[...].astype(F32), axis=0, keepdims=True)
        size = count // N_DP
        for p in range(N_DP):
            hits[p : p + 1, :] = total[:, p * size : (p + 1) * size]
    for b in range(steps):
        at = pl.ds(b * block, block)
        pltpu.make_async_copy(res.at[at, :], rows.at[at, :], sems.at[1 + b]).wait()


def serve(m, with_hits, wanted, table):
    shards, lanes = wanted.shape
    capacity = lanes // MB
    slots = shards * capacity
    count, width = table.shape
    rows = jax.ShapeDtypeStruct((slots, width), BF)
    extra = [pltpu.VMEM((16, count), BF)] if with_hits else []
    return pl.pallas_call(
        lambda *refs: serve_kernel(m, with_hits, *refs),
        in_specs=[VMEM, HBM],
        out_specs=(HBM, VMEM) if with_hits else HBM,
        out_shape=(rows, jax.ShapeDtypeStruct((N_DP, count // N_DP), F32))
        if with_hits
        else rows,
        scratch_shapes=[
            pltpu.VMEM(table.shape, BF),
            pltpu.VMEM((512, count), BF),
            pltpu.VMEM((slots, width), BF),
        ]
        + extra
        + [pltpu.SemaphoreType.DMA((1 + shards // 8,))],
        compiler_params=params(),
        name="serve_rows",
    )(wanted, table)


def id_tiles(wanted, m):
    ids = wanted[...]
    other = pltpu.roll(ids, 64, 1)
    left, right = (ids, other) if m == 0 else (other, ids)
    low = iota((1, 128), 1) < 64
    return [
        jnp.where(low, left[2 * i : 2 * i + 1], right[2 * i + 1 : 2 * i + 2])
        for i in range(ids.shape[0] // 2)
    ]


def owner_match(tiles, base, match, subs):
    size = match.shape[0]
    for i, tile in enumerate(tiles):
        mine = jnp.broadcast_to(tile - base, (16, 128)).astype(jnp.int16)
        same = subs == jnp.concatenate([mine] * (size // 16), axis=0)
        match[:, i * 128 : (i + 1) * 128] = as_one(same)


def owner_kernel(flip, at_ref, wanted, hits, *refs):
    grads_h = refs[:MB]
    outs = refs[MB : -4]
    grads, match, res, sems = refs[-4:]
    size = match.shape[1]
    copies = load_all([(grads_h[m], grads.at[m]) for m in range(MB)], sems)
    tiles = [id_tiles(wanted, m) for m in range(MB)]
    subs = iota((size, 128), 0).astype(jnp.int16)
    for c in copies:
        c.wait()

    def body(k, carry):
        chunk = mine_of(at_ref[0], k, flip)
        at = pl.multiple_of(chunk * size, size)
        total = None
        for m in range(MB):
            owner_match(tiles[m], at, match.at[m], subs)
            term = jnp.dot(match[m], grads[m], preferred_element_type=F32)
            total = term if total is None else total + term
        res[k, :size, :] = total.astype(BF)
        mine = hits[pl.ds(chunk, 1), :]
        res[k, size:, :] = jnp.broadcast_to(mine, (16, size)).astype(BF)
        return carry

    lax.fori_loop(0, N_X, body, 0)
    if flip:
        done = load_all([(res, outs[0])], sems)
    else:
        done = load_all([(res.at[k], outs[k]) for k in range(N_X)], sems)
    for c in done:
        c.wait()


def owner(flip, dp_at, wanted, hits, grads):
    slots, width = grads[0].shape
    size = hits.shape[1]
    part = (size + 16, width)
    whole = (jax.ShapeDtypeStruct((N_X,) + part, BF),)
    each = (jax.ShapeDtypeStruct(part, BF),) * N_X
    return pl.pallas_call(
        lambda *refs: owner_kernel(flip, *refs),
        in_specs=[SMEM, VMEM, VMEM] + [HBM] * MB,
        out_specs=(HBM,) * (1 if flip else N_X),
        out_shape=whole if flip else each,
        scratch_shapes=[
            pltpu.VMEM((MB, slots, width), BF),
            pltpu.VMEM((MB, size, slots), BF),
            pltpu.VMEM((N_X,) + part, BF),
            pltpu.SemaphoreType.DMA((MB + N_X,)),
        ],
        compiler_params=small_params(),
        name="owner_other" if flip else "owner_mine",
    )(dp_at, wanted, hits, *grads)


def to_col(row, eye):
    return jnp.sum(jnp.where(eye, row, 0.0), axis=1, keepdims=True)


def to_row(col, eye):
    return jnp.sum(jnp.where(eye, col, 0.0), axis=0, keepdims=True)


def adagrad(table, accum, grad):
    accum_new = accum + jnp.mean(grad * grad, axis=-1, keepdims=True)
    return table - learn_rate * grad / jnp.sqrt(accum_new), accum_new


def pick_kernel(at_ref, table_h, bits_h, table_out, bits_out, table, bits, sems):
    size = table.shape[0]
    rows = pl.ds(pl.multiple_of(at_ref[0] * size, size), size)
    for pairs in (
        [(table_h.at[rows, :], table), (bits_h.at[rows, :], bits)],
        [(table, table_out), (bits, bits_out)],
    ):
        for c in load_all(pairs, sems):
            c.wait()


def pick(dp_at, table, bits):
    shape = (table.shape[0] // N_DP, table.shape[1])
    return pl.pallas_call(
        pick_kernel,
        in_specs=[SMEM, HBM, HBM],
        out_specs=(HBM, HBM),
        out_shape=(
            jax.ShapeDtypeStruct(shape, table.dtype),
            jax.ShapeDtypeStruct(shape, bits.dtype),
        ),
        scratch_shapes=[
            pltpu.VMEM(shape, table.dtype),
            pltpu.VMEM(shape, bits.dtype),
            pltpu.SemaphoreType.DMA((2,)),
        ],
        compiler_params=params(),
        name="pick_rows",
    )(dp_at, table, bits)


def cold_update_kernel(at_ref, *refs):
    ins = refs[: 3 + N_X]
    out = refs[3 + N_X]
    table, accum, bits, parts, res, sems = refs[4 + N_X :]
    size = table.shape[0]
    spots = [table, accum, bits] + [parts.at[k] for k in range(N_X)]
    copies = load_all(list(zip(ins, spots)), sems)
    eye = iota((size, size), 0) == iota((size, size), 1)
    for c in copies:
        c.wait()
    total = parts[0].astype(F32)
    for k in range(1, N_X):
        total = total + parts[k].astype(F32)
    touched = to_col(total[size : size + 1], eye)
    averaged = total[:size] / jnp.maximum(touched, 1.0)
    at = at_ref[0] * 2
    old = jnp.concatenate([accum[pl.ds(at, 1), :], accum[pl.ds(at + 1, 1), :]], axis=1)
    old = to_col(old, eye)
    updated, accum_new = adagrad(table[...].astype(F32), old, averaged)
    grid_step = jnp.max(jnp.abs(updated), axis=-1, keepdims=True) / 8.0
    dither = bits[...].astype(F32) * (1.0 / 65280.0) - 0.5
    res[:size, :] = jnp.where(touched > 0.5, updated + grid_step * dither, updated).astype(BF)
    row = to_row(accum_new, eye)
    high = row.astype(BF).astype(F32)
    middle = (row - high).astype(BF).astype(F32)
    low = (row - high) - middle
    which = iota((16, size), 0)
    packed = jnp.where(which == 0, high, jnp.where(which == 1, middle, low))
    res[size:, :] = packed.astype(BF)
    done = pltpu.make_async_copy(res, out, sems.at[0])
    done.start()
    done.wait()


def cold_update(dp_at, table, accum, bits, parts):
    shape = parts[0].shape
    return pl.pallas_call(
        cold_update_kernel,
        in_specs=[SMEM] + [HBM] * (3 + N_X),
        out_specs=HBM,
        out_shape=jax.ShapeDtypeStruct(shape, BF),
        scratch_shapes=[
            pltpu.VMEM(table.shape, BF),
            pltpu.VMEM(accum.shape, F32),
            pltpu.VMEM(bits.shape, jnp.int32),
            pltpu.VMEM((N_X,) + shape, BF),
            pltpu.VMEM(shape, BF),
            pltpu.SemaphoreType.DMA((3 + N_X,)),
        ],
        compiler_params=small_params(),
        name="cold_update",
    )(dp_at, table, accum, bits, *parts)


def cold_join_kernel(at_ref, *refs):
    parts = refs[:N_DP]
    out, accum_out, sems = refs[N_DP:]
    size = out.shape[0] // N_DP
    done = []
    for i in range(N_DP):
        chunk = chunk_of(at_ref[0], i)
        dst = out.at[pl.ds(pl.multiple_of(chunk * size, size), size), :]
        done.append(pltpu.make_async_copy(parts[i].at[pl.ds(0, size), :], dst, sems.at[i]))
        done[i].start()
    for i in range(N_DP):
        chunk = chunk_of(at_ref[0], i)
        rows = parts[i][size:, :].astype(F32)
        row = (rows[2:3] + rows[1:2]) + rows[0:1]
        accum_out[pl.ds(chunk * 2, 1), :] = row[:, :128]
        accum_out[pl.ds(chunk * 2 + 1, 1), :] = row[:, 128:]
    for c in done:
        c.wait()


def cold_join(dp_at, parts):
    width = parts[0].shape[1]
    size = parts[0].shape[0] - 16
    return pl.pallas_call(
        cold_join_kernel,
        in_specs=[SMEM] + [VMEM] * N_DP,
        out_specs=(HBM, VMEM),
        out_shape=(
            jax.ShapeDtypeStruct((N_DP * size, width), BF),
            jax.ShapeDtypeStruct((N_DP * size // 128, 128), F32),
        ),
        scratch_shapes=[pltpu.SemaphoreType.DMA((N_DP,))],
        compiler_params=small_params(),
        name="cold_join",
    )(dp_at, *parts)


def pair_sum_kernel(*refs):
    mine_h = refs[:N_X]
    other_h = refs[N_X]
    outs = refs[N_X + 1 : 2 * N_X + 1]
    mine, other, sems = refs[2 * N_X + 1 :]
    copies = load_all([(mine_h[k], mine.at[k]) for k in range(N_X)] + [(other_h, other)], sems)
    for c in copies:
        c.wait()
    mine[...] = (mine[...].astype(F32) + other[...].astype(F32)).astype(mine.dtype)
    done = load_all([(mine.at[k], outs[k]) for k in range(N_X)], sems)
    for c in done:
        c.wait()


def pair_sum(mine, other):
    outs = tuple(jax.ShapeDtypeStruct(part.shape, part.dtype) for part in mine)
    return pl.pallas_call(
        pair_sum_kernel,
        in_specs=[HBM] * (N_X + 1),
        out_specs=(HBM,) * N_X,
        out_shape=outs,
        scratch_shapes=[
            pltpu.VMEM(other.shape, other.dtype),
            pltpu.VMEM(other.shape, other.dtype),
            pltpu.SemaphoreType.DMA((N_X + 1,)),
        ],
        compiler_params=small_params(),
        name="pair_sum",
    )(*mine, other)


def sum_parts_kernel(*refs):
    parts_h = refs[:N_X]
    out, parts, res, sems = refs[N_X:]
    copies = load_all([(parts_h[k], parts.at[k]) for k in range(N_X)], sems)
    for c in copies:
        c.wait()
    res[...] = (parts[0] + parts[1]) + (parts[2] + parts[3])
    done = pltpu.make_async_copy(res, out, sems.at[0])
    done.start()
    done.wait()


def sum_parts(parts):
    shape = parts[0].shape
    return pl.pallas_call(
        sum_parts_kernel,
        in_specs=[HBM] * N_X,
        out_specs=HBM,
        out_shape=jax.ShapeDtypeStruct(shape, F32),
        scratch_shapes=[
            pltpu.VMEM((N_X,) + shape, F32),
            pltpu.VMEM(shape, F32),
            pltpu.SemaphoreType.DMA((N_X,)),
        ],
        compiler_params=small_params(),
        name="sum_parts",
    )(*parts)


def hot_update_kernel(at_ref, table_h, accum_h, *refs):
    grads = refs[:N_DP]
    out, accum_out, table, accum, res, sems = refs[N_DP:]
    size = grads[0].shape[0]
    copies = load_all([(table_h, table), (accum_h, accum)], sems)
    eye = iota((size, size), 0) == iota((size, size), 1)
    for c in copies:
        c.wait()
    done = []
    for k in range(N_DP):
        chunk = chunk_of(at_ref[0], k)
        rows = pl.ds(pl.multiple_of(chunk * size, size), size)
        old = to_col(accum[pl.ds(chunk, 1), :], eye)
        updated, accum_new = adagrad(table[rows, :], old, grads[k][...])
        res[rows, :] = updated
        accum_out[pl.ds(chunk, 1), :] = to_row(accum_new, eye)
        done.append(pltpu.make_async_copy(res.at[rows, :], out.at[rows, :], sems.at[2 + k]))
        done[k].start()
    for c in done:
        c.wait()


def hot_update(dp_at, table, accum, grads):
    count, width = table.shape
    size = count // N_DP
    return pl.pallas_call(
        hot_update_kernel,
        in_specs=[SMEM] + [HBM] * 2 + [VMEM] * N_DP,
        out_specs=(HBM, VMEM),
        out_shape=(
            jax.ShapeDtypeStruct((count, width), F32),
            jax.ShapeDtypeStruct((N_DP, size), F32),
        ),
        scratch_shapes=[
            pltpu.VMEM((count, width), F32),
            pltpu.VMEM((N_DP, size), F32),
            pltpu.VMEM((count, width), F32),
            pltpu.SemaphoreType.DMA((2 + N_DP,)),
        ],
        compiler_params=small_params(),
        name="hot_update",
    )(dp_at, table, accum, *grads)


def exchange(value, axis):
    return lax.all_to_all(value, axis, split_axis=0, concat_axis=0, tiled=True)


def along_x(value, k):
    perm = [(i, ((i // 2 + k) % N_X) * 2 + i % 2) for i in range(N_DP)]
    return lax.ppermute(value, "dp", perm)


def to_partner(value):
    return lax.ppermute(value, "dp", [(i, i ^ 1) for i in range(N_DP)])


def to_owners(parts):
    *mine, other = parts
    other = to_partner(other)
    mine = pair_sum(mine, other)
    return [mine[0]] + [along_x(mine[k], k) for k in range(1, N_X)]


def to_all(part):
    along = [part] + [along_x(part, k) for k in range(1, N_X)]
    return along + [to_partner(value) for value in along]


def step(
    cold_table,
    cold_accum,
    dither_bits,
    hot_table,
    hot_accum,
    w_flat,
    w_inter,
    hidden_bias,
    w_out,
    targets,
    hot_ids,
    cold_slots,
    requests,
    counts,
):
    shards = lax.axis_size("shard")
    capacity = requests.shape[1]
    _, row_width = cold_table.shape
    hot_count = hot_table.shape[0]
    slots = shards * capacity
    dp_at = lax.axis_index("dp").astype(jnp.int32).reshape(1)

    live = jnp.arange(capacity, dtype=jnp.int32) < counts[:, :, None]
    asked = jnp.where(live, requests.reshape(MB, shards, capacity), -1)
    asked = asked.transpose(1, 0, 2).reshape(shards, MB * capacity)
    wanted = exchange(asked, "shard")

    fetched = []
    for m in range(MB):
        rows = serve(m, m == 1, wanted, cold_table)
        if m == 1:
            rows, hits = rows
        rows = exchange(rows.reshape(shards, capacity, row_width), "shard")
        fetched.append(rows.reshape(slots, row_width))
    own_table, own_bits = pick(dp_at, cold_table, dither_bits)
    xh = hot_rows(hot_ids, hot_table, cold_slots)

    owned = []
    hot_parts = []
    for m in range(MB):
        slot_grad, *hot_part = backprop(
            m,
            fetched[m],
            xh,
            cold_slots,
            cold_slots.T,
            targets.reshape(1, -1),
            w_flat,
            w_inter,
            hidden_bias.reshape(1, -1),
            w_out.reshape(1, -1),
        )
        hot_parts += hot_part
        rows = exchange(slot_grad.reshape(shards, capacity, row_width), "shard")
        owned.append(rows.reshape(slots, row_width))

    hot_grads = hot_scatter(dp_at, hot_ids.T, *hot_parts, hot_count)
    hot_grads = to_owners(hot_grads)
    hot_all = sum_parts(hot_grads)
    step_bit = shards // 2
    while step_bit:
        perm = [(i, i ^ step_bit) for i in range(shards)]
        hot_all = hot_all + lax.ppermute(hot_all, "shard", perm)
        step_bit //= 2
    hot_all = to_all(hot_all)
    hot_out, hot_accum_out = hot_update(
        dp_at, hot_table, hot_accum.reshape(N_DP, -1), hot_all
    )

    other = owner(1, dp_at, wanted, hits, owned)
    mine = owner(0, dp_at, wanted, hits, owned)
    parts = to_owners([*mine, *other])
    packed = cold_update(dp_at, own_table, cold_accum.reshape(-1, 128), own_bits, parts)
    parts = to_all(packed)
    cold_out, cold_accum_out = cold_join(dp_at, parts)
    return (cold_out, cold_accum_out.reshape(-1), hot_out, hot_accum_out.reshape(-1))


def solution(mesh):
    return jax.shard_map(
        step,
        mesh=mesh,
        in_specs=(
            P("shard", None),
            P("shard"),
            P("shard", None),
            P(),
            P(),
            P(),
            P(),
            P(),
            P(),
            P(("shard", "dp")),
            P(("shard", "dp"), None),
            P(("shard", "dp"), None),
            P(("shard", "dp"), None),
            P(("shard", "dp"), None),
        ),
        out_specs=(P("shard", None), P("shard"), P(), P()),
        check_vma=False,
    )
```

```python
import functools

import jax
import jax.numpy as jnp
from jax import lax
from jax.experimental import pallas as pl
from jax.experimental.pallas import tpu as pltpu
from jax.sharding import PartitionSpec as P


MB = 2
GROUP = 16
FEATS = 16
F_COLD = 8
BF = jnp.bfloat16
F32 = jnp.float32
NT = (((1,), (1,)), ((), ()))
HBM = pl.BlockSpec(memory_space=pltpu.HBM)
VMEM = pl.BlockSpec(memory_space=pltpu.VMEM)
SMEM = pl.BlockSpec(memory_space=pltpu.SMEM)
N_DP = 8
N_X = 4
VMEM_LIMIT = 64 << 20
learn_rate = 0.3
UNROLL = 4


def iota(shape, axis):
    return lax.broadcasted_iota(jnp.int32, shape, axis)


def as_one(same):
    return jnp.where(same, jnp.ones(same.shape, BF), jnp.zeros(same.shape, BF))


def mine_of(at, k, flip):
    return (((at >> 1) + k) & (N_X - 1)) * 2 + ((at & 1) ^ flip)


def chunk_of(at, i):
    x = ((at >> 1) - (i & 3)) & 3
    return x * 2 + ((at & 1) ^ (i >> 2))


def params():
    return pltpu.CompilerParams(vmem_limit_bytes=VMEM_LIMIT)


def small_params():
    return pltpu.CompilerParams(vmem_limit_bytes=24 << 20)


def load_all(pairs, sems):
    copies = [pltpu.make_async_copy(s, d, sems.at[i]) for i, (s, d) in enumerate(pairs)]
    for c in copies:
        c.start()
    return copies


def match_rows(ids, match, at, count):
    lanes = iota((GROUP, count), 1).astype(jnp.int16)
    for f in range(F_COLD):
        mine = jnp.broadcast_to(ids[:, f : f + 1], (GROUP, 128)).astype(jnp.int16)
        same = lanes == jnp.concatenate([mine] * (count // 128), axis=1)
        match[pl.ds(at + f * GROUP, GROUP), :count] = as_one(same)


def hot_rows_kernel(hot_ids, table, later, out, ids, src, match, res, sems):
    copies = load_all([(hot_ids, ids), (table, src)], sems)
    for c in copies:
        c.wait()
    source = src[...].astype(BF)
    half = F_COLD * GROUP
    block = 4
    steps = ids.shape[0] // GROUP // block

    def body(b, carry):
        for q in range(block):
            part = pl.ds(pl.multiple_of((b * block + q) * GROUP, GROUP), GROUP)
            match_rows(ids[part, :], match, q * half, source.shape[0])
        rows = pl.ds(pl.multiple_of(b * block * half, block * half), block * half)
        res[rows, :] = jnp.dot(match[...], source, preferred_element_type=F32).astype(BF)
        return carry

    lax.fori_loop(0, steps, body, 0)
    done = pltpu.make_async_copy(res, out, sems.at[2])
    done.start()
    done.wait()


def hot_rows(hot_ids, table, later):
    count, width = table.shape
    rows = hot_ids.shape[0] * F_COLD
    return pl.pallas_call(
        hot_rows_kernel,
        in_specs=[HBM] * 3,
        out_specs=HBM,
        out_shape=jax.ShapeDtypeStruct((rows, width), BF),
        scratch_shapes=[
            pltpu.VMEM(hot_ids.shape, jnp.int32),
            pltpu.VMEM(table.shape, F32),
            pltpu.VMEM((512, count), BF),
            pltpu.VMEM((rows, width), BF),
            pltpu.SemaphoreType.DMA((3,)),
        ],
        compiler_params=params(),
        name="hot_rows",
    )(hot_ids, table, later)


def step_kernel(m, *refs):
    (
        fetched_h, xh_h, slots_h, slots_t_h, targets_h, flat_h, inter_h, bias_h, w_out_h,
        slot_grad, hot_hi, hot_lo,
        fetched, x, slots, slots_t, targets, w_flat, w_inter, bias, w_out,
        a, pairs, back, mirror, g_hi, g_lo, h_hi, h_lo, match, slopes, sems,
    ) = refs
    width = fetched.shape[1]
    samples = targets.shape[1]
    groups = samples // GROUP
    lane_group = FEATS * GROUP
    half = F_COLD * GROUP
    scale = width ** (-0.5)
    block = 4
    first = m * samples

    head = load_all(
        [
            (slots_h.at[pl.ds(first, samples), :], slots),
            (fetched_h, fetched),
        ],
        sems,
    )
    hot_copies = [
        pltpu.make_async_copy(
            xh_h.at[pl.ds((m * groups + g) * half, half), :],
            x.at[pl.ds(g * lane_group + half, half), :],
            sems.at[2],
        )
        for g in range(groups)
    ]
    for c in hot_copies:
        c.start()
    tail = load_all(
        [
            (flat_h, w_flat),
            (inter_h, w_inter),
            (bias_h, bias),
            (w_out_h, w_out),
            (targets_h.at[:, pl.ds(first, samples)], targets),
            (slots_t_h.at[:, pl.ds(first, samples)], slots_t),
        ],
        sems.at[pl.ds(3, 6)],
    )

    sq = (lane_group, lane_group)
    i_hi = iota(sq, 0) >> 4
    i_lo = iota(sq, 0) & 15
    j_hi = iota(sq, 1) >> 4
    j_lo = iota(sq, 1) & 15
    spread = jnp.where(i_hi == j_lo, 1.0, 0.0).astype(BF)
    spread_t = jnp.where(i_lo == j_hi, 1.0, 0.0).astype(BF)
    swap = jnp.where((i_hi == j_lo) & (i_lo == j_hi), 1.0, 0.0).astype(BF)

    for c in head:
        c.wait()

    def gather(b, carry):
        for q in range(block):
            part = pl.ds(pl.multiple_of((b * block + q) * GROUP, GROUP), GROUP)
            match_rows(slots[part, :], match, q * half, fetched.shape[0])
        picked = jnp.dot(match[...], fetched[...], preferred_element_type=F32).astype(BF)
        for q in range(block):
            dst = pl.multiple_of((b * block + q) * lane_group, lane_group)
            x[pl.ds(dst, half), :] = picked[q * half : (q + 1) * half]
        return carry

    lax.fori_loop(0, groups // block, gather, 0)
    for c in hot_copies:
        c.wait()

    def dots(i, carry):
        for u in range(UNROLL):
            g = i * UNROLL + u
            rows = pl.ds(pl.multiple_of(g * lane_group, lane_group), lane_group)
            part = pl.ds(pl.multiple_of(g * GROUP, GROUP), GROUP)
            xg = x[rows, :]
            for f in range(FEATS):
                a[part, f * width : (f + 1) * width] = xg[f * GROUP : (f + 1) * GROUP]
            gram = lax.dot_general(xg, xg, NT, preferred_element_type=F32) * scale
            own = jnp.where(i_lo == j_lo, gram, 0.0).astype(BF)
            wide = jnp.dot(own, spread, preferred_element_type=F32)
            wide = jnp.where(i_hi == j_hi, wide, 0.0)
            pairs[part, :] = jnp.sum(
                wide.reshape(FEATS, GROUP, lane_group), axis=0
            ).astype(BF)
        return carry

    lax.fori_loop(0, groups // UNROLL, dots, 0)
    for c in tail:
        c.wait()

    pre = jnp.dot(a[...], w_flat[...], preferred_element_type=F32)
    pre = pre + jnp.dot(pairs[...], w_inter[...], preferred_element_type=F32)
    pre = pre + bias[...]
    gated = jax.nn.sigmoid(pre)
    logits = jnp.sum(pre * gated * w_out[...], axis=-1, keepdims=True)
    eye = iota((samples, samples), 0) == iota((samples, samples), 1)
    target = jnp.sum(jnp.where(eye, targets[...], 0.0), axis=1, keepdims=True)
    residual = jax.nn.sigmoid(logits) - target
    slopes[...] = (residual * w_out[...] * gated * (1.0 + pre * (1.0 - gated))).astype(BF)

    inter_t = jnp.dot(swap, w_inter[...], preferred_element_type=F32).astype(BF)
    both = lax.dot_general(slopes[...], w_inter[...], NT, preferred_element_type=F32)
    both = both + lax.dot_general(slopes[...], inter_t, NT, preferred_element_type=F32)
    mirror[...] = (both * scale).astype(BF)

    def flat_back(f, carry):
        rows = pl.ds(pl.multiple_of(f * width, width), width)
        back[f] = lax.dot_general(
            slopes[...], w_flat[rows, :], NT, preferred_element_type=F32
        )
        return carry

    lax.fori_loop(0, FEATS, flat_back, 0)

    def grads(i, carry):
        for u in range(UNROLL):
            g = i * UNROLL + u
            rows = pl.ds(pl.multiple_of(g * lane_group, lane_group), lane_group)
            part = pl.ds(pl.multiple_of(g * GROUP, GROUP), GROUP)
            mine = mirror[part, :].astype(F32)
            tall = jnp.broadcast_to(mine[None], (FEATS, GROUP, lane_group)).reshape(sq)
            tall = jnp.where(i_hi == j_hi, tall, 0.0).astype(BF)
            wide = jnp.dot(tall, spread_t, preferred_element_type=F32)
            wide = jnp.where(i_lo == j_lo, wide, 0.0).astype(BF)
            total = jnp.dot(wide, x[rows, :], preferred_element_type=F32)
            total = total + back[:, part, :].reshape(lane_group, width)
            hi = total.astype(BF)
            lo = (total - hi.astype(F32)).astype(BF)
            for f in range(F_COLD):
                dst = pl.ds(pl.multiple_of(f * samples + g * GROUP, GROUP), GROUP)
                at = f * GROUP
                g_hi[dst, :] = hi[at : at + GROUP]
                g_lo[dst, :] = lo[at : at + GROUP]
                h_hi[dst, :] = hi[half + at : half + at + GROUP]
                h_lo[dst, :] = lo[half + at : half + at + GROUP]
        return carry

    lax.fori_loop(0, groups // UNROLL, grads, 0)
    outs = load_all([(h_hi, hot_hi), (h_lo, hot_lo)], sems.at[pl.ds(0, 2)])

    rows_blk = 512

    def scatter(b, carry):
        at = pl.multiple_of(b * rows_blk, rows_blk)
        subs = iota((rows_blk, samples), 0).astype(jnp.int16)
        for f in range(F_COLD):
            mine = jnp.broadcast_to(slots_t[f : f + 1, :] - at, (16, samples)).astype(jnp.int16)
            same = subs == jnp.concatenate([mine] * (rows_blk // 16), axis=0)
            match[:, f * samples : (f + 1) * samples] = as_one(same)
        total = jnp.dot(match[...], g_hi[...], preferred_element_type=F32)
        total = total + jnp.dot(match[...], g_lo[...], preferred_element_type=F32)
        fetched[pl.ds(at, rows_blk), :] = total.astype(BF)
        pltpu.make_async_copy(
            fetched.at[pl.ds(at, rows_blk), :], slot_grad.at[pl.ds(at, rows_blk), :], sems.at[3 + b]
        ).start()
        return carry

    n_out = slot_grad.shape[0] // rows_blk
    lax.fori_loop(0, n_out, scatter, 0)
    for b in range(n_out):
        pltpu.make_async_copy(
            fetched.at[pl.ds(b * rows_blk, rows_blk), :],
            slot_grad.at[pl.ds(b * rows_blk, rows_blk), :],
            sems.at[3 + b],
        ).wait()
    for c in outs:
        c.wait()


def backprop(m, fetched, xh, slots, slots_t, targets, w_flat, w_inter, bias, w_out):
    count, width = fetched.shape
    samples = slots.shape[0] // MB
    hidden = w_flat.shape[1]
    lookups = samples * F_COLD
    wide = FEATS * width
    rows = jax.ShapeDtypeStruct((lookups, width), BF)
    return pl.pallas_call(
        lambda *refs: step_kernel(m, *refs),
        in_specs=[HBM] * 9,
        out_specs=(HBM,) * 3,
        out_shape=(jax.ShapeDtypeStruct((count, width), BF), rows, rows),
        scratch_shapes=[
            pltpu.VMEM((count, width), BF),
            pltpu.VMEM((samples * FEATS, width), BF),
            pltpu.VMEM((samples, F_COLD), jnp.int32),
            pltpu.VMEM((F_COLD, samples), jnp.int32),
            pltpu.VMEM((1, samples), F32),
            pltpu.VMEM(w_flat.shape, BF),
            pltpu.VMEM(w_inter.shape, BF),
            pltpu.VMEM((1, hidden), F32),
            pltpu.VMEM((1, hidden), F32),
            pltpu.VMEM((samples, wide), BF),
            pltpu.VMEM((samples, FEATS * FEATS), BF),
            pltpu.VMEM((FEATS, samples, width), F32),
            pltpu.VMEM((samples, FEATS * FEATS), BF),
            pltpu.VMEM((lookups, width), BF),
            pltpu.VMEM((lookups, width), BF),
            pltpu.VMEM((lookups, width), BF),
            pltpu.VMEM((lookups, width), BF),
            pltpu.VMEM((512, 2048), BF),
            pltpu.VMEM((samples, hidden), BF),
            pltpu.SemaphoreType.DMA((9,)),
        ],
        compiler_params=params(),
        name="train_step",
    )(fetched, xh, slots, slots_t, targets, w_flat, w_inter, bias, w_out)


def hot_scatter_kernel(at_ref, ids_h, hi0, lo0, hi1, lo1, *refs):
    outs = refs[:N_X]
    other, ids, h0, l0, h1, l1, match, res, sems = refs[N_X:]
    copies = load_all([(ids_h, ids), (hi0, h0), (lo0, l0), (hi1, h1), (lo1, l1)], sems)
    samples = ids.shape[1] // MB
    block = match.shape[0]
    size = res.shape[0] // N_DP
    subs = iota((block, samples), 0).astype(jnp.int16)
    copies[0].wait()

    def body(m, hi, lo, b, carry):
        at = pl.multiple_of(b * block, block)
        for f in range(F_COLD):
            row = ids[f : f + 1, m * samples : (m + 1) * samples] - at
            mine = jnp.broadcast_to(row, (16, samples)).astype(jnp.int16)
            same = subs == jnp.concatenate([mine] * (block // 16), axis=0)
            match[:, f * samples : (f + 1) * samples] = as_one(same)
        total = jnp.dot(match[...], hi[...], preferred_element_type=F32)
        total = total + jnp.dot(match[...], lo[...], preferred_element_type=F32)
        if m:
            total = total + res[pl.ds(at, block), :]
        res[pl.ds(at, block), :] = total
        return carry

    for m, (hi, lo) in enumerate(((h0, l0), (h1, l1))):
        copies[1 + 2 * m].wait()
        copies[2 + 2 * m].wait()
        lax.fori_loop(0, res.shape[0] // block, functools.partial(body, m, hi, lo), 0)
    done = []
    for k in range(N_X):
        for flip, dst in ((0, outs[k]), (1, other.at[k])):
            chunk = mine_of(at_ref[0], k, flip)
            src = res.at[pl.ds(pl.multiple_of(chunk * size, size), size), :]
            done.append(pltpu.make_async_copy(src, dst, sems.at[2 * k + flip]))
            done[-1].start()
    for c in done:
        c.wait()


def hot_scatter(dp_at, ids, hi0, lo0, hi1, lo1, count):
    rows, width = hi0.shape
    return pl.pallas_call(
        hot_scatter_kernel,
        in_specs=[SMEM] + [HBM] * 5,
        out_specs=(HBM,) * (N_X + 1),
        out_shape=(jax.ShapeDtypeStruct((count // N_DP, width), F32),) * N_X
        + (jax.ShapeDtypeStruct((N_X, count // N_DP, width), F32),),
        scratch_shapes=[pltpu.VMEM(ids.shape, jnp.int32)]
        + [pltpu.VMEM((rows, width), BF)] * 4
        + [
            pltpu.VMEM((256, rows), BF),
            pltpu.VMEM((count, width), F32),
            pltpu.SemaphoreType.DMA((5 + N_DP,)),
        ],
        compiler_params=params(),
        name="hot_scatter",
    )(dp_at, ids, hi0, lo0, hi1, lo1)


def serve_kernel(m, with_hits, wanted, table_h, rows, *refs):
    if with_hits:
        hits, table, match, res, count_acc, sems = refs
    else:
        table, match, res, sems = refs
    load = pltpu.make_async_copy(table_h, table, sems.at[0])
    load.start()
    shards, lanes = wanted.shape
    capacity = lanes // MB
    count = table.shape[0]
    per = 8
    block = per * capacity
    ids = jnp.concatenate([wanted[...], jnp.zeros((lanes - shards, lanes), jnp.int32)], axis=0)
    turned = ids.T
    names = iota((capacity, count), 1).astype(jnp.int16)
    if with_hits:
        count_acc[...] = jnp.zeros_like(count_acc)

    def ones_of(part, mb, j):
        col = part[mb * capacity : (mb + 1) * capacity, j : j + 1]
        mine = jnp.broadcast_to(col, (capacity, 128)).astype(jnp.int16)
        return as_one(names == jnp.concatenate([mine] * (count // 128), axis=1))

    def add_hits(one):
        tall = one[0:16] + one[16:32] + one[32:48] + one[48:64]
        count_acc[...] += tall

    def build(part):
        for j in range(per):
            one = ones_of(part, m, j)
            match[j * capacity : (j + 1) * capacity, :] = one
            if with_hits:
                add_hits(one)
                for other in range(MB):
                    if other != m:
                        add_hits(ones_of(part, other, j))

    def finish(b):
        at = pl.ds(pl.multiple_of(b * block, block), block)
        res[at, :] = jnp.dot(match[...], table[...], preferred_element_type=F32).astype(BF)
        pltpu.make_async_copy(res.at[at, :], rows.at[at, :], sems.at[1 + b]).start()

    def body(b, carry):
        build(pltpu.roll(turned, lanes - b * per, 1))
        finish(b)
        return carry

    steps = shards // per
    if with_hits:
        load.wait()
        lax.fori_loop(0, steps, body, 0)
    else:
        build(turned)
        load.wait()
        finish(0)
        lax.fori_loop(1, steps, body, 0)
    if with_hits:
        total = jnp.sum(count_acc[...].astype(F32), axis=0, keepdims=True)
        size = count // N_DP
        for p in range(N_DP):
            hits[p : p + 1, :] = total[:, p * size : (p + 1) * size]
    for b in range(steps):
        at = pl.ds(b * block, block)
        pltpu.make_async_copy(res.at[at, :], rows.at[at, :], sems.at[1 + b]).wait()


def serve(m, with_hits, wanted, table):
    shards, lanes = wanted.shape
    capacity = lanes // MB
    slots = shards * capacity
    count, width = table.shape
    rows = jax.ShapeDtypeStruct((slots, width), BF)
    extra = [pltpu.VMEM((16, count), BF)] if with_hits else []
    return pl.pallas_call(
        lambda *refs: serve_kernel(m, with_hits, *refs),
        in_specs=[VMEM, HBM],
        out_specs=(HBM, VMEM) if with_hits else HBM,
        out_shape=(rows, jax.ShapeDtypeStruct((N_DP, count // N_DP), F32))
        if with_hits
        else rows,
        scratch_shapes=[
            pltpu.VMEM(table.shape, BF),
            pltpu.VMEM((512, count), BF),
            pltpu.VMEM((slots, width), BF),
        ]
        + extra
        + [pltpu.SemaphoreType.DMA((1 + shards // 8,))],
        compiler_params=params(),
        name="serve_rows",
    )(wanted, table)


def id_tiles(wanted, m):
    ids = wanted[...]
    other = pltpu.roll(ids, 64, 1)
    left, right = (ids, other) if m == 0 else (other, ids)
    low = iota((1, 128), 1) < 64
    return [
        jnp.where(low, left[2 * i : 2 * i + 1], right[2 * i + 1 : 2 * i + 2])
        for i in range(ids.shape[0] // 2)
    ]


def owner_match(tiles, base, match, subs):
    size = match.shape[0]
    for i, tile in enumerate(tiles):
        mine = jnp.broadcast_to(tile - base, (16, 128)).astype(jnp.int16)
        same = subs == jnp.concatenate([mine] * (size // 16), axis=0)
        match[:, i * 128 : (i + 1) * 128] = as_one(same)


def owner_kernel(flip, at_ref, wanted, hits, *refs):
    grads_h = refs[:MB]
    outs = refs[MB : -4]
    grads, match, res, sems = refs[-4:]
    size = match.shape[1]
    copies = load_all([(grads_h[m], grads.at[m]) for m in range(MB)], sems)
    tiles = [id_tiles(wanted, m) for m in range(MB)]
    subs = iota((size, 128), 0).astype(jnp.int16)
    for c in copies:
        c.wait()

    def body(k, carry):
        chunk = mine_of(at_ref[0], k, flip)
        at = pl.multiple_of(chunk * size, size)
        total = None
        for m in range(MB):
            owner_match(tiles[m], at, match.at[m], subs)
            term = jnp.dot(match[m], grads[m], preferred_element_type=F32)
            total = term if total is None else total + term
        res[k, :size, :] = total.astype(BF)
        mine = hits[pl.ds(chunk, 1), :]
        res[k, size:, :] = jnp.broadcast_to(mine, (16, size)).astype(BF)
        return carry

    lax.fori_loop(0, N_X, body, 0)
    if flip:
        done = load_all([(res, outs[0])], sems)
    else:
        done = load_all([(res.at[k], outs[k]) for k in range(N_X)], sems)
    for c in done:
        c.wait()


def owner(flip, dp_at, wanted, hits, grads):
    slots, width = grads[0].shape
    size = hits.shape[1]
    part = (size + 16, width)
    whole = (jax.ShapeDtypeStruct((N_X,) + part, BF),)
    each = (jax.ShapeDtypeStruct(part, BF),) * N_X
    return pl.pallas_call(
        lambda *refs: owner_kernel(flip, *refs),
        in_specs=[SMEM, VMEM, VMEM] + [HBM] * MB,
        out_specs=(HBM,) * (1 if flip else N_X),
        out_shape=whole if flip else each,
        scratch_shapes=[
            pltpu.VMEM((MB, slots, width), BF),
            pltpu.VMEM((MB, size, slots), BF),
            pltpu.VMEM((N_X,) + part, BF),
            pltpu.SemaphoreType.DMA((MB + N_X,)),
        ],
        compiler_params=small_params(),
        name="owner_other" if flip else "owner_mine",
    )(dp_at, wanted, hits, *grads)


def to_col(row, eye):
    return jnp.sum(jnp.where(eye, row, 0.0), axis=1, keepdims=True)


def to_row(col, eye):
    return jnp.sum(jnp.where(eye, col, 0.0), axis=0, keepdims=True)


def adagrad(table, accum, grad):
    accum_new = accum + jnp.mean(grad * grad, axis=-1, keepdims=True)
    return table - learn_rate * grad / jnp.sqrt(accum_new), accum_new


def pick_kernel(at_ref, table_h, bits_h, table_out, bits_out, table, bits, sems):
    size = table.shape[0]
    rows = pl.ds(pl.multiple_of(at_ref[0] * size, size), size)
    for pairs in (
        [(table_h.at[rows, :], table), (bits_h.at[rows, :], bits)],
        [(table, table_out), (bits, bits_out)],
    ):
        for c in load_all(pairs, sems):
            c.wait()


def pick(dp_at, table, bits):
    shape = (table.shape[0] // N_DP, table.shape[1])
    return pl.pallas_call(
        pick_kernel,
        in_specs=[SMEM, HBM, HBM],
        out_specs=(HBM, HBM),
        out_shape=(
            jax.ShapeDtypeStruct(shape, table.dtype),
            jax.ShapeDtypeStruct(shape, bits.dtype),
        ),
        scratch_shapes=[
            pltpu.VMEM(shape, table.dtype),
            pltpu.VMEM(shape, bits.dtype),
            pltpu.SemaphoreType.DMA((2,)),
        ],
        compiler_params=params(),
        name="pick_rows",
    )(dp_at, table, bits)


def cold_update_kernel(at_ref, *refs):
    ins = refs[: 3 + N_X]
    out = refs[3 + N_X]
    table, accum, bits, parts, res, sems = refs[4 + N_X :]
    size = table.shape[0]
    spots = [table, accum, bits] + [parts.at[k] for k in range(N_X)]
    copies = load_all(list(zip(ins, spots)), sems)
    eye = iota((size, size), 0) == iota((size, size), 1)
    for c in copies:
        c.wait()
    total = parts[0].astype(F32)
    for k in range(1, N_X):
        total = total + parts[k].astype(F32)
    touched = to_col(total[size : size + 1], eye)
    averaged = total[:size] / jnp.maximum(touched, 1.0)
    at = at_ref[0] * 2
    old = jnp.concatenate([accum[pl.ds(at, 1), :], accum[pl.ds(at + 1, 1), :]], axis=1)
    old = to_col(old, eye)
    updated, accum_new = adagrad(table[...].astype(F32), old, averaged)
    grid_step = jnp.max(jnp.abs(updated), axis=-1, keepdims=True) / 8.0
    dither = bits[...].astype(F32) * (1.0 / 65280.0) - 0.5
    res[:size, :] = jnp.where(touched > 0.5, updated + grid_step * dither, updated).astype(BF)
    row = to_row(accum_new, eye)
    high = row.astype(BF).astype(F32)
    middle = (row - high).astype(BF).astype(F32)
    low = (row - high) - middle
    which = iota((16, size), 0)
    packed = jnp.where(which == 0, high, jnp.where(which == 1, middle, low))
    res[size:, :] = packed.astype(BF)
    done = pltpu.make_async_copy(res, out, sems.at[0])
    done.start()
    done.wait()


def cold_update(dp_at, table, accum, bits, parts):
    shape = parts[0].shape
    return pl.pallas_call(
        cold_update_kernel,
        in_specs=[SMEM] + [HBM] * (3 + N_X),
        out_specs=HBM,
        out_shape=jax.ShapeDtypeStruct(shape, BF),
        scratch_shapes=[
            pltpu.VMEM(table.shape, BF),
            pltpu.VMEM(accum.shape, F32),
            pltpu.VMEM(bits.shape, jnp.int32),
            pltpu.VMEM((N_X,) + shape, BF),
            pltpu.VMEM(shape, BF),
            pltpu.SemaphoreType.DMA((3 + N_X,)),
        ],
        compiler_params=small_params(),
        name="cold_update",
    )(dp_at, table, accum, bits, *parts)


def cold_join_kernel(at_ref, *refs):
    parts = refs[:N_DP]
    out, accum_out, sems = refs[N_DP:]
    size = out.shape[0] // N_DP
    done = []
    for i in range(N_DP):
        chunk = chunk_of(at_ref[0], i)
        dst = out.at[pl.ds(pl.multiple_of(chunk * size, size), size), :]
        done.append(pltpu.make_async_copy(parts[i].at[pl.ds(0, size), :], dst, sems.at[i]))
        done[i].start()
    for i in range(N_DP):
        chunk = chunk_of(at_ref[0], i)
        rows = parts[i][size:, :].astype(F32)
        row = (rows[2:3] + rows[1:2]) + rows[0:1]
        accum_out[pl.ds(chunk * 2, 1), :] = row[:, :128]
        accum_out[pl.ds(chunk * 2 + 1, 1), :] = row[:, 128:]
    for c in done:
        c.wait()


def cold_join(dp_at, parts):
    width = parts[0].shape[1]
    size = parts[0].shape[0] - 16
    return pl.pallas_call(
        cold_join_kernel,
        in_specs=[SMEM] + [VMEM] * N_DP,
        out_specs=(HBM, VMEM),
        out_shape=(
            jax.ShapeDtypeStruct((N_DP * size, width), BF),
            jax.ShapeDtypeStruct((N_DP * size // 128, 128), F32),
        ),
        scratch_shapes=[pltpu.SemaphoreType.DMA((N_DP,))],
        compiler_params=small_params(),
        name="cold_join",
    )(dp_at, *parts)


def pair_sum_kernel(*refs):
    mine_h = refs[:N_X]
    other_h = refs[N_X]
    outs = refs[N_X + 1 : 2 * N_X + 1]
    mine, other, sems = refs[2 * N_X + 1 :]
    copies = load_all([(mine_h[k], mine.at[k]) for k in range(N_X)] + [(other_h, other)], sems)
    for c in copies:
        c.wait()
    mine[...] = (mine[...].astype(F32) + other[...].astype(F32)).astype(mine.dtype)
    done = load_all([(mine.at[k], outs[k]) for k in range(N_X)], sems)
    for c in done:
        c.wait()


def pair_sum(mine, other, compiler_params):
    outs = tuple(jax.ShapeDtypeStruct(part.shape, part.dtype) for part in mine)
    return pl.pallas_call(
        pair_sum_kernel,
        in_specs=[HBM] * (N_X + 1),
        out_specs=(HBM,) * N_X,
        out_shape=outs,
        scratch_shapes=[
            pltpu.VMEM(other.shape, other.dtype),
            pltpu.VMEM(other.shape, other.dtype),
            pltpu.SemaphoreType.DMA((N_X + 1,)),
        ],
        compiler_params=compiler_params,
        name="pair_sum",
    )(*mine, other)


def sum_parts_kernel(*refs):
    parts_h = refs[:N_X]
    out, parts, res, sems = refs[N_X:]
    copies = load_all([(parts_h[k], parts.at[k]) for k in range(N_X)], sems)
    for c in copies:
        c.wait()
    res[...] = (parts[0] + parts[1]) + (parts[2] + parts[3])
    done = pltpu.make_async_copy(res, out, sems.at[0])
    done.start()
    done.wait()


def sum_parts(parts):
    shape = parts[0].shape
    return pl.pallas_call(
        sum_parts_kernel,
        in_specs=[HBM] * N_X,
        out_specs=HBM,
        out_shape=jax.ShapeDtypeStruct(shape, F32),
        scratch_shapes=[
            pltpu.VMEM((N_X,) + shape, F32),
            pltpu.VMEM(shape, F32),
            pltpu.SemaphoreType.DMA((N_X,)),
        ],
        compiler_params=small_params(),
        name="sum_parts",
    )(*parts)


def hot_update_kernel(at_ref, table_h, accum_h, *refs):
    grads = refs[:N_DP]
    out, accum_out, table, accum, res, sems = refs[N_DP:]
    size = grads[0].shape[0]
    copies = load_all([(table_h, table), (accum_h, accum)], sems)
    eye = iota((size, size), 0) == iota((size, size), 1)
    for c in copies:
        c.wait()
    done = []
    for k in range(N_DP):
        chunk = chunk_of(at_ref[0], k)
        rows = pl.ds(pl.multiple_of(chunk * size, size), size)
        old = to_col(accum[pl.ds(chunk, 1), :], eye)
        updated, accum_new = adagrad(table[rows, :], old, grads[k][...])
        res[rows, :] = updated
        accum_out[pl.ds(chunk, 1), :] = to_row(accum_new, eye)
        done.append(pltpu.make_async_copy(res.at[rows, :], out.at[rows, :], sems.at[2 + k]))
        done[k].start()
    for c in done:
        c.wait()


def hot_update(dp_at, table, accum, grads):
    count, width = table.shape
    size = count // N_DP
    return pl.pallas_call(
        hot_update_kernel,
        in_specs=[SMEM] + [HBM] * 2 + [VMEM] * N_DP,
        out_specs=(HBM, VMEM),
        out_shape=(
            jax.ShapeDtypeStruct((count, width), F32),
            jax.ShapeDtypeStruct((N_DP, size), F32),
        ),
        scratch_shapes=[
            pltpu.VMEM((count, width), F32),
            pltpu.VMEM((N_DP, size), F32),
            pltpu.VMEM((count, width), F32),
            pltpu.SemaphoreType.DMA((2 + N_DP,)),
        ],
        compiler_params=small_params(),
        name="hot_update",
    )(dp_at, table, accum, *grads)


def exchange(value, axis):
    return lax.all_to_all(value, axis, split_axis=0, concat_axis=0, tiled=True)


def along_x(value, k):
    perm = [(i, ((i // 2 + k) % N_X) * 2 + i % 2) for i in range(N_DP)]
    return lax.ppermute(value, "dp", perm)


def to_partner(value):
    return lax.ppermute(value, "dp", [(i, i ^ 1) for i in range(N_DP)])


def to_owners(parts, compiler_params):
    *mine, other = parts
    other = to_partner(other)
    mine = pair_sum(mine, other, compiler_params)
    return [mine[0]] + [along_x(mine[k], k) for k in range(1, N_X)]


def to_all(part):
    along = [part] + [along_x(part, k) for k in range(1, N_X)]
    return along + [to_partner(value) for value in along]


def step(
    cold_table,
    cold_accum,
    dither_bits,
    hot_table,
    hot_accum,
    w_flat,
    w_inter,
    hidden_bias,
    w_out,
    targets,
    hot_ids,
    cold_slots,
    requests,
    counts,
):
    shards = lax.axis_size("shard")
    capacity = requests.shape[1]
    _, row_width = cold_table.shape
    hot_count = hot_table.shape[0]
    slots = shards * capacity
    dp_at = lax.axis_index("dp").astype(jnp.int32).reshape(1)

    live = jnp.arange(capacity, dtype=jnp.int32) < counts[:, :, None]
    asked = jnp.where(live, requests.reshape(MB, shards, capacity), -1)
    asked = asked.transpose(1, 0, 2).reshape(shards, MB * capacity)
    wanted = exchange(asked, "shard")

    fetched = []
    for m in range(MB):
        rows = serve(m, m == 1, wanted, cold_table)
        if m == 1:
            rows, hits = rows
        rows = exchange(rows.reshape(shards, capacity, row_width), "shard")
        fetched.append(rows.reshape(slots, row_width))
    own_table, own_bits = pick(dp_at, cold_table, dither_bits)
    xh = hot_rows(hot_ids, hot_table, cold_slots)

    owned = []
    hot_parts = []
    for m in range(MB):
        slot_grad, *hot_part = backprop(
            m,
            fetched[m],
            xh,
            cold_slots,
            cold_slots.T,
            targets.reshape(1, -1),
            w_flat,
            w_inter,
            hidden_bias.reshape(1, -1),
            w_out.reshape(1, -1),
        )
        hot_parts += hot_part
        rows = exchange(slot_grad.reshape(shards, capacity, row_width), "shard")
        owned.append(rows.reshape(slots, row_width))

    hot_grads = hot_scatter(dp_at, hot_ids.T, *hot_parts, hot_count)
    hot_grads = to_owners(hot_grads, params())
    hot_all = sum_parts(hot_grads)
    step_bit = shards // 2
    while step_bit:
        perm = [(i, i ^ step_bit) for i in range(shards)]
        hot_all = hot_all + lax.ppermute(hot_all, "shard", perm)
        step_bit //= 2
    hot_all = to_all(hot_all)
    hot_out, hot_accum_out = hot_update(
        dp_at, hot_table, hot_accum.reshape(N_DP, -1), hot_all
    )

    other = owner(1, dp_at, wanted, hits, owned)
    mine = owner(0, dp_at, wanted, hits, owned)
    parts = to_owners([*mine, *other], small_params())
    packed = cold_update(dp_at, own_table, cold_accum.reshape(-1, 128), own_bits, parts)
    parts = to_all(packed)
    cold_out, cold_accum_out = cold_join(dp_at, parts)
    return (cold_out, cold_accum_out.reshape(-1), hot_out, hot_accum_out.reshape(-1))


def solution(mesh):
    return jax.shard_map(
        step,
        mesh=mesh,
        in_specs=(
            P("shard", None),
            P("shard"),
            P("shard", None),
            P(),
            P(),
            P(),
            P(),
            P(),
            P(),
            P(("shard", "dp")),
            P(("shard", "dp"), None),
            P(("shard", "dp"), None),
            P(("shard", "dp"), None),
            P(("shard", "dp"), None),
        ),
        out_specs=(P("shard", None), P("shard"), P(), P()),
        check_vma=False,
    )
```
